32 devices in a mesh: seg: 4 (over y, core), ep: 8 (over z, x).
Axes of the slice: x: 2, y: 2, z: 4, core: 2. Of those that a mesh axis runs over, the one named last changes fastest.
Arguments:
- queries: bfloat16 [2048, 2048], P(('seg', 'ep')), may hold values from -6 to 6
- keys: bfloat16 [2048, 2048], P(('seg', 'ep')), may hold values from -1.25 to 1.25
- values: bfloat16 [2048, 2048], P(('seg', 'ep')), may hold values from -54 to 54
- log_decay: float32 [2048, 16], P('seg', 'ep'), may hold values from -1 to 0
- out_gain: float32 [2048], replicated, may hold values from 0.1 to 1.9
- out_proj: bfloat16 [2048, 6144], P('ep', 'seg'), may hold values from -0.125 to 0.125
- experts: int32 [256, 2], P(('seg', 'ep')), may hold values from 0 to 3, all different within a row; in each aligned block of 8 rows (0 to 7, 8 to 15, ...) at most 8 rows name the same one
- gates: float32 [256, 2], P(('seg', 'ep')), may hold values from 0.2 to 1
- up_weight: bfloat16 [8, 6144, 2304], P('ep', None, 'seg'), may hold values from -0.078125 to 0.078125
- down_weight: bfloat16 [8, 2304, 6144], P('ep', 'seg'), may hold values from -0.09375 to 0.09375
Outputs:
- attn_out: bfloat16 [2048, 2048], P(('seg', 'ep'))
- moe_out: bfloat16 [256, 6144], P(('seg', 'ep'))
The draws below stay inside these ranges and needn't reach their ends.
Inputs may be any that keep to these rules, and one draw needn't show every extreme that they name: Each row names two different experts. The 8 rows of one device name any one expert at most 8 times, and in some devices one expert exactly 8 times.
All inputs are finite; a program needn't handle non-finite values.
Results may differ from the reference program's by a relative error of at most 0.025.
Values may be sent and summed in bfloat16 or wider, within the bound.
A program may use at most 128 MiB of HBM per device.

```python
import math
import jax
import jax.numpy as jnp
import numpy as np
from jax import lax

D = 6144
HEAD_DIM = 128
EXPERT_FF = 4608
TOK_DEV = 64
MOE_TOK = 8
HEAD_COUNT = 16
EXPERTS = 4
FF_DEV = 576
CAP = 8
SEG_LEN = 512
TOKEN_COUNT = 2048
MOE_TOKENS = 256
N_SEG = 4
DEVICES = 32


def draw_values(key, part):
    key_sequence = jax.random.split(jax.random.fold_in(key, 11), 3)
    columns = HEAD_COUNT * HEAD_DIM
    column_scale = jnp.exp(jax.random.uniform(key_sequence[0], (1, columns), jnp.float32, math.log(0.3), math.log(3.0)))
    row_scale = jnp.exp(jax.random.uniform(key_sequence[1], (TOKEN_COUNT, 1), jnp.float32, math.log(0.3), math.log(3.0)))
    base = jnp.clip(jax.random.normal(key_sequence[2], (TOKEN_COUNT, columns), jnp.float32), -6.0, 6.0)
    return (base * column_scale * row_scale).astype(jnp.bfloat16)


def draw_log_decay(key, part):
    key_sequence = jax.random.split(jax.random.fold_in(key, 23), 6)
    fast_share = 0.5
    fast_heads = jax.random.uniform(key_sequence[0], (HEAD_COUNT,), jnp.float32) < fast_share
    fast_rate = jnp.exp(jax.random.uniform(key_sequence[1], (HEAD_COUNT,), jnp.float32, math.log(1.0 / 50.0), math.log(1.0 / 30.0)))
    slow_rate = 0.25 / TOKEN_COUNT
    baseline_rate = jnp.where(fast_heads, fast_rate, slow_rate)
    block_count = TOKEN_COUNT // TOK_DEV
    block_multiplier = jnp.exp(jax.random.uniform(key_sequence[2], (block_count, HEAD_COUNT), jnp.float32, math.log(0.5), math.log(2.0)))
    block_multiplier = jnp.repeat(block_multiplier, TOK_DEV, axis=0)
    jaggedness = jax.random.uniform(key_sequence[3], (TOKEN_COUNT, HEAD_COUNT), jnp.float32, 0.5, 1.5)
    spike_locations = jax.random.randint(key_sequence[4], (2, HEAD_COUNT), 0, TOKEN_COUNT)
    token_positions = jnp.arange(TOKEN_COUNT, dtype=jnp.int32)[:, None]
    spike_mask = (token_positions == spike_locations[0][None, :]) | (token_positions == spike_locations[1][None, :])
    spike_magnitude = jax.random.uniform(key_sequence[5], (TOKEN_COUNT, HEAD_COUNT), jnp.float32, 0.22, 0.69)
    decay_rate = baseline_rate[None, :] * block_multiplier * jaggedness + jnp.where(spike_mask, spike_magnitude, 0.0)
    return (-decay_rate).astype(jnp.float32)


def block_scale(key, extent, cuts, smallest, high):
    def one(dim, shards_of):
        draws = jax.random.uniform(jax.random.fold_in(jax.random.fold_in(key, 6), dim), (shards_of,), jnp.float32, smallest / len(cuts), high / len(cuts))
        return jnp.repeat(jnp.exp(draws), extent[dim] // shards_of).reshape((-1,) + (1,) * (len(extent) - dim - 1))

    factor_of = one(*cuts[0])
    for cut in cuts[1:]:
        factor_of = factor_of * one(*cut)
    return factor_of


def deal_out(stream_key, own, number, rows, number_of, top, bound, lean):
    sequence = jax.random.permutation(stream_key, number_of)
    crowded, usual = portions_of(number_of, rows * top, bound, lean, True), portions_of(number_of, rows * top, bound, lean, False)
    places = jnp.arange(number_of)

    def named(lengths, rotation):
        used = int((lengths > 0).sum())
        fixed = max(1, used // 4)
        moved = fixed + (places - fixed + rotation * (used - fixed)) % max(1, number_of - fixed)
        return jnp.zeros((number_of,), jnp.int32).at[sequence[jnp.where(places < fixed, places, moved)]].set(jnp.asarray(lengths, jnp.int32))

    lengths = jnp.where(number % 4 == 0, named(crowded, number // 4), named(usual, number - number // 4 - 1))
    mixed = jax.random.permutation(jax.random.fold_in(own, 3), number_of)
    giver, sink = mixed[0:number_of // 2 * 2:2], mixed[1:number_of // 2 * 2:2]
    margin = jnp.minimum(lengths[giver] - 1, bound - lengths[sink]) // 2
    margin = jnp.where((giver == sequence[0]) | (sink == sequence[0]) | (lengths[sink] == 0), 0, jnp.maximum(margin, 0))
    moved = jax.random.randint(jax.random.fold_in(own, 4), (number_of // 2,), 0, 1 << 20) % (margin + 1)
    lengths = lengths.at[giver].add(-moved).at[sink].add(moved)
    members = jnp.searchsorted(jnp.cumsum(lengths), jnp.arange(rows * top), side="right").astype(jnp.int32)
    table = members.reshape(top, rows).T
    table = table[jax.random.permutation(jax.random.fold_in(own, 1), rows)]
    rotation = jax.random.randint(jax.random.fold_in(own, 2), (rows, 1), 0, top)
    return jnp.take_along_axis(table, (jnp.arange(top)[None, :] + rotation) % top, axis=1)


def portions_of(count, total, limit, slope, full):
    loads = [(1 << 20) // math.isqrt(rank ** slope) + 1 for rank in range(1, count + 1)]
    largest = limit if full else min(limit, max(-(-total // count), total * loads[0] // sum(loads)))
    least = 1 if total - largest >= count - 1 else 0
    counts, rest = [largest] + [least] * (count - 1), total - largest - least * (count - 1)
    while rest > 0:
        free = [i for i in range(1, count) if counts[i] < largest] or [i for i in range(1, count) if counts[i] < limit]
        pool, budget = sum([loads[i] for i in free]), rest
        for i in free:
            addition = min(limit - counts[i], max(1, budget * loads[i] // pool), rest)
            counts[i] = counts[i] + addition
            rest = rest - addition
    return np.array(counts)


def normal_values(own_key, dims, deviation, most, cuts=(), kind=jnp.bfloat16):
    values = jax.random.normal(own_key, dims, jnp.float32) * deviation
    if len(cuts) > 0:
        values = block_scale(own_key, dims, cuts, -0.22, 0.18) * values
    return jnp.clip(values, min=-most, max=most).astype(kind)


def setup_inputs(seed: int = 0) -> dict:
    arg_keys = jax.random.split(jax.random.key(seed), 11)
    queries = normal_values(arg_keys[0], (TOKEN_COUNT, HEAD_COUNT * HEAD_DIM), 1.0, 6.0, ((0, 32),))
    keys = normal_values(arg_keys[1], (TOKEN_COUNT, HEAD_COUNT * HEAD_DIM), (HEAD_DIM ** -0.5), 1.25, ((0, 32),))
    values = draw_values(jax.random.fold_in(arg_keys[10], 71), 0)
    log_decay = draw_log_decay(jax.random.fold_in(arg_keys[10], 71), 0)
    out_gain = jnp.clip(1.0 + 0.18 * jax.random.normal(arg_keys[4], (HEAD_COUNT * HEAD_DIM,), jnp.float32), 0.1, 1.9)
    out_proj = normal_values(arg_keys[5], (HEAD_COUNT * HEAD_DIM, D), (HEAD_COUNT * HEAD_DIM) ** -0.5, 0.125, ((0, 8), (1, 4)))
    experts_keys = jax.random.split(jax.random.fold_in(arg_keys[6], 1), MOE_TOKENS // MOE_TOK)
    experts_turns = jax.random.permutation(jax.random.fold_in(arg_keys[6], 3), MOE_TOKENS // MOE_TOK)
    experts = jax.vmap(lambda own, number: deal_out(jax.random.fold_in(arg_keys[6], 2), own, number, MOE_TOK, EXPERTS, 2, CAP, 2))(experts_keys, experts_turns).reshape((MOE_TOKENS, 2))
    gates = jnp.clip(0.2 + 0.8 * jax.random.uniform(arg_keys[7], (MOE_TOKENS, 2), jnp.float32) ** block_scale(arg_keys[7], (MOE_TOKENS, 2), ((0, 32),), -0.2, 0.2), 0.2, 1.0)
    up_weight = normal_values(arg_keys[8], (2 * EXPERTS, D, EXPERT_FF // 2), D ** -0.5, 0.078125, ((0, 8), (2, 4)))
    down_weight = normal_values(arg_keys[9], (2 * EXPERTS, EXPERT_FF // 2, D), EXPERT_FF ** -0.5, 0.09375, ((0, 8), (1, 4)))
    return {"queries": queries, "keys": keys, "values": values, "log_decay": log_decay, "out_gain": out_gain, "out_proj": out_proj, "experts": experts, "gates": gates, "up_weight": up_weight, "down_weight": down_weight}


def reference(queries, keys, values, log_decay, out_gain, out_proj, experts, gates, up_weight, down_weight):
    highest = lax.Precision.HIGHEST
    grid = (N_SEG, SEG_LEN, HEAD_COUNT, HEAD_DIM)
    query_groups = queries.reshape(grid).astype(jnp.float32)
    key_groups = keys.reshape(grid).astype(jnp.float32)
    value_groups = values.reshape(grid).astype(jnp.float32)
    decay_groups = log_decay.reshape(N_SEG, SEG_LEN, HEAD_COUNT)
    causal_mask = jnp.arange(SEG_LEN)[:, None] >= jnp.arange(SEG_LEN)[None, :]

    def head_inside(inputs):
        query_head, key_head, value_head, cum_head = inputs
        log_gap = cum_head[:, None] - cum_head[None, :]
        weight = jnp.where(causal_mask, jnp.exp(jnp.where(causal_mask, log_gap, 0.0)), 0.0)
        scores = jnp.dot(query_head, key_head.T, precision=highest)
        mixing = lax.optimization_barrier((scores * weight).astype(jnp.bfloat16)).astype(jnp.float32)
        return jnp.dot(mixing, value_head, precision=highest)

    def group_step(state, inputs):
        query_block, key_block, value_block, decay_block = inputs
        cumulative = jnp.cumsum(decay_block, axis=0)
        inside = lax.map(head_inside, (query_block.transpose(1, 0, 2), key_block.transpose(1, 0, 2), value_block.transpose(1, 0, 2), cumulative.T)).transpose(1, 0, 2)
        outside = jnp.exp(cumulative)[:, :, None] * jnp.einsum('thd,hde->the', query_block, state, precision=highest)
        mixture = (inside + outside).astype(jnp.bfloat16)
        ending = cumulative[-1]
        to_end = jnp.exp(ending[None, :] - cumulative)
        local_state = jnp.einsum('sh,shd,she->hde', to_end, key_block, value_block, precision=highest)
        new_state = jnp.exp(ending)[:, None, None] * state + local_state
        return (new_state, mixture)
    start_state = jnp.zeros((HEAD_COUNT, HEAD_DIM, HEAD_DIM), jnp.float32)
    final_state, mixtures = lax.scan(group_step, start_state, (query_groups, key_groups, value_groups, decay_groups))
    heads_mix = mixtures.reshape(TOKEN_COUNT, HEAD_COUNT * HEAD_DIM).astype(jnp.float32)
    inv_rms = lax.rsqrt(lax.optimization_barrier(jnp.mean(heads_mix * heads_mix, axis=1, keepdims=True)) + 1e-06)
    attn_out = (heads_mix * inv_rms * out_gain[None, :]).astype(jnp.bfloat16)
    selected = attn_out.reshape(MOE_TOKENS, TOKEN_COUNT // MOE_TOKENS, HEAD_COUNT * HEAD_DIM)[:, 0]
    moe_in = jnp.dot(selected, out_proj, preferred_element_type=jnp.float32).astype(jnp.bfloat16)
    flattened = experts.reshape(DEVICES, 2 * MOE_TOK)
    onehot = (flattened[:, :, None] == jnp.arange(EXPERTS, dtype=jnp.int32)[None, None, :]).astype(jnp.int32)
    earlier = jnp.cumsum(onehot, axis=1) - onehot
    position = lax.optimization_barrier(jnp.sum(earlier * onehot, axis=2)).astype(jnp.int32)
    slot_of = position.reshape(DEVICES, MOE_TOK, 2)
    expert_of = experts.reshape(DEVICES, MOE_TOK, 2)
    rows_by_device = moe_in.reshape(DEVICES, MOE_TOK, D).astype(jnp.float32)
    capacity_ids = jnp.arange(CAP, dtype=jnp.int32)

    def per_expert(expert):
        matches = (expert_of == expert)[:, :, :, None] & (slot_of[:, :, :, None] == capacity_ids[None, None, None, :])
        chosen = jnp.any(matches, axis=2).astype(jnp.float32)
        row_data = jnp.einsum('dtc,dtk->dck', chosen, rows_by_device, precision=highest)
        row_data = row_data.astype(jnp.bfloat16).reshape(DEVICES * CAP, D)
        running = jnp.zeros((DEVICES * CAP, D), jnp.float32)
        for half_index in range(2):
            row_index = (2 * expert + half_index).astype(jnp.int32)
            up_half = lax.dynamic_index_in_dim(up_weight, row_index, 0, keepdims=False)
            down_half = lax.dynamic_index_in_dim(down_weight, row_index, 0, keepdims=False)
            hidden = jax.nn.silu(jnp.dot(row_data, up_half, preferred_element_type=jnp.float32)).astype(jnp.bfloat16)
            hidden_pieces = hidden.reshape(DEVICES * CAP, N_SEG, FF_DEV).astype(jnp.float32)
            down_pieces = down_half.reshape(N_SEG, FF_DEV, D).astype(jnp.float32)
            slice_terms = jnp.einsum('rgk,gkd->grd', hidden_pieces, down_pieces, precision=highest)
            rounded = lax.optimization_barrier(slice_terms.astype(jnp.bfloat16)).astype(jnp.float32)
            running = running + lax.optimization_barrier(jnp.sum(rounded, axis=0))
        return running
    results = lax.map(per_expert, jnp.arange(EXPERTS, dtype=jnp.int32))
    device_index = jnp.arange(DEVICES, dtype=jnp.int32)[:, None, None]
    flat_index = (expert_of * (DEVICES * CAP) + device_index * CAP + slot_of).astype(jnp.int32)
    picked = results.reshape(EXPERTS * DEVICES * CAP, D)[flat_index.reshape(-1)].reshape(DEVICES, MOE_TOK, 2, D)
    weighted = lax.optimization_barrier(jnp.sum(picked * gates.reshape(DEVICES, MOE_TOK, 2, 1), axis=2))
    moe_out = weighted.astype(jnp.bfloat16).reshape(MOE_TOKENS, D)
    return (attn_out, moe_out)
```

```python
import functools
import math

import jax
import jax.numpy as jnp
from jax import lax
from jax.experimental import pallas as pl
from jax.experimental.pallas import tpu as pltpu
from jax.sharding import PartitionSpec as P

epsilon = 1e-06
MESH = pl.DeviceIdType.MESH
VM = pltpu.VMEM


def prefix(x, axis, join, neutral):
    place = lax.axis_index(axis)
    gathered = jax.tree.map(
        lambda a, kind: lax.all_gather(a.astype(kind), axis), x, (jnp.bfloat16, jnp.bfloat16)
    )
    state = jax.tree.map(lambda a, e: jnp.zeros_like(a) + jnp.asarray(e, a.dtype), x, neutral)

    def one(turn, state):
        return join(
            state,
            jax.tree.map(
                lambda a, own: lax.dynamic_index_in_dim(a, turn, 0, False).astype(own.dtype),
                gathered,
                x,
            ),
        )

    return lax.fori_loop(0, place, one, state)


def chain_combine(first_part, second_part):
    return (
        first_part[0] * second_part[0],
        second_part[0][:, None, None] * first_part[1] + second_part[1],
    )


def route_tables(experts, gates, expert_count, capacity):
    token_count = experts.shape[0]
    flattened = experts.reshape(-1)
    onehot = (flattened[:, None] == jnp.arange(expert_count, dtype=jnp.int32)[None, :]).astype(
        jnp.int32
    )
    earlier = jnp.cumsum(onehot, axis=0) - onehot
    position = jnp.sum(earlier * onehot, axis=1)
    slot_index = (flattened * capacity + position).reshape(token_count, 2)
    columns = jnp.arange(expert_count * capacity, dtype=jnp.int32)
    matches = slot_index[:, :, None] == columns[None, None, :]
    dispatch = jnp.any(matches, axis=1).T.astype(jnp.bfloat16)
    combine = jnp.sum(jnp.where(matches, gates[:, :, None], 0.0), axis=1)
    return (dispatch, combine)


def expert_output(row_data, up_piece, down_piece):
    hidden = jax.nn.silu(jnp.dot(row_data, up_piece, preferred_element_type=jnp.float32)).astype(
        jnp.bfloat16
    )
    return jnp.dot(hidden, down_piece, preferred_element_type=jnp.float32)


def on_device_routed(
    queries, keys, values, log_decay, out_gain, out_proj, experts, gates, up_weight, down_weight
):
    highest = lax.Precision.HIGHEST
    ep_count = lax.axis_size("ep")
    heads_local = log_decay.shape[1]
    head_dim = queries.shape[1] // (heads_local * ep_count)
    query_heads, key_heads, value_heads = (
        lax.all_to_all(queries, "ep", split_axis=1, concat_axis=0, tiled=True),
        lax.all_to_all(keys, "ep", split_axis=1, concat_axis=0, tiled=True),
        lax.all_to_all(values, "ep", split_axis=1, concat_axis=0, tiled=True),
    )
    seg_length = query_heads.shape[0]
    query_heads = query_heads.reshape(seg_length, heads_local, head_dim)
    key_heads = key_heads.reshape(seg_length, heads_local, head_dim)
    value_heads = value_heads.reshape(seg_length, heads_local, head_dim)
    cumulative = jnp.cumsum(log_decay, axis=0)
    across = cumulative.T
    block_size = math.gcd(seg_length, 512)
    starts = jnp.arange(seg_length // block_size, dtype=jnp.int32) * block_size
    token_positions = jnp.arange(seg_length, dtype=jnp.int32)

    def block_mix(start):
        query_block = lax.dynamic_slice_in_dim(query_heads, start, block_size, 0)
        cum_block = lax.dynamic_slice_in_dim(across, start, block_size, 1)
        row_ids = start + jnp.arange(block_size, dtype=jnp.int32)
        causal = (row_ids[:, None] >= token_positions[None, :])[None]
        log_gap = cum_block[:, :, None] - across[:, None, :]
        weight = jnp.where(causal, jnp.exp(jnp.where(causal, log_gap, 0.0)), 0.0)
        scores = jnp.einsum(
            "thd,shd->hts", query_block, key_heads, preferred_element_type=jnp.float32
        )
        mixing = (scores * weight).astype(jnp.bfloat16)
        return jnp.einsum("hts,she->the", mixing, value_heads, preferred_element_type=jnp.float32)

    inside = lax.map(block_mix, starts).reshape(seg_length, heads_local, head_dim)
    ending = cumulative[-1]
    to_end = jnp.exp(ending[None, :] - cumulative)
    key_float = key_heads.astype(jnp.float32)
    value_float = value_heads.astype(jnp.float32)
    local_state = jnp.einsum("sh,shd,she->hde", to_end, key_float, value_float, precision=highest)
    identity = (jnp.ones_like(ending), jnp.zeros_like(local_state))
    carried = prefix((jnp.exp(ending), local_state), "seg", chain_combine, identity)[1]
    outside = jnp.exp(cumulative)[:, :, None] * jnp.einsum(
        "thd,hde->the", query_heads.astype(jnp.float32), carried, precision=highest
    )
    mixture = (inside + outside).astype(jnp.bfloat16).reshape(seg_length, heads_local * head_dim)
    token_mix = lax.all_to_all(mixture, "ep", split_axis=0, concat_axis=1, tiled=True)
    as_float = token_mix.astype(jnp.float32)
    inv_rms = lax.rsqrt(jnp.mean(as_float * as_float, axis=1, keepdims=True) + epsilon)
    attn_out = (as_float * inv_rms * out_gain[None, :]).astype(jnp.bfloat16)
    row_stride = 8
    own_width = heads_local * head_dim
    feature_count = own_width * ep_count
    picked_float = mixture.reshape(seg_length // row_stride, row_stride, own_width)[:, 0].astype(
        jnp.float32
    )
    square_sums = lax.psum(jnp.sum(picked_float * picked_float, axis=1), "ep")
    picked_rms = lax.rsqrt(square_sums[:, None] / feature_count + epsilon)
    gain_slice = lax.dynamic_slice_in_dim(out_gain, lax.axis_index("ep") * own_width, own_width, 0)
    normed_rows = (picked_float * picked_rms * gain_slice[None, :]).astype(jnp.bfloat16)
    proj_terms = jnp.dot(
        normed_rows,
        lax.all_gather(out_proj, "seg", axis=1, tiled=True),
        preferred_element_type=jnp.float32,
    )
    moe_in = lax.psum_scatter(
        proj_terms.astype(jnp.bfloat16), "ep", scatter_dimension=0, tiled=True
    )
    expert_count = ep_count // 2
    token_count, model_width = moe_in.shape
    capacity = max(2, 4 * token_count // expert_count)
    dispatch, combine = route_tables(experts, gates, expert_count, capacity)
    up_piece = up_weight[0]
    down_piece = down_weight[0]
    slot_rows = jnp.dot(dispatch, moe_in, preferred_element_type=jnp.float32).astype(jnp.bfloat16)
    outgoing = jnp.repeat(slot_rows.reshape(expert_count, capacity, model_width), 2, axis=0)
    arrived = lax.all_to_all(outgoing, "ep", split_axis=0, concat_axis=0, tiled=True).reshape(
        ep_count * capacity, model_width
    )
    gathered = lax.all_gather(arrived, "seg", axis=0, tiled=True)
    owned_sums = lax.psum_scatter(
        expert_output(gathered, up_piece, down_piece).astype(jnp.bfloat16),
        "seg",
        scatter_dimension=0,
        tiled=True,
    ).astype(jnp.float32)
    returned_back = lax.all_to_all(
        owned_sums.reshape(ep_count, capacity, model_width).astype(jnp.bfloat16),
        "ep",
        split_axis=0,
        concat_axis=0,
        tiled=True,
    ).astype(jnp.float32)
    paired = returned_back.reshape(expert_count, 2, capacity, model_width)
    halves = (paired[:, 0] + paired[:, 1]).reshape(expert_count * capacity, model_width)
    summed = jnp.dot(combine, halves, precision=highest)
    moe_out = summed.astype(jnp.bfloat16)
    return (attn_out, moe_out)


def remote(src, dst, send, recv, **target):
    return pltpu.make_async_remote_copy(
        src_ref=src, dst_ref=dst, send_sem=send, recv_sem=recv,
        device_id=target, device_id_type=MESH,
    )


def greet(seg_count, ep_count):
    seg, ep = lax.axis_index("seg"), lax.axis_index("ep")
    barrier = pltpu.get_barrier_semaphore()
    for j in range(1, ep_count):
        pl.semaphore_signal(
            barrier, inc=1, device_id={"ep": lax.rem(ep + j, ep_count)}, device_id_type=MESH
        )
    for k in range(1, seg_count):
        pl.semaphore_signal(
            barrier, inc=1, device_id={"seg": lax.rem(seg + k, seg_count)}, device_id_type=MESH
        )
    pl.semaphore_wait(barrier, ep_count + seg_count - 2)
    return seg, ep


def step_kernel(
    seg_count, ep_count, heads, dim, tile, wide, lags,
    q_ref, k_ref, v_ref, proj_hbm, up_hbm, down_hbm,
    turned_ref, experts_ref, gates_ref, gain_ref,
    attn_ref, out_ref,
    qb, kb, vb, states, ends, table_ref, mix_ref,
    up, down, proj, rows, part, x_sum, z_part, z_in, full, acc, hidden, tokens,
    terms, core_in, both, y_in, x_in, middle, line, line_in,
    load_sem, in_send, in_recv, gate_send, gate_recv,
    st_send, st_recv, end_send, end_recv, row_send, row_recv, pick_send, pick_recv,
    rx_send, rx_recv, rz_send, rz_recv,
    ag_send, ag_recv, x_send, x_recv, y_send, y_recv, c_send, c_recv,
    t_send, t_recv, tc_send, tc_recv, ty_send, ty_recv, tx_send, tx_recv, tz_send, tz_recv,
):
    f32, bf16 = jnp.float32, jnp.bfloat16
    seg, ep = greet(seg_count, ep_count)
    width = heads * dim
    tokens_own, moe_own = q_ref.shape[0], experts_ref.shape[1]
    y_count, half = seg_count // 2, ep_count // 2
    core, y = lax.rem(seg, 2), lax.div(seg, 2)
    x, z = lax.rem(ep, 2), lax.div(ep, 2)
    x_mate = ep + 1 - 2 * x
    mate = seg + 1 - 2 * core

    def seg_at(d, i):
        return lax.rem(y + d + y_count, y_count) * 2 + (core if i == 0 else 1 - core)

    triples = ((k_ref, kb), (v_ref, vb), (q_ref, qb))
    sends = {}
    own = pl.ds(pl.multiple_of(ep * width, width), width)
    keep = []
    for i, (ref, buf) in enumerate(triples):
        sends[i] = []
        for j in range(1, ep_count):
            other = lax.rem(ep + j, ep_count)
            columns = pl.ds(pl.multiple_of(other * width, width), width)
            copy = remote(
                ref.at[:, columns], buf.at[ep], in_send.at[i, j], in_recv.at[i, j], ep=other
            )
            copy.start()
            sends[i].append(copy)
        copy = pltpu.make_async_copy(ref.at[:, own], buf.at[ep], load_sem.at[3 + i])
        copy.start()
        keep.append(copy)
    loads = [
        pltpu.make_async_copy(proj_hbm, proj, load_sem.at[0]),
        pltpu.make_async_copy(up_hbm.at[0], up, load_sem.at[1]),
        pltpu.make_async_copy(down_hbm.at[0], down, load_sem.at[2]),
    ]
    for load in loads:
        load.start()
    lanes = lax.broadcasted_iota(jnp.int32, (moe_own, 128), 1).astype(f32)
    corner = (
        lax.broadcasted_iota(jnp.int32, (moe_own, moe_own), 0)
        == lax.broadcasted_iota(jnp.int32, (moe_own, moe_own), 1)
    )

    def upright(line):
        spread = jnp.broadcast_to(line, (moe_own, moe_own))
        return jnp.sum(jnp.where(corner, spread, 0.0), axis=1, keepdims=True)

    table_ref[seg, ep] = sum(
        jnp.where(
            upright(experts_ref[i : i + 1, :].astype(f32)) == lanes,
            upright(gates_ref[i : i + 1, :]),
            0.0,
        )
        for i in range(experts_ref.shape[0])
    )
    gates = []
    for j in range(1, ep_count):
        copy = remote(
            table_ref.at[seg, ep], table_ref.at[seg, ep], gate_send.at[j], gate_recv.at[j],
            ep=lax.rem(ep + j, ep_count),
        )
        copy.start()
        gates.append(copy)
    length = tokens_own * ep_count
    highest = lax.Precision.HIGHEST
    rows_at = lax.broadcasted_iota(jnp.int32, (length, length), 0)
    columns_at = lax.broadcasted_iota(jnp.int32, (length, length), 1)
    causal = rows_at >= columns_at
    lower = causal.astype(f32)
    turned_decay = turned_ref[...]
    across = lax.dot_general(
        turned_decay, lower, (((1,), (1,)), ((), ())), precision=highest,
        preferred_element_type=f32,
    )
    cum = lax.dot_general(
        lower, turned_decay, (((1,), (1,)), ((), ())), precision=highest,
        preferred_element_type=f32,
    )
    for copy in keep:
        copy.wait()
    for i in (0, 1):
        for copy in sends[i]:
            copy.wait()
    keys, values = (
        jnp.concatenate([b[p] for p in range(ep_count)], axis=0) for b in (kb, vb)
    )
    ending = cum[length - 1 : length, :]
    unit = (
        lax.broadcasted_iota(jnp.int32, (dim, dim), 0)
        == lax.broadcasted_iota(jnp.int32, (dim, dim), 1)
    ).astype(f32).astype(bf16)
    for h in range(heads):
        cols = slice(h * dim, (h + 1) * dim)
        to_end = jnp.exp(ending[:, h : h + 1] - across[h : h + 1, :])
        turned = lax.dot_general(
            unit, keys[:, cols], (((1,), (1,)), ((), ())), preferred_element_type=f32
        )
        states[seg, h] = jnp.dot(
            (turned * to_end).astype(bf16), values[:, cols],
            preferred_element_type=f32,
        ).astype(bf16)
        ends[seg, h : h + 1] = jnp.broadcast_to(ending[:, h : h + 1], (1, dim))
    moved = []
    for k in range(1, seg_count):
        other = lax.rem(seg + k, seg_count)
        for buf, send, recv in ((states, st_send, st_recv), (ends, end_send, end_recv)):
            copy = remote(buf.at[seg], buf.at[seg], send.at[k], recv.at[k], seg=other)
            copy.start()
            moved.append(copy)
    for copy in sends[2]:
        copy.wait()
    queries = jnp.concatenate([qb[p] for p in range(ep_count)], axis=0)
    inside = []
    for h in range(heads):
        cols = slice(h * dim, (h + 1) * dim)
        gap = cum[:, h : h + 1] - across[h : h + 1, :]
        weight = jnp.where(causal, jnp.exp(jnp.where(causal, gap, 0.0)), 0.0)
        scores = lax.dot_general(
            queries[:, cols], keys[:, cols], (((1,), (1,)), ((), ())),
            preferred_element_type=f32,
        )
        inside.append(
            jnp.dot(
                (scores * weight).astype(bf16), values[:, cols],
                preferred_element_type=f32,
            )
        )
    for copy in moved:
        copy.wait()
    outs = []
    for h in range(heads):
        cols = slice(h * dim, (h + 1) * dim)
        carried = jnp.zeros((dim, dim), f32)
        for c in range(seg_count):
            joined = jnp.exp(ends[c, h : h + 1]) * carried + states[c, h].astype(f32)
            carried = jnp.where(c < seg, joined, carried)
        outside = jnp.exp(cum[:, h : h + 1]) * jnp.dot(
            queries[:, cols], carried.astype(bf16), preferred_element_type=f32
        )
        outs.append((inside[h] + outside).astype(bf16))
    mixture = jnp.concatenate(outs, axis=1)
    mix_ref[...] = mixture.reshape(mix_ref.shape)
    count = length // tokens_own * moe_own
    stride = length // count
    pick = (
        lax.broadcasted_iota(jnp.int32, (count, length), 1)
        == stride * lax.broadcasted_iota(jnp.int32, (count, length), 0)
    )
    rows[seg] = jnp.dot(
        pick.astype(f32).astype(bf16), mixture, preferred_element_type=f32
    ).astype(bf16)
    own_rows = rows.shape[1]
    total = own_rows * seg_count
    mine = own_rows // ep_count
    cols = proj.shape[1]
    features = width * ep_count
    sources = [(d, i) for d in range(y_count) for i in range(2)]
    row_moves = {}
    for d, i in sources[1:]:
        row_moves[d, i] = remote(
            rows.at[seg], rows.at[seg], pick_send.at[d, i], pick_recv.at[d, i], seg=seg_at(d, i)
        )
        row_moves[d, i].start()
    lane = lax.broadcasted_iota(jnp.int32, (own_rows, 128), 1)
    pieces = {n: [(0, cols + 128)] for n in range(seg_count)}
    pieces[0] = [(t, tile) for t in range(0, cols - tile, tile)] + [(cols - tile, tile + 128)]
    x_moves, z_moves = {}, {}

    def source(n):
        d, i = sources[n]
        return seg_at(-d, i)

    def project(n):
        if n:
            row_moves[sources[n]].wait_recv()
        picked = rows[source(n)].astype(f32)
        squares = jnp.sum(picked * picked, axis=1, keepdims=True)
        high = squares.astype(bf16).astype(f32)
        pair = jnp.where(lane < 64, high, squares - high).reshape(half, 2, mine, 128).astype(bf16)
        scaled = (picked * gain_ref[:, own]).astype(bf16)
        for i in range(2):
            part[n, i, :, :, cols:] = pair[:, i]
        for p, (at, size) in enumerate(pieces[n]):
            for t in range(at, min(at + size, cols), tile):
                value = (
                    jnp.dot(scaled, proj[:, t : t + tile], preferred_element_type=f32)
                    .reshape(half, 2, mine, tile)
                    .astype(bf16)
                )
                for i in range(2):
                    part[n, i, :, :, t : t + tile] = value[:, i]
            span = pl.ds(at, size)
            x_moves[n, p] = remote(
                part.at[n, 1 - x, :, :, span], x_sum.at[n, :, :, span],
                rx_send.at[n, p], rx_recv.at[n, p], ep=x_mate,
            )
            x_moves[n, p].start()

    def combine(n):
        for p, (at, size) in enumerate(pieces[n]):
            x_moves[n, p].wait_recv()
            span = pl.ds(at, size)
            value = part[n, x, :, :, span].astype(f32) + x_sum[n, :, :, span].astype(f32)
            z_part[n, :, :, span] = value.astype(bf16)
            if at + size > cols:
                pair = value[:, :, size - 128 :].reshape(half * mine, 128)
                squares = pair[:, :1] + pair[:, 64:65]
                high = squares.astype(bf16).astype(f32)
                pair = jnp.where(lane[: half * mine] < 64, high, squares - high).astype(bf16)
                z_part[n, :, :, cols:] = pair.reshape(half, mine, 128)
            for k in range(1, half):
                other = lax.rem(z + k, half)
                z_moves[n, p, k] = remote(
                    z_part.at[n, other, :, span], z_in.at[n, k, :, span],
                    rz_send.at[n, p, k], rz_recv.at[n, p, k], ep=other * 2 + x,
                )
                z_moves[n, p, k].start()

    def finish(n):
        value = z_part[n, z].astype(f32)
        for k in range(1, half):
            for p in range(len(pieces[n])):
                z_moves[n, p, k].wait_recv()
            value = value + z_in[n, k].astype(f32)
        square = value[:, cols : cols + 1] + value[:, cols + 64 : cols + 65]
        inv_rms = lax.rsqrt(square / features + epsilon)
        full[seg, source(n), ep] = (value[:, :cols] * inv_rms).astype(bf16)

    loads[0].wait()
    project(0)
    for copy in gates:
        copy.wait()
    table_moves = []
    for k in range(1, seg_count):
        copy = remote(
            table_ref.at[seg], table_ref.at[seg], row_send.at[k], row_recv.at[k],
            seg=lax.rem(seg + k, seg_count),
        )
        copy.start()
        table_moves.append(copy)
    for n in range(1, seg_count):
        project(n)
        combine(n - 1)
    combine(seg_count - 1)
    for n in range(seg_count):
        finish(n)
    flying = [*row_moves.values(), *x_moves.values(), *z_moves.values()]

    def send(place, send_sem, recv_sem, **target):
        copy = remote(place, place, send_sem, recv_sem, **target)
        copy.start()
        flying.append(copy)
        return copy

    def on_line(e, k):
        return lax.rem(e - 2 * k + ep_count, ep_count)

    def y_seg(k):
        return seg_at(k, 0)

    z_copies = {}
    for k in range(1, half):
        z_copies[k] = send(
            full.at[seg, :, ep], ag_send.at[k], ag_recv.at[k], ep=lax.rem(ep + 2 * k, ep_count)
        )
    x_copies, y_copies = {}, {}
    for k in range(half):
        if k > 0:
            z_copies[k].wait_recv()
        place = full.at[seg, :, on_line(ep, k)]
        x_copies[k, 0] = send(place, x_send.at[k, 0], x_recv.at[k, 0], ep=x_mate)
        for d in range(1, y_count):
            y_copies[k, 0, d] = send(
                place, y_send.at[k, 0, d], y_recv.at[k, 0, d], seg=y_seg(d)
            )
        send(place, c_send.at[k, 0, 0], c_recv.at[k, 0, 0], seg=mate)
    for k in range(half):
        x_copies[k, 0].wait_recv()
        place = full.at[seg, :, on_line(x_mate, k)]
        if k % 2 == 0:
            for d in range(1, y_count):
                y_copies[k, 1, d] = send(
                    place, y_send.at[k, 1, d], y_recv.at[k, 1, d], seg=y_seg(d)
                )
        send(place, c_send.at[k, 1, 0], c_recv.at[k, 1, 0], seg=mate)
        for d in range(1, y_count):
            y_copies[k, 0, d].wait_recv()
            place = full.at[y_seg(-d), :, on_line(ep, k)]
            if k % 2 == 1:
                x_copies[k, d] = send(place, x_send.at[k, d], x_recv.at[k, d], ep=x_mate)
            send(place, c_send.at[k, 0, d], c_recv.at[k, 0, d], seg=mate)
    loads[1].wait()
    acc[...] = jnp.zeros_like(acc)

    def multiply(s):
        def step(n, carry):
            at = pl.multiple_of(n * tile, tile)
            block = full[s, :, :, :, pl.ds(at, tile)].reshape(total, tile)
            lines = pl.ds(pl.multiple_of(s * cols + n * tile, tile), tile)
            acc[...] += lax.dot_general(
                block, up[:, lines], (((1,), (1,)), ((), ())), preferred_element_type=f32
            )
            return carry

        lax.fori_loop(0, cols // tile, step, 0)

    multiply(seg)
    for k in range(half):
        for d in range(1, y_count):
            (y_copies[k, 1, d] if k % 2 == 0 else x_copies[k, d]).wait_recv()
            send(
                full.at[y_seg(-d), :, on_line(x_mate, k)],
                c_send.at[k, 1, d], c_recv.at[k, 1, d], seg=mate,
            )
    for d in range(1, y_count):
        multiply(y_seg(-d))
    for k in range(half):
        for i in range(2):
            for d in range(y_count):
                place = full.at[seg, :, ep]
                remote(place, place, c_send.at[k, i, d], c_recv.at[k, i, d], seg=mate).wait_recv()
    for copy in flying:
        copy.wait_send()
    backs = []
    tokens[ep] = mix_ref[ep]
    for j in range(1, ep_count):
        other = lax.rem(ep + j, ep_count)
        copy = remote(mix_ref.at[other], tokens.at[ep], t_send.at[j], t_recv.at[j], ep=other)
        copy.start()
        backs.append(copy)
    for k in range(y_count):
        multiply(seg_at(k, 1))
    value = acc[...]
    hidden[...] = (value / (1.0 + jnp.exp(-value))).astype(bf16)
    for copy in table_moves:
        copy.wait()
    table = table_ref[...].reshape(total, 128)
    lane = lax.broadcasted_iota(jnp.int32, (total, 128), 1)
    gate = jnp.sum(jnp.where(lane == z, table, 0.0), axis=1, keepdims=True)
    loads[2].wait()
    steps = seg_count * cols // wide
    core_moves = {}

    def product(c):
        value = jnp.dot(
            hidden[...], down[:, c * wide : (c + 1) * wide], preferred_element_type=f32
        )
        value = jnp.where(gate != 0.0, value * gate, 0.0).astype(bf16)
        terms[c] = value.reshape(seg_count, own_rows, wide)
        core_moves[c] = []
        for k in range(y_count):
            copy = remote(
                terms.at[c, k * 2 + 1 - core], core_in.at[c, k],
                tc_send.at[c, k], tc_recv.at[c, k], seg=mate,
            )
            copy.start()
            core_moves[c].append(copy)

    first, second, last = {}, {}, {}

    def joined(c):
        for copy in core_moves[c]:
            copy.wait()
        for k in range(y_count):
            value = (terms[c, k * 2 + core].astype(f32) + core_in[c, k].astype(f32)).reshape(
                half, 2, mine, wide
            ).astype(bf16)
            for i in range(2):
                both[c, k, i] = value[:, i]
        first[c] = []
        if c % 2 == 0:
            for d in range(1, y_count):
                first[c].append(
                    remote(
                        both.at[c, lax.rem(y + d, y_count)], y_in.at[c, d],
                        ty_send.at[c, d], ty_recv.at[c, d], seg=y_seg(d),
                    )
                )
        else:
            first[c].append(
                remote(
                    both.at[c, :, 1 - x], x_in.at[c], tx_send.at[c], tx_recv.at[c], ep=x_mate
                )
            )
        for copy in first[c]:
            copy.start()

    def crossed(c):
        for copy in first[c]:
            copy.wait()
        second[c] = []
        if c % 2 == 0:
            for i in range(2):
                value = both[c, y, i].astype(f32)
                for d in range(1, y_count):
                    value = value + y_in[c, d, i].astype(f32)
                middle[c, i] = value.astype(bf16)
            second[c].append(
                remote(
                    middle.at[c, 1 - x], x_in.at[c, 0], tx_send.at[c], tx_recv.at[c], ep=x_mate
                )
            )
        else:
            for k in range(y_count):
                middle[c, k] = (both[c, k, x].astype(f32) + x_in[c, k].astype(f32)).astype(bf16)
            for d in range(1, y_count):
                second[c].append(
                    remote(
                        middle.at[c, lax.rem(y + d, y_count)], y_in.at[c, d, 0],
                        ty_send.at[c, d], ty_recv.at[c, d], seg=y_seg(d),
                    )
                )
        for copy in second[c]:
            copy.start()

    def along(c):
        for copy in second[c]:
            copy.wait()
        if c % 2 == 0:
            value = middle[c, x].astype(f32) + x_in[c, 0].astype(f32)
        else:
            value = middle[c, y].astype(f32)
            for d in range(1, y_count):
                value = value + y_in[c, d, 0].astype(f32)
        line[c] = value.astype(bf16)
        last[c] = []
        for k in range(1, half):
            other = lax.rem(z + k, half)
            copy = remote(
                line.at[c, other], line_in.at[c, k], tz_send.at[c, k], tz_recv.at[c, k],
                ep=other * 2 + x,
            )
            copy.start()
            last[c].append(copy)

    def settle():
        for copy in backs:
            copy.wait()
        mixed = [tokens[p].astype(f32) for p in range(ep_count)]
        square = sum(jnp.sum(m * m, axis=1, keepdims=True) for m in mixed)
        inv_rms = lax.rsqrt(square / features + epsilon)
        for p in range(ep_count):
            at = slice(p * width, (p + 1) * width)
            attn_ref[:, at] = (mixed[p] * inv_rms * gain_ref[:, at]).astype(bf16)

    for c in range(steps + lags[2]):
        if c < steps:
            product(c)
        if 0 <= c - lags[0] < steps:
            joined(c - lags[0])
        if 0 <= c - lags[1] < steps:
            crossed(c - lags[1])
        if 0 <= c - lags[2] < steps:
            along(c - lags[2])
    settle()
    for c in range(steps):
        value = line[c, z].astype(f32)
        for j, copy in enumerate(last[c]):
            copy.wait()
            value = value + line_in[c, j + 1].astype(f32)
        out_ref[:, c * wide : (c + 1) * wide] = value.astype(bf16)


def on_device_dense(
    queries, keys, values, log_decay, out_gain, out_proj, experts, gates, up_weight, down_weight
):
    f32, bf16 = jnp.float32, jnp.bfloat16
    dma = pltpu.SemaphoreType.DMA
    seg_count, ep_count = lax.axis_size("seg"), lax.axis_size("ep")
    y_count, half = seg_count // 2, ep_count // 2
    tokens_own, features = queries.shape
    heads = log_decay.shape[1]
    width = features // ep_count
    dim = width // heads
    moe_own = experts.shape[0]
    seg_rows = moe_own * ep_count
    total = seg_rows * seg_count
    cols = out_proj.shape[1]
    model, units = up_weight.shape[1:]
    tile = math.gcd(cols, 512)
    wide = tile
    steps = model // wide
    vmem = pl.BlockSpec(memory_space=pltpu.VMEM)
    hbm = pl.BlockSpec(memory_space=pl.ANY)
    return pl.pallas_call(
        functools.partial(step_kernel, seg_count, ep_count, heads, dim, tile, wide, (1, 3, 5)),
        out_shape=(
            jax.ShapeDtypeStruct((tokens_own, features), bf16),
            jax.ShapeDtypeStruct((moe_own, model), bf16),
        ),
        in_specs=[hbm] * 6 + [vmem] * 4,
        out_specs=(vmem, vmem),
        scratch_shapes=[VM((ep_count, tokens_own, width), bf16)] * 3
        + [
            VM((seg_count, heads, dim, dim), bf16),
            VM((seg_count, 8, dim), f32),
            VM((seg_count, ep_count, moe_own, 128), f32),
            VM((ep_count, tokens_own, width), bf16),
            VM((units, model), bf16),
            VM((units, model), bf16),
            VM((width, cols), bf16),
            VM((seg_count, seg_rows, width), bf16),
            VM((seg_count, 2, half, moe_own, cols + 128), bf16),
            VM((seg_count, half, moe_own, cols + 128), bf16),
            VM((seg_count, half, moe_own, cols + 128), bf16),
            VM((seg_count, half, moe_own, cols + 128), bf16),
            VM((seg_count, seg_count, ep_count, moe_own, cols), bf16),
            VM((total, units), f32),
            VM((total, units), bf16),
            VM((ep_count, tokens_own, width), bf16),
            VM((steps, seg_count, seg_rows, wide), bf16),
            VM((steps, y_count, seg_rows, wide), bf16),
            VM((steps, y_count, 2, half, moe_own, wide), bf16),
            VM((steps, y_count, 2, half, moe_own, wide), bf16),
            VM((steps, y_count, half, moe_own, wide), bf16),
            VM((steps, max(2, y_count), half, moe_own, wide), bf16),
            VM((steps, half, moe_own, wide), bf16),
            VM((steps, half, moe_own, wide), bf16),
            dma((6,)),
        ]
        + [dma((3, ep_count))] * 2
        + [dma((ep_count,))] * 2
        + [dma((seg_count,))] * 6
        + [dma((y_count, 2))] * 2
        + [dma((seg_count, cols // tile))] * 2
        + [dma((seg_count, cols // tile, half))] * 2
        + [dma((half,))] * 2
        + [dma((half, y_count))] * 2
        + [dma((half, 2, y_count))] * 4
        + [dma((ep_count,))] * 2
        + [dma((steps, y_count))] * 4
        + [dma((steps,))] * 2
        + [dma((steps, half))] * 2,
        compiler_params=pltpu.CompilerParams(
            collective_id=1, has_side_effects=True, vmem_limit_bytes=62 * 2**20
        ),
    )(
        queries, keys, values, out_proj, jnp.swapaxes(up_weight, 1, 2), down_weight,
        log_decay.T, experts.T, gates.T, out_gain[None, :],
    )


def on_device(*args):
    experts, ep_count = args[6], lax.axis_size("ep")
    full_rows = max(2, 4 * experts.shape[0] // (ep_count // 2)) >= experts.shape[0]
    return (on_device_dense if full_rows else on_device_routed)(*args)


def solution(mesh):
    placed = (
        P(("seg", "ep"), None),
        P(("seg", "ep"), None),
        P(("seg", "ep"), None),
        P("seg", "ep"),
        P(),
        P("ep", "seg"),
        P(("seg", "ep"), None),
        P(("seg", "ep"), None),
        P("ep", None, "seg"),
        P("ep", "seg", None),
    )
    return jax.shard_map(
        on_device,
        mesh=mesh,
        in_specs=placed,
        out_specs=(P(("seg", "ep"), None), P(("seg", "ep"), None)),
        check_vma=False,
    )
```

```python
import functools
import math

import jax
import jax.numpy as jnp
from jax import lax
from jax.experimental import pallas as pl
from jax.experimental.pallas import tpu as pltpu
from jax.sharding import PartitionSpec as P

epsilon = 1e-06
MESH = pl.DeviceIdType.MESH
VM = pltpu.VMEM


def prefix(x, axis, join, neutral):
    place = lax.axis_index(axis)
    gathered = jax.tree.map(
        lambda a, kind: lax.all_gather(a.astype(kind), axis), x, (jnp.bfloat16, jnp.bfloat16)
    )
    state = jax.tree.map(lambda a, e: jnp.zeros_like(a) + jnp.asarray(e, a.dtype), x, neutral)

    def one(turn, state):
        return join(
            state,
            jax.tree.map(
                lambda a, own: lax.dynamic_index_in_dim(a, turn, 0, False).astype(own.dtype),
                gathered,
                x,
            ),
        )

    return lax.fori_loop(0, place, one, state)


def chain_combine(first_part, second_part):
    return (
        first_part[0] * second_part[0],
        second_part[0][:, None, None] * first_part[1] + second_part[1],
    )


def route_tables(experts, gates, expert_count, capacity):
    token_count = experts.shape[0]
    flattened = experts.reshape(-1)
    onehot = (flattened[:, None] == jnp.arange(expert_count, dtype=jnp.int32)[None, :]).astype(
        jnp.int32
    )
    earlier = jnp.cumsum(onehot, axis=0) - onehot
    position = jnp.sum(earlier * onehot, axis=1)
    slot_index = (flattened * capacity + position).reshape(token_count, 2)
    columns = jnp.arange(expert_count * capacity, dtype=jnp.int32)
    matches = slot_index[:, :, None] == columns[None, None, :]
    dispatch = jnp.any(matches, axis=1).T.astype(jnp.bfloat16)
    combine = jnp.sum(jnp.where(matches, gates[:, :, None], 0.0), axis=1)
    return (dispatch, combine)


def expert_output(row_data, up_piece, down_piece):
    hidden = jax.nn.silu(jnp.dot(row_data, up_piece, preferred_element_type=jnp.float32)).astype(
        jnp.bfloat16
    )
    return jnp.dot(hidden, down_piece, preferred_element_type=jnp.float32)


def on_device_routed(
    queries, keys, values, log_decay, out_gain, out_proj, experts, gates, up_weight, down_weight
):
    highest = lax.Precision.HIGHEST
    ep_count = lax.axis_size("ep")
    heads_local = log_decay.shape[1]
    head_dim = queries.shape[1] // (heads_local * ep_count)
    query_heads, key_heads, value_heads = (
        lax.all_to_all(queries, "ep", split_axis=1, concat_axis=0, tiled=True),
        lax.all_to_all(keys, "ep", split_axis=1, concat_axis=0, tiled=True),
        lax.all_to_all(values, "ep", split_axis=1, concat_axis=0, tiled=True),
    )
    seg_length = query_heads.shape[0]
    query_heads = query_heads.reshape(seg_length, heads_local, head_dim)
    key_heads = key_heads.reshape(seg_length, heads_local, head_dim)
    value_heads = value_heads.reshape(seg_length, heads_local, head_dim)
    cumulative = jnp.cumsum(log_decay, axis=0)
    across = cumulative.T
    block_size = math.gcd(seg_length, 512)
    starts = jnp.arange(seg_length // block_size, dtype=jnp.int32) * block_size
    token_positions = jnp.arange(seg_length, dtype=jnp.int32)

    def block_mix(start):
        query_block = lax.dynamic_slice_in_dim(query_heads, start, block_size, 0)
        cum_block = lax.dynamic_slice_in_dim(across, start, block_size, 1)
        row_ids = start + jnp.arange(block_size, dtype=jnp.int32)
        causal = (row_ids[:, None] >= token_positions[None, :])[None]
        log_gap = cum_block[:, :, None] - across[:, None, :]
        weight = jnp.where(causal, jnp.exp(jnp.where(causal, log_gap, 0.0)), 0.0)
        scores = jnp.einsum(
            "thd,shd->hts", query_block, key_heads, preferred_element_type=jnp.float32
        )
        mixing = (scores * weight).astype(jnp.bfloat16)
        return jnp.einsum("hts,she->the", mixing, value_heads, preferred_element_type=jnp.float32)

    inside = lax.map(block_mix, starts).reshape(seg_length, heads_local, head_dim)
    ending = cumulative[-1]
    to_end = jnp.exp(ending[None, :] - cumulative)
    key_float = key_heads.astype(jnp.float32)
    value_float = value_heads.astype(jnp.float32)
    local_state = jnp.einsum("sh,shd,she->hde", to_end, key_float, value_float, precision=highest)
    identity = (jnp.ones_like(ending), jnp.zeros_like(local_state))
    carried = prefix((jnp.exp(ending), local_state), "seg", chain_combine, identity)[1]
    outside = jnp.exp(cumulative)[:, :, None] * jnp.einsum(
        "thd,hde->the", query_heads.astype(jnp.float32), carried, precision=highest
    )
    mixture = (inside + outside).astype(jnp.bfloat16).reshape(seg_length, heads_local * head_dim)
    token_mix = lax.all_to_all(mixture, "ep", split_axis=0, concat_axis=1, tiled=True)
    as_float = token_mix.astype(jnp.float32)
    inv_rms = lax.rsqrt(jnp.mean(as_float * as_float, axis=1, keepdims=True) + epsilon)
    attn_out = (as_float * inv_rms * out_gain[None, :]).astype(jnp.bfloat16)
    row_stride = 8
    own_width = heads_local * head_dim
    feature_count = own_width * ep_count
    picked_float = mixture.reshape(seg_length // row_stride, row_stride, own_width)[:, 0].astype(
        jnp.float32
    )
    square_sums = lax.psum(jnp.sum(picked_float * picked_float, axis=1), "ep")
    picked_rms = lax.rsqrt(square_sums[:, None] / feature_count + epsilon)
    gain_slice = lax.dynamic_slice_in_dim(out_gain, lax.axis_index("ep") * own_width, own_width, 0)
    normed_rows = (picked_float * picked_rms * gain_slice[None, :]).astype(jnp.bfloat16)
    proj_terms = jnp.dot(
        normed_rows,
        lax.all_gather(out_proj, "seg", axis=1, tiled=True),
        preferred_element_type=jnp.float32,
    )
    moe_in = lax.psum_scatter(
        proj_terms.astype(jnp.bfloat16), "ep", scatter_dimension=0, tiled=True
    )
    expert_count = ep_count // 2
    token_count, model_width = moe_in.shape
    capacity = max(2, 4 * token_count // expert_count)
    dispatch, combine = route_tables(experts, gates, expert_count, capacity)
    up_piece = up_weight[0]
    down_piece = down_weight[0]
    slot_rows = jnp.dot(dispatch, moe_in, preferred_element_type=jnp.float32).astype(jnp.bfloat16)
    outgoing = jnp.repeat(slot_rows.reshape(expert_count, capacity, model_width), 2, axis=0)
    arrived = lax.all_to_all(outgoing, "ep", split_axis=0, concat_axis=0, tiled=True).reshape(
        ep_count * capacity, model_width
    )
    gathered = lax.all_gather(arrived, "seg", axis=0, tiled=True)
    owned_sums = lax.psum_scatter(
        expert_output(gathered, up_piece, down_piece).astype(jnp.bfloat16),
        "seg",
        scatter_dimension=0,
        tiled=True,
    ).astype(jnp.float32)
    returned_back = lax.all_to_all(
        owned_sums.reshape(ep_count, capacity, model_width).astype(jnp.bfloat16),
        "ep",
        split_axis=0,
        concat_axis=0,
        tiled=True,
    ).astype(jnp.float32)
    paired = returned_back.reshape(expert_count, 2, capacity, model_width)
    halves = (paired[:, 0] + paired[:, 1]).reshape(expert_count * capacity, model_width)
    summed = jnp.dot(combine, halves, precision=highest)
    moe_out = summed.astype(jnp.bfloat16)
    return (attn_out, moe_out)


def remote(src, dst, send, recv, **target):
    return pltpu.make_async_remote_copy(
        src_ref=src, dst_ref=dst, send_sem=send, recv_sem=recv,
        device_id=target, device_id_type=MESH,
    )


def greet(seg_count, ep_count):
    seg, ep = lax.axis_index("seg"), lax.axis_index("ep")
    barrier = pltpu.get_barrier_semaphore()
    for j in range(1, ep_count):
        pl.semaphore_signal(
            barrier, inc=1, device_id={"ep": lax.rem(ep + j, ep_count)}, device_id_type=MESH
        )
    for k in range(1, seg_count):
        pl.semaphore_signal(
            barrier, inc=1, device_id={"seg": lax.rem(seg + k, seg_count)}, device_id_type=MESH
        )
    pl.semaphore_wait(barrier, ep_count + seg_count - 2)
    return seg, ep


def step_kernel(
    seg_count, ep_count, heads, dim, tile, wide, lags, by_x,
    q_ref, k_ref, v_ref, proj_hbm, up_hbm, down_hbm,
    turned_hbm, experts_hbm, gates_hbm, gain_hbm,
    attn_hbm, out_hbm,
    turned_ref, experts_ref, gates_ref, gain_ref, attn_ref, out_ref,
    kvb, qb, q_own, q_out, q_in, states, ends, table_ref, mix_ref,
    up, down, proj, rows, part, x_sum, z_part, z_in, full, acc, hidden, tokens,
    terms, core_in, both, y_in, x_in, middle, line, line_in,
    load_sem, one_send, one_recv, pick_recv, rx_recv, rz_recv,
    ag_recv, x_recv, y_recv, xy_recv, c_recv, tc_recv, ty_recv, tx_recv, tz_recv,
):
    f32, bf16 = jnp.float32, jnp.bfloat16
    smalls = [
        pltpu.make_async_copy(src, dst, load_sem.at[4 + i])
        for i, (src, dst) in enumerate(
            (
                (turned_hbm, turned_ref), (experts_hbm, experts_ref), (gates_hbm, gates_ref),
                (gain_hbm, gain_ref),
            )
        )
    ]
    early = pltpu.make_async_copy(q_ref, q_own, load_sem.at[3])
    early.start()
    for copy in smalls:
        copy.start()
    seg, ep = greet(seg_count, ep_count)
    width = heads * dim
    tokens_own, moe_own = q_ref.shape[0], experts_ref.shape[1]
    y_count, half = seg_count // 2, ep_count // 2
    core, y = lax.rem(seg, 2), lax.div(seg, 2)
    x, z = lax.rem(ep, 2), lax.div(ep, 2)
    x_mate = ep + 1 - 2 * x
    mate = seg + 1 - 2 * core

    def seg_at(d, i):
        return lax.rem(y + d + 2 * y_count, y_count) * 2 + (core if i == 0 else 1 - core)

    own = pl.ds(pl.multiple_of(ep * width, width), width)
    pending = []

    def waiter(ref, recv, **target):
        return remote(ref, ref, one_send.at[0], recv, **target)

    def collect(ref, recv):
        waiter(ref, recv, ep=x_mate).wait_recv()

    def later(ref, index):
        pending.append(remote(ref, ref, one_send.at[index], one_recv.at[0], ep=x_mate))

    def scatter(ref, buf, index):
        for j in range(1, ep_count):
            other = lax.rem(ep + j, ep_count)
            columns = pl.ds(pl.multiple_of(other * width, width), width)
            remote(
                ref.at[:, columns], buf.at[ep], one_send.at[index], one_recv.at[index], ep=other
            ).start()
        pltpu.make_async_copy(ref.at[:, own], buf.at[ep], one_recv.at[index]).start()

    others = pl.ds(1, ep_count - 1)
    other_segs = pl.ds(1, seg_count - 1)
    scatter(k_ref, kvb.at[0], 0)
    scatter(v_ref, kvb.at[1], 0)
    later(kvb.at[:, others], 0)
    loads = [
        pltpu.make_async_copy(proj_hbm, proj, load_sem.at[0]),
        pltpu.make_async_copy(up_hbm.at[0], up, load_sem.at[1]),
        pltpu.make_async_copy(down_hbm.at[0], down, load_sem.at[2]),
    ]
    for load in loads:
        load.start()
    stride = tokens_own // moe_own
    few = (
        lax.broadcasted_iota(jnp.int32, (moe_own, tokens_own), 1)
        == stride * lax.broadcasted_iota(jnp.int32, (moe_own, tokens_own), 0)
    )
    early.wait()
    chosen = jnp.dot(
        few.astype(f32).astype(bf16), q_own[...], preferred_element_type=f32
    ).astype(bf16)
    for p in range(ep_count):
        q_out[p] = chosen[:, p * width : (p + 1) * width]
    for j in range(1, ep_count):
        other = lax.rem(ep + j, ep_count)
        remote(q_out.at[other], q_in.at[ep], one_send.at[2], one_recv.at[2], ep=other).start()
    later(q_in.at[others], 2)
    q_in[ep] = q_out[ep]
    for copy in smalls:
        copy.wait()
    lanes = lax.broadcasted_iota(jnp.int32, (moe_own, 128), 1).astype(f32)
    corner = (
        lax.broadcasted_iota(jnp.int32, (moe_own, moe_own), 0)
        == lax.broadcasted_iota(jnp.int32, (moe_own, moe_own), 1)
    )

    def upright(line):
        spread = jnp.broadcast_to(line, (moe_own, moe_own))
        return jnp.sum(jnp.where(corner, spread, 0.0), axis=1, keepdims=True)

    table_ref[seg, ep] = sum(
        jnp.where(
            upright(experts_ref[i : i + 1, :].astype(f32)) == lanes,
            upright(gates_ref[i : i + 1, :]),
            0.0,
        )
        for i in range(experts_ref.shape[0])
    )
    for j in range(1, ep_count):
        remote(
            table_ref.at[seg, ep], table_ref.at[seg, ep], one_send.at[3], one_recv.at[3],
            ep=lax.rem(ep + j, ep_count),
        ).start()
    later(table_ref.at[0, others], 3)
    length = tokens_own * ep_count
    highest = lax.Precision.HIGHEST
    rows_at = lax.broadcasted_iota(jnp.int32, (length, length), 0)
    columns_at = lax.broadcasted_iota(jnp.int32, (length, length), 1)
    causal = rows_at >= columns_at
    lower = causal.astype(f32)
    turned_decay = turned_ref[...]
    across = lax.dot_general(
        turned_decay, lower, (((1,), (1,)), ((), ())), precision=highest,
        preferred_element_type=f32,
    )
    cum = lax.dot_general(
        lower, turned_decay, (((1,), (1,)), ((), ())), precision=highest,
        preferred_element_type=f32,
    )
    count = ep_count * moe_own
    causal_few = lax.broadcasted_iota(
        jnp.int32, (count, length), 1
    ) <= stride * lax.broadcasted_iota(jnp.int32, (count, length), 0)
    cum_few = lax.dot_general(
        causal_few.astype(f32), turned_decay, (((1,), (1,)), ((), ())), precision=highest,
        preferred_element_type=f32,
    )
    collect(kvb, one_recv.at[0])
    keys, values = (
        jnp.concatenate([kvb[i, p] for p in range(ep_count)], axis=0) for i in range(2)
    )
    ending = cum[length - 1 : length, :]
    unit = (
        lax.broadcasted_iota(jnp.int32, (dim, dim), 0)
        == lax.broadcasted_iota(jnp.int32, (dim, dim), 1)
    ).astype(f32).astype(bf16)
    for h in range(heads):
        cols = slice(h * dim, (h + 1) * dim)
        to_end = jnp.exp(ending[:, h : h + 1] - across[h : h + 1, :])
        turned = lax.dot_general(
            unit, keys[:, cols], (((1,), (1,)), ((), ())), preferred_element_type=f32
        )
        states[seg, h] = jnp.dot(
            (turned * to_end).astype(bf16), values[:, cols],
            preferred_element_type=f32,
        ).astype(bf16)
        ends[seg, h : h + 1] = jnp.broadcast_to(ending[:, h : h + 1], (1, dim))
    for k in range(1, seg_count):
        other = lax.rem(seg + k, seg_count)
        for buf, index in ((states, 4), (ends, 5)):
            remote(
                buf.at[seg], buf.at[seg], one_send.at[index], one_recv.at[index], seg=other
            ).start()
    later(states.at[other_segs], 4)
    later(ends.at[other_segs], 5)

    def within(asked, mask, cum, h):
        cols = slice(h * dim, (h + 1) * dim)
        gap = cum[:, h : h + 1] - across[h : h + 1, :]
        weight = jnp.where(mask, jnp.exp(jnp.where(mask, gap, 0.0)), 0.0)
        scores = lax.dot_general(
            asked[:, cols], keys[:, cols], (((1,), (1,)), ((), ())),
            preferred_element_type=f32,
        )
        return jnp.dot(
            (scores * weight).astype(bf16), values[:, cols], preferred_element_type=f32
        )

    def before(asked, cum, h):
        cols = slice(h * dim, (h + 1) * dim)
        return jnp.exp(cum[:, h : h + 1]) * jnp.dot(
            asked[:, cols], carried[h], preferred_element_type=f32
        )

    collect(q_in.at[others], one_recv.at[2])
    asked = q_in[...].reshape(count, width)
    inside = [within(asked, causal_few, cum_few, h) for h in range(heads)]
    scatter(q_ref, qb, 1)
    later(qb.at[others], 1)
    collect(states.at[other_segs], one_recv.at[4])
    collect(ends.at[other_segs], one_recv.at[5])
    carried = []
    for h in range(heads):
        joined = jnp.zeros((dim, dim), f32)
        for c in range(seg_count):
            after = jnp.exp(ends[c, h : h + 1]) * joined + states[c, h].astype(f32)
            joined = jnp.where(c < seg, after, joined)
        carried.append(joined.astype(bf16))
    for h in range(heads):
        rows[seg, :, h * dim : (h + 1) * dim] = (
            inside[h] + before(asked, cum_few, h)
        ).astype(bf16)

    def mix_all():
        collect(qb, one_recv.at[1])
        queries = jnp.concatenate([qb[p] for p in range(ep_count)], axis=0)
        for h in range(heads):
            value = within(queries, causal, cum, h) + before(queries, cum, h)
            mix_ref[:, :, h * dim : (h + 1) * dim] = value.astype(bf16).reshape(
                ep_count, tokens_own, dim
            )

    own_rows = rows.shape[1]
    total = own_rows * seg_count
    mine = own_rows // ep_count
    cols = proj.shape[1]
    features = width * ep_count
    sources = [(d, i) for d in range(y_count) for i in range(2)]
    row_moves = {}
    for d, i in sources[1:]:
        row_moves[d, i] = remote(
            rows.at[seg], rows.at[seg], one_send.at[6], pick_recv.at[d * 2 + i - 1],
            seg=seg_at(d, i),
        )
        row_moves[d, i].start()
    later(rows.at[other_segs], 6)
    lane = lax.broadcasted_iota(jnp.int32, (own_rows, 128), 1)
    pieces = {n: [(0, cols + 128)] for n in range(seg_count)}
    pieces[0] = [(t, tile) for t in range(0, cols - tile, tile)] + [(cols - tile, tile + 128)]
    x_moves = {}

    def source(n):
        d, i = sources[n]
        return seg_at(-d, i)

    def project(n):
        if n:
            row_moves[sources[n]].wait_recv()
        picked = rows[source(n)].astype(f32)
        squares = jnp.sum(picked * picked, axis=1, keepdims=True)
        high = squares.astype(bf16).astype(f32)
        pair = jnp.where(lane < 64, high, squares - high).reshape(half, 2, mine, 128).astype(bf16)
        scaled = (picked * gain_ref[:, own]).astype(bf16)
        for i in range(2):
            part[n, i, :, :, cols:] = pair[:, i]
        for p, (at, size) in enumerate(pieces[n]):
            for t in range(at, min(at + size, cols), tile):
                value = (
                    jnp.dot(scaled, proj[:, t : t + tile], preferred_element_type=f32)
                    .reshape(half, 2, mine, tile)
                    .astype(bf16)
                )
                for i in range(2):
                    part[n, i, :, :, t : t + tile] = value[:, i]
            span = pl.ds(at, size)
            x_moves[n, p] = remote(
                part.at[n, 1 - x, :, :, span], x_sum.at[n, :, :, span],
                one_send.at[7], rx_recv.at[(n + len(pieces[0]) - 1 if n else p)], ep=x_mate,
            )
            x_moves[n, p].start()

    def combine(n):
        for p, (at, size) in enumerate(pieces[n]):
            x_moves[n, p].wait_recv()
            span = pl.ds(at, size)
            value = part[n, x, :, :, span].astype(f32) + x_sum[n, :, :, span].astype(f32)
            z_part[n, :, :, span] = value.astype(bf16)
            if at + size > cols:
                pair = value[:, :, size - 128 :].reshape(half * mine, 128)
                squares = pair[:, :1] + pair[:, 64:65]
                high = squares.astype(bf16).astype(f32)
                pair = jnp.where(lane[: half * mine] < 64, high, squares - high).astype(bf16)
                z_part[n, :, :, cols:] = pair.reshape(half, mine, 128)
            for k in range(1, half):
                other = lax.rem(z + k, half)
                remote(
                    z_part.at[n, other, :, span], z_in.at[n, k, :, span],
                    one_send.at[8], rz_recv.at[n], ep=other * 2 + x,
                ).start()

    def finish(n):
        collect(z_in.at[n, pl.ds(1, half - 1)], rz_recv.at[n])
        value = z_part[n, z].astype(f32)
        for k in range(1, half):
            value = value + z_in[n, k].astype(f32)
        square = value[:, cols : cols + 1] + value[:, cols + 64 : cols + 65]
        inv_rms = lax.rsqrt(square / features + epsilon)
        full[seg, source(n), ep] = (value[:, :cols] * inv_rms).astype(bf16)

    loads[0].wait()
    project(0)
    later(x_sum, 7)
    later(z_in.at[:, pl.ds(1, half - 1)], 8)
    collect(table_ref.at[0, others], one_recv.at[3])
    for k in range(1, seg_count):
        remote(
            table_ref.at[seg], table_ref.at[seg], one_send.at[9], one_recv.at[9],
            seg=lax.rem(seg + k, seg_count),
        ).start()
    later(table_ref.at[other_segs], 9)
    def send(place, index, recv_sem, **target):
        copy = remote(place, place, one_send.at[index], recv_sem, **target)
        copy.start()
        return copy

    def on_line(e, k):
        return lax.rem(e - 2 * k + ep_count, ep_count)

    def y_seg(k):
        return seg_at(k, 0)

    def block(n, d, e):
        at, i = sources[n]
        return full.at[y_seg(-d), seg_at(-d - at, i), e]

    z_copies, x_copies, y_copies = {}, {}, {}

    def spread(n, k):
        if k > 0:
            z_copies[n, k].wait_recv()
        place = block(n, 0, on_line(ep, k))
        x_copies[n, k] = send(place, 11, x_recv.at[n, k], ep=x_mate)
        for d in range(1, y_count):
            y_copies[n, k, d] = send(place, 12, y_recv.at[n, k, d - 1], seg=y_seg(d))
        send(place, 15, c_recv.at[0], seg=mate)

    def gather_z(n):
        for k in range(1, half):
            z_copies[n, k] = send(
                block(n, 0, ep), 10, ag_recv.at[n, k - 1], ep=lax.rem(ep + 2 * k, ep_count)
            )
        spread(n, 0)

    def gather_xy(n):
        for k in range(1, half):
            spread(n, k)

    def relay(n):
        for k in range(half):
            x_copies[n, k].wait_recv()
            place = block(n, 0, on_line(x_mate, k))
            if k not in by_x:
                for d in range(1, y_count):
                    send(place, 13, xy_recv.at[n, 0], seg=y_seg(d))
            send(place, 15, c_recv.at[0], seg=mate)
            for d in range(1, y_count):
                y_copies[n, k, d].wait_recv()
                place = block(n, d, on_line(ep, k))
                if k in by_x:
                    send(place, 14, xy_recv.at[n, 1], ep=x_mate)
                send(place, 15, c_recv.at[d], seg=mate)

    by_y = [k for k in range(half) if k not in by_x]

    def blocks(count):
        return full.at[0, 0, pl.ds(0, count)]

    def hand_over(n):
        for i, ks in enumerate((by_y, by_x)):
            if ks and y_count > 1:
                collect(blocks(len(ks) * (y_count - 1)), xy_recv.at[n, i])
            for k in ks:
                for d in range(1, y_count):
                    send(block(n, d, on_line(x_mate, k)), 15, c_recv.at[d], seg=mate)

    later(full.at[0, :, pl.ds(0, half - 1)], 10)
    later(full.at[0, :, pl.ds(0, half)], 11)
    if y_count > 1:
        later(full.at[0, :, pl.ds(0, half * (y_count - 1))], 12)
        for i, ks in enumerate((by_y, by_x)):
            if ks:
                later(full.at[0, :, pl.ds(0, len(ks) * (y_count - 1))], 13 + i)
    later(full.at[pl.ds(0, y_count)], 15)

    def attend():
        mix_all()

    for stage, n in (
        (project, 1), (combine, 0), (project, 2), (project, 3), (combine, 1), (attend, None),
        (combine, 2), (finish, 0), (gather_z, 0), (combine, 3), (finish, 1), (gather_z, 1),
        (gather_xy, 0), (finish, 2), (gather_z, 2), (gather_xy, 1), (relay, 0),
        (finish, 3), (gather_z, 3), (gather_xy, 2), (relay, 1), (gather_xy, 3), (hand_over, 0),
        (relay, 2), (hand_over, 1), (relay, 3),
    ):
        stage(*([] if n is None else [n]))
    loads[1].wait()
    acc[...] = jnp.zeros_like(acc)

    def multiply(s):
        def step(n, carry):
            at = pl.multiple_of(n * tile, tile)
            block = full[s, :, :, :, pl.ds(at, tile)].reshape(total, tile)
            lines = pl.ds(pl.multiple_of(s * cols + n * tile, tile), tile)
            acc[...] += lax.dot_general(
                block, up[:, lines], (((1,), (1,)), ((), ())), preferred_element_type=f32
            )
            return carry

        lax.fori_loop(0, cols // tile, step, 0)

    multiply(seg)
    for n in range(2, seg_count):
        hand_over(n)
    for d in range(1, y_count):
        multiply(y_seg(-d))
    tokens[ep] = mix_ref[ep]
    for j in range(1, ep_count):
        other = lax.rem(ep + j, ep_count)
        remote(
            mix_ref.at[other], tokens.at[ep], one_send.at[16], one_recv.at[16], ep=other
        ).start()
    later(tokens.at[others], 16)
    for k in range(y_count):
        waiter(full.at[0], c_recv.at[k], seg=mate).wait_recv()
        multiply(seg_at(-k, 1))
    value = acc[...]
    hidden[...] = (value / (1.0 + jnp.exp(-value))).astype(bf16)
    collect(table_ref.at[other_segs], one_recv.at[9])
    table = table_ref[...].reshape(total, 128)
    lane = lax.broadcasted_iota(jnp.int32, (total, 128), 1)
    gate = jnp.sum(jnp.where(lane == z, table, 0.0), axis=1, keepdims=True)
    loads[2].wait()
    steps = seg_count * cols // wide
    core_moves = {}

    def product(c):
        value = jnp.dot(
            hidden[...], down[:, c * wide : (c + 1) * wide], preferred_element_type=f32
        )
        value = jnp.where(gate != 0.0, value * gate, 0.0).astype(bf16)
        terms[c] = value.reshape(y_count, 2, own_rows, wide)
        remote(
            terms.at[c, :, 1 - core], core_in.at[c], one_send.at[17], tc_recv.at[c], seg=mate
        ).start()

    later(core_in, 17)
    def joined(c):
        waiter(core_in.at[c], tc_recv.at[c], seg=mate).wait_recv()
        for k in range(y_count):
            value = (terms[c, k, core].astype(f32) + core_in[c, k].astype(f32)).reshape(
                half, 2, mine, wide
            ).astype(bf16)
            for i in range(2):
                both[c, k, i] = value[:, i]
        if c % 2 == 0:
            for d in range(1, y_count):
                remote(
                    both.at[c, lax.rem(y + d, y_count)], y_in.at[c, d],
                    one_send.at[18], ty_recv.at[c], seg=y_seg(d),
                ).start()
        else:
            remote(
                both.at[c, :, 1 - x], x_in.at[c, pl.ds(0, y_count)], one_send.at[19],
                tx_recv.at[c], ep=x_mate,
            ).start()

    other_ys = pl.ds(1, y_count - 1)
    evens, odds = pl.ds(0, (steps + 1) // 2), pl.ds(0, steps // 2)
    later(y_in.at[evens, other_ys], 18)
    later(x_in.at[odds, pl.ds(0, y_count)], 19)

    def crossed(c):
        if c % 2 == 0:
            collect(y_in.at[c, other_ys], ty_recv.at[c])
            for i in range(2):
                value = both[c, y, i].astype(f32)
                for d in range(1, y_count):
                    value = value + y_in[c, d, i].astype(f32)
                middle[c, i] = value.astype(bf16)
            remote(
                middle.at[c, 1 - x], x_in.at[c, 0], one_send.at[20], tx_recv.at[c], ep=x_mate
            ).start()
        else:
            collect(x_in.at[c, pl.ds(0, y_count)], tx_recv.at[c])
            for k in range(y_count):
                middle[c, k] = (both[c, k, x].astype(f32) + x_in[c, k].astype(f32)).astype(bf16)
            for d in range(1, y_count):
                remote(
                    middle.at[c, lax.rem(y + d, y_count)], y_in.at[c, d, 0],
                    one_send.at[21], ty_recv.at[c], seg=y_seg(d),
                ).start()

    later(x_in.at[evens, 0], 20)
    later(y_in.at[odds, other_ys, 0], 21)

    def along(c):
        if c % 2 == 0:
            collect(x_in.at[c, 0], tx_recv.at[c])
            value = middle[c, x].astype(f32) + x_in[c, 0].astype(f32)
        else:
            collect(y_in.at[c, other_ys, 0], ty_recv.at[c])
            value = middle[c, y].astype(f32)
            for d in range(1, y_count):
                value = value + y_in[c, d, 0].astype(f32)
        line[c] = value.astype(bf16)
        for k in range(1, half):
            other = lax.rem(z + k, half)
            remote(
                line.at[c, other], line_in.at[c, k], one_send.at[22], tz_recv.at[c],
                ep=other * 2 + x,
            ).start()

    later(line_in.at[:, pl.ds(1, half - 1)], 22)

    def settle():
        collect(tokens.at[others], one_recv.at[16])
        mixed = [tokens[p].astype(f32) for p in range(ep_count)]
        square = sum(jnp.sum(m * m, axis=1, keepdims=True) for m in mixed)
        inv_rms = lax.rsqrt(square / features + epsilon)
        for p in range(ep_count):
            at = slice(p * width, (p + 1) * width)
            attn_ref[:, at] = (mixed[p] * inv_rms * gain_ref[:, at]).astype(bf16)
        result.start()

    result = pltpu.make_async_copy(attn_ref, attn_hbm, load_sem.at[8])
    for c in range(steps + lags[2]):
        if c < steps:
            product(c)
        if 0 <= c - lags[0] < steps:
            joined(c - lags[0])
        if 0 <= c - lags[1] < steps:
            crossed(c - lags[1])
        if 0 <= c - lags[2] < steps:
            along(c - lags[2])
    settle()
    for c in range(steps):
        value = line[c, z].astype(f32)
        collect(line_in.at[c, pl.ds(1, half - 1)], tz_recv.at[c])
        for k in range(1, half):
            value = value + line_in[c, k].astype(f32)
        out_ref[:, c * wide : (c + 1) * wide] = value.astype(bf16)
    whole = pltpu.make_async_copy(out_ref, out_hbm, load_sem.at[9])
    whole.start()
    for copy in pending:
        copy.wait_send()
    result.wait()
    whole.wait()


def carry_kernel(a_in, b_in, a_out, b_out, a_held, b_held, sem):
    inward = [
        pltpu.make_async_copy(src, held, sem.at[0, i])
        for i, (src, held) in enumerate(((a_in, a_held), (b_in, b_held)))
    ]
    outward = [
        pltpu.make_async_copy(held, dst, sem.at[1, i])
        for i, (held, dst) in enumerate(((a_held, a_out), (b_held, b_out)))
    ]
    for copy in inward:
        copy.start()
    for copy, after in zip(inward, outward):
        copy.wait()
        after.start()
    for copy in outward:
        copy.wait()


def on_device_dense(
    queries, keys, values, log_decay, out_gain, out_proj, experts, gates, up_weight, down_weight
):
    f32, bf16 = jnp.float32, jnp.bfloat16
    dma = pltpu.SemaphoreType.DMA
    seg_count, ep_count = lax.axis_size("seg"), lax.axis_size("ep")
    y_count, half = seg_count // 2, ep_count // 2
    tokens_own, features = queries.shape
    heads = log_decay.shape[1]
    width = features // ep_count
    dim = width // heads
    moe_own = experts.shape[0]
    seg_rows = moe_own * ep_count
    total = seg_rows * seg_count
    cols = out_proj.shape[1]
    model, units = up_weight.shape[1:]
    tile = math.gcd(cols, 512)
    wide = tile
    steps = model // wide
    hbm = pl.BlockSpec(memory_space=pl.ANY)
    results = pl.pallas_call(
        functools.partial(step_kernel, seg_count, ep_count, heads, dim, tile, wide, (1, 6, 11), tuple(range(1, half, 2))),
        out_shape=(
            jax.ShapeDtypeStruct((tokens_own, features), bf16),
            jax.ShapeDtypeStruct((moe_own, model), bf16),
        ),
        in_specs=[hbm] * 10,
        out_specs=(hbm, hbm),
        scratch_shapes=[
            VM((heads, log_decay.shape[0]), f32),
            VM((experts.shape[1], moe_own), jnp.int32),
            VM((experts.shape[1], moe_own), f32),
            VM((1, features), f32),
            VM((tokens_own, features), bf16),
            VM((moe_own, model), bf16),
            VM((2, ep_count, tokens_own, width), bf16),
            VM((ep_count, tokens_own, width), bf16),
            VM((tokens_own, features), bf16),
            VM((ep_count, moe_own, width), bf16),
            VM((ep_count, moe_own, width), bf16),
            VM((seg_count, heads, dim, dim), bf16),
            VM((seg_count, 8, dim), f32),
            VM((seg_count, ep_count, moe_own, 128), f32),
            VM((ep_count, tokens_own, width), bf16),
            VM((units, model), bf16),
            VM((units, model), bf16),
            VM((width, cols), bf16),
            VM((seg_count, seg_rows, width), bf16),
            VM((seg_count, 2, half, moe_own, cols + 128), bf16),
            VM((seg_count, half, moe_own, cols + 128), bf16),
            VM((seg_count, half, moe_own, cols + 128), bf16),
            VM((seg_count, half, moe_own, cols + 128), bf16),
            VM((seg_count, seg_count, ep_count, moe_own, cols), bf16),
            VM((total, units), f32),
            VM((total, units), bf16),
            VM((ep_count, tokens_own, width), bf16),
            VM((steps, y_count, 2, seg_rows, wide), bf16),
            VM((steps, y_count, seg_rows, wide), bf16),
            VM((steps, y_count, 2, half, moe_own, wide), bf16),
            VM((steps, y_count, 2, half, moe_own, wide), bf16),
            VM((steps, max(2, y_count), half, moe_own, wide), bf16),
            VM((steps, max(2, y_count), half, moe_own, wide), bf16),
            VM((steps, half, moe_own, wide), bf16),
            VM((steps, half, moe_own, wide), bf16),
            dma((10,)),
            dma((23,)),
            dma((17,)),
            dma((seg_count - 1,)),
            dma((seg_count - 1 + cols // tile,)),
            dma((seg_count,)),
            dma((seg_count, half - 1)),
            dma((seg_count, half)),
            dma((seg_count, half, max(1, y_count - 1))),
            dma((seg_count, 2)),
            dma((y_count,)),
        ]
        + [dma((steps,))] * 4,
        compiler_params=pltpu.CompilerParams(
            collective_id=1, has_side_effects=True, vmem_limit_bytes=62 * 2**20
        ),
    )(
        queries, keys, values, out_proj, jnp.swapaxes(up_weight, 1, 2), down_weight,
        log_decay.T, experts.T, gates.T, out_gain[None, :],
    )
    return pl.pallas_call(
        carry_kernel,
        out_shape=tuple(jax.ShapeDtypeStruct(r.shape, r.dtype) for r in results),
        in_specs=[hbm] * 2,
        out_specs=(hbm, hbm),
        scratch_shapes=[VM(r.shape, r.dtype) for r in results] + [dma((2, 2))],
    )(*results)


def on_device(*args):
    experts, ep_count = args[6], lax.axis_size("ep")
    full_rows = max(2, 4 * experts.shape[0] // (ep_count // 2)) >= experts.shape[0]
    return (on_device_dense if full_rows else on_device_routed)(*args)


def solution(mesh):
    placed = (
        P(("seg", "ep"), None),
        P(("seg", "ep"), None),
        P(("seg", "ep"), None),
        P("seg", "ep"),
        P(),
        P("ep", "seg"),
        P(("seg", "ep"), None),
        P(("seg", "ep"), None),
        P("ep", None, "seg"),
        P("ep", "seg", None),
    )
    return jax.shard_map(
        on_device,
        mesh=mesh,
        in_specs=placed,
        out_specs=(P(("seg", "ep"), None), P(("seg", "ep"), None)),
        check_vma=False,
    )
```

```python
import functools
import math

import jax
import jax.numpy as jnp
from jax import lax
from jax.experimental import pallas as pl
from jax.experimental.pallas import tpu as pltpu
from jax.sharding import PartitionSpec as P

epsilon = 1e-06
BYX = (1, 3)
PACE = ((2.8, 0.71, 3.2, 9.7, 2.5, 3.2, 0.5, 6.0, 11.5), (2.8, 0.71, 3.2, 6.4, 2.5, 3.2, 0.5, 6.0, 13.0))
MESH = pl.DeviceIdType.MESH
VM = pltpu.VMEM


def prefix(x, axis, join, neutral):
    place = lax.axis_index(axis)
    gathered = jax.tree.map(
        lambda a, kind: lax.all_gather(a.astype(kind), axis), x, (jnp.bfloat16, jnp.bfloat16)
    )
    state = jax.tree.map(lambda a, e: jnp.zeros_like(a) + jnp.asarray(e, a.dtype), x, neutral)

    def one(turn, state):
        return join(
            state,
            jax.tree.map(
                lambda a, own: lax.dynamic_index_in_dim(a, turn, 0, False).astype(own.dtype),
                gathered,
                x,
            ),
        )

    return lax.fori_loop(0, place, one, state)


def chain_combine(first_part, second_part):
    return (
        first_part[0] * second_part[0],
        second_part[0][:, None, None] * first_part[1] + second_part[1],
    )


def route_tables(experts, gates, expert_count, capacity):
    token_count = experts.shape[0]
    flattened = experts.reshape(-1)
    onehot = (flattened[:, None] == jnp.arange(expert_count, dtype=jnp.int32)[None, :]).astype(
        jnp.int32
    )
    earlier = jnp.cumsum(onehot, axis=0) - onehot
    position = jnp.sum(earlier * onehot, axis=1)
    slot_index = (flattened * capacity + position).reshape(token_count, 2)
    columns = jnp.arange(expert_count * capacity, dtype=jnp.int32)
    matches = slot_index[:, :, None] == columns[None, None, :]
    dispatch = jnp.any(matches, axis=1).T.astype(jnp.bfloat16)
    combine = jnp.sum(jnp.where(matches, gates[:, :, None], 0.0), axis=1)
    return (dispatch, combine)


def expert_output(row_data, up_piece, down_piece):
    hidden = jax.nn.silu(jnp.dot(row_data, up_piece, preferred_element_type=jnp.float32)).astype(
        jnp.bfloat16
    )
    return jnp.dot(hidden, down_piece, preferred_element_type=jnp.float32)


def on_device_routed(
    queries, keys, values, log_decay, out_gain, out_proj, experts, gates, up_weight, down_weight
):
    highest = lax.Precision.HIGHEST
    ep_count = lax.axis_size("ep")
    heads_local = log_decay.shape[1]
    head_dim = queries.shape[1] // (heads_local * ep_count)
    query_heads, key_heads, value_heads = (
        lax.all_to_all(queries, "ep", split_axis=1, concat_axis=0, tiled=True),
        lax.all_to_all(keys, "ep", split_axis=1, concat_axis=0, tiled=True),
        lax.all_to_all(values, "ep", split_axis=1, concat_axis=0, tiled=True),
    )
    seg_length = query_heads.shape[0]
    query_heads = query_heads.reshape(seg_length, heads_local, head_dim)
    key_heads = key_heads.reshape(seg_length, heads_local, head_dim)
    value_heads = value_heads.reshape(seg_length, heads_local, head_dim)
    cumulative = jnp.cumsum(log_decay, axis=0)
    across = cumulative.T
    block_size = math.gcd(seg_length, 512)
    starts = jnp.arange(seg_length // block_size, dtype=jnp.int32) * block_size
    token_positions = jnp.arange(seg_length, dtype=jnp.int32)

    def block_mix(start):
        query_block = lax.dynamic_slice_in_dim(query_heads, start, block_size, 0)
        cum_block = lax.dynamic_slice_in_dim(across, start, block_size, 1)
        row_ids = start + jnp.arange(block_size, dtype=jnp.int32)
        causal = (row_ids[:, None] >= token_positions[None, :])[None]
        log_gap = cum_block[:, :, None] - across[:, None, :]
        weight = jnp.where(causal, jnp.exp(jnp.where(causal, log_gap, 0.0)), 0.0)
        scores = jnp.einsum(
            "thd,shd->hts", query_block, key_heads, preferred_element_type=jnp.float32
        )
        mixing = (scores * weight).astype(jnp.bfloat16)
        return jnp.einsum("hts,she->the", mixing, value_heads, preferred_element_type=jnp.float32)

    inside = lax.map(block_mix, starts).reshape(seg_length, heads_local, head_dim)
    ending = cumulative[-1]
    to_end = jnp.exp(ending[None, :] - cumulative)
    key_float = key_heads.astype(jnp.float32)
    value_float = value_heads.astype(jnp.float32)
    local_state = jnp.einsum("sh,shd,she->hde", to_end, key_float, value_float, precision=highest)
    identity = (jnp.ones_like(ending), jnp.zeros_like(local_state))
    carried = prefix((jnp.exp(ending), local_state), "seg", chain_combine, identity)[1]
    outside = jnp.exp(cumulative)[:, :, None] * jnp.einsum(
        "thd,hde->the", query_heads.astype(jnp.float32), carried, precision=highest
    )
    mixture = (inside + outside).astype(jnp.bfloat16).reshape(seg_length, heads_local * head_dim)
    token_mix = lax.all_to_all(mixture, "ep", split_axis=0, concat_axis=1, tiled=True)
    as_float = token_mix.astype(jnp.float32)
    inv_rms = lax.rsqrt(jnp.mean(as_float * as_float, axis=1, keepdims=True) + epsilon)
    attn_out = (as_float * inv_rms * out_gain[None, :]).astype(jnp.bfloat16)
    row_stride = 8
    own_width = heads_local * head_dim
    feature_count = own_width * ep_count
    picked_float = mixture.reshape(seg_length // row_stride, row_stride, own_width)[:, 0].astype(
        jnp.float32
    )
    square_sums = lax.psum(jnp.sum(picked_float * picked_float, axis=1), "ep")
    picked_rms = lax.rsqrt(square_sums[:, None] / feature_count + epsilon)
    gain_slice = lax.dynamic_slice_in_dim(out_gain, lax.axis_index("ep") * own_width, own_width, 0)
    normed_rows = (picked_float * picked_rms * gain_slice[None, :]).astype(jnp.bfloat16)
    proj_terms = jnp.dot(
        normed_rows,
        lax.all_gather(out_proj, "seg", axis=1, tiled=True),
        preferred_element_type=jnp.float32,
    )
    moe_in = lax.psum_scatter(
        proj_terms.astype(jnp.bfloat16), "ep", scatter_dimension=0, tiled=True
    )
    expert_count = ep_count // 2
    token_count, model_width = moe_in.shape
    capacity = max(2, 4 * token_count // expert_count)
    dispatch, combine = route_tables(experts, gates, expert_count, capacity)
    up_piece = up_weight[0]
    down_piece = down_weight[0]
    slot_rows = jnp.dot(dispatch, moe_in, preferred_element_type=jnp.float32).astype(jnp.bfloat16)
    outgoing = jnp.repeat(slot_rows.reshape(expert_count, capacity, model_width), 2, axis=0)
    arrived = lax.all_to_all(outgoing, "ep", split_axis=0, concat_axis=0, tiled=True).reshape(
        ep_count * capacity, model_width
    )
    gathered = lax.all_gather(arrived, "seg", axis=0, tiled=True)
    owned_sums = lax.psum_scatter(
        expert_output(gathered, up_piece, down_piece).astype(jnp.bfloat16),
        "seg",
        scatter_dimension=0,
        tiled=True,
    ).astype(jnp.float32)
    returned_back = lax.all_to_all(
        owned_sums.reshape(ep_count, capacity, model_width).astype(jnp.bfloat16),
        "ep",
        split_axis=0,
        concat_axis=0,
        tiled=True,
    ).astype(jnp.float32)
    paired = returned_back.reshape(expert_count, 2, capacity, model_width)
    halves = (paired[:, 0] + paired[:, 1]).reshape(expert_count * capacity, model_width)
    summed = jnp.dot(combine, halves, precision=highest)
    moe_out = summed.astype(jnp.bfloat16)
    return (attn_out, moe_out)


def remote(src, dst, send, recv, **target):
    return pltpu.make_async_remote_copy(
        src_ref=src, dst_ref=dst, send_sem=send, recv_sem=recv,
        device_id=target, device_id_type=MESH,
    )


def greet(seg_count, ep_count):
    seg, ep = lax.axis_index("seg"), lax.axis_index("ep")
    barrier = pltpu.get_barrier_semaphore()
    for j in range(1, ep_count):
        pl.semaphore_signal(
            barrier, inc=1, device_id={"ep": lax.rem(ep + j, ep_count)}, device_id_type=MESH
        )
    for k in range(1, seg_count):
        pl.semaphore_signal(
            barrier, inc=1, device_id={"seg": lax.rem(seg + k, seg_count)}, device_id_type=MESH
        )
    pl.semaphore_wait(barrier, ep_count + seg_count - 2)
    return seg, ep


def step_kernel(
    seg_count, ep_count, heads, dim, tile, wide, lags, by_x, pace,
    q_ref, k_ref, v_ref, proj_hbm, up_hbm, down_hbm,
    turned_hbm, experts_hbm, gates_hbm, gain_hbm,
    attn_hbm, out_hbm,
    turned_ref, experts_ref, gates_ref, gain_ref, attn_ref, out_ref,
    kvb, qb, q_own, q_out, q_in, states, ends, table_ref, mix_ref,
    up, down, proj, rows, part, x_sum, z_part, chain_in, near_out, far_out, scale_ref, full, acc, hidden, tokens,
    terms, core_in, both, y_in, x_in, middle, line, line_in,
    load_sem, one_send, one_recv, pick_recv, rx_recv, chain_recv,
    x_recv, y_recv, xy_recv, c_recv, tc_recv, ty_recv, tx_recv, tz_recv,
):
    f32, bf16 = jnp.float32, jnp.bfloat16
    smalls = [
        pltpu.make_async_copy(src, dst, load_sem.at[4 + i])
        for i, (src, dst) in enumerate(
            (
                (turned_hbm, turned_ref), (experts_hbm, experts_ref), (gates_hbm, gates_ref),
                (gain_hbm, gain_ref),
            )
        )
    ]
    early = pltpu.make_async_copy(q_ref, q_own, load_sem.at[3])
    early.start()
    for copy in smalls:
        copy.start()
    seg, ep = greet(seg_count, ep_count)
    width = heads * dim
    tokens_own, moe_own = q_ref.shape[0], experts_ref.shape[1]
    y_count, half = seg_count // 2, ep_count // 2
    core, y = lax.rem(seg, 2), lax.div(seg, 2)
    x, z = lax.rem(ep, 2), lax.div(ep, 2)
    x_mate = ep + 1 - 2 * x
    mate = seg + 1 - 2 * core

    nearer = jnp.where(z * 2 < half, 0, 1)
    at_end = (z == 0) | (z == half - 1)
    ahead = (z + 1 - 2 * nearer) * 2 + x
    behind = (z - 1 + 2 * nearer) * 2 + x

    def seg_at(d, i):
        return lax.rem(y + d + 2 * y_count, y_count) * 2 + (core if i == 0 else 1 - core)

    own = pl.ds(pl.multiple_of(ep * width, width), width)
    pending = []

    def waiter(ref, recv, **target):
        return remote(ref, ref, one_send.at[0], recv, **target)

    def collect(ref, recv):
        waiter(ref, recv, ep=x_mate).wait_recv()

    def later(ref, index):
        pending.append(remote(ref, ref, one_send.at[index], one_recv.at[0], ep=x_mate))

    def scatter(ref, buf, index):
        for j in range(1, ep_count):
            other = lax.rem(ep + j, ep_count)
            columns = pl.ds(pl.multiple_of(other * width, width), width)
            remote(
                ref.at[:, columns], buf.at[ep], one_send.at[index], one_recv.at[index], ep=other
            ).start()
        pltpu.make_async_copy(ref.at[:, own], buf.at[ep], one_recv.at[index]).start()

    others = pl.ds(1, ep_count - 1)
    other_segs = pl.ds(1, seg_count - 1)
    scatter(k_ref, kvb.at[0], 0)
    scatter(v_ref, kvb.at[1], 0)
    later(kvb.at[:, others], 0)
    loads = [
        pltpu.make_async_copy(proj_hbm, proj, load_sem.at[0]),
        pltpu.make_async_copy(up_hbm.at[0], up, load_sem.at[1]),
        pltpu.make_async_copy(down_hbm.at[0], down, load_sem.at[2]),
    ]
    for load in loads:
        load.start()
    stride = tokens_own // moe_own
    few = (
        lax.broadcasted_iota(jnp.int32, (moe_own, tokens_own), 1)
        == stride * lax.broadcasted_iota(jnp.int32, (moe_own, tokens_own), 0)
    )
    early.wait()
    chosen = jnp.dot(
        few.astype(f32).astype(bf16), q_own[...], preferred_element_type=f32
    ).astype(bf16)
    for p in range(ep_count):
        q_out[p] = chosen[:, p * width : (p + 1) * width]
    for j in range(1, ep_count):
        other = lax.rem(ep + j, ep_count)
        remote(q_out.at[other], q_in.at[ep], one_send.at[2], one_recv.at[2], ep=other).start()
    later(q_in.at[others], 2)
    q_in[ep] = q_out[ep]
    for copy in smalls:
        copy.wait()
    lanes = lax.broadcasted_iota(jnp.int32, (moe_own, 128), 1).astype(f32)
    corner = (
        lax.broadcasted_iota(jnp.int32, (moe_own, moe_own), 0)
        == lax.broadcasted_iota(jnp.int32, (moe_own, moe_own), 1)
    )

    def upright(line):
        spread = jnp.broadcast_to(line, (moe_own, moe_own))
        return jnp.sum(jnp.where(corner, spread, 0.0), axis=1, keepdims=True)

    table_ref[seg, ep] = sum(
        jnp.where(
            upright(experts_ref[i : i + 1, :].astype(f32)) == lanes,
            upright(gates_ref[i : i + 1, :]),
            0.0,
        )
        for i in range(experts_ref.shape[0])
    )
    for j in range(1, ep_count):
        remote(
            table_ref.at[seg, ep], table_ref.at[seg, ep], one_send.at[3], one_recv.at[3],
            ep=lax.rem(ep + j, ep_count),
        ).start()
    later(table_ref.at[0, others], 3)
    length = tokens_own * ep_count
    highest = lax.Precision.HIGHEST
    rows_at = lax.broadcasted_iota(jnp.int32, (length, length), 0)
    columns_at = lax.broadcasted_iota(jnp.int32, (length, length), 1)
    causal = rows_at >= columns_at
    lower = causal.astype(f32)
    turned_decay = turned_ref[...]
    across = lax.dot_general(
        turned_decay, lower, (((1,), (1,)), ((), ())), precision=highest,
        preferred_element_type=f32,
    )
    cum = lax.dot_general(
        lower, turned_decay, (((1,), (1,)), ((), ())), precision=highest,
        preferred_element_type=f32,
    )
    count = ep_count * moe_own
    causal_few = lax.broadcasted_iota(
        jnp.int32, (count, length), 1
    ) <= stride * lax.broadcasted_iota(jnp.int32, (count, length), 0)
    cum_few = lax.dot_general(
        causal_few.astype(f32), turned_decay, (((1,), (1,)), ((), ())), precision=highest,
        preferred_element_type=f32,
    )
    collect(kvb, one_recv.at[0])
    keys, values = (
        jnp.concatenate([kvb[i, p] for p in range(ep_count)], axis=0) for i in range(2)
    )
    ending = cum[length - 1 : length, :]
    unit = (
        lax.broadcasted_iota(jnp.int32, (dim, dim), 0)
        == lax.broadcasted_iota(jnp.int32, (dim, dim), 1)
    ).astype(f32).astype(bf16)
    for h in range(heads):
        cols = slice(h * dim, (h + 1) * dim)
        to_end = jnp.exp(ending[:, h : h + 1] - across[h : h + 1, :])
        turned = lax.dot_general(
            unit, keys[:, cols], (((1,), (1,)), ((), ())), preferred_element_type=f32
        )
        states[seg, h] = jnp.dot(
            (turned * to_end).astype(bf16), values[:, cols],
            preferred_element_type=f32,
        ).astype(bf16)
        ends[seg, h : h + 1] = jnp.broadcast_to(ending[:, h : h + 1], (1, dim))
    for k in range(1, seg_count):
        other = lax.rem(seg + k, seg_count)
        for buf, index in ((states, 4), (ends, 5)):
            remote(
                buf.at[seg], buf.at[seg], one_send.at[index], one_recv.at[index], seg=other
            ).start()
    later(states.at[other_segs], 4)
    later(ends.at[other_segs], 5)

    def within(asked, mask, cum, h):
        cols = slice(h * dim, (h + 1) * dim)
        gap = cum[:, h : h + 1] - across[h : h + 1, :]
        weight = jnp.where(mask, jnp.exp(jnp.where(mask, gap, 0.0)), 0.0)
        scores = lax.dot_general(
            asked[:, cols], keys[:, cols], (((1,), (1,)), ((), ())),
            preferred_element_type=f32,
        )
        return jnp.dot(
            (scores * weight).astype(bf16), values[:, cols], preferred_element_type=f32
        )

    def before(asked, cum, h):
        cols = slice(h * dim, (h + 1) * dim)
        return jnp.exp(cum[:, h : h + 1]) * jnp.dot(
            asked[:, cols], carried[h], preferred_element_type=f32
        )

    collect(q_in.at[others], one_recv.at[2])
    asked = q_in[...].reshape(count, width)
    inside = [within(asked, causal_few, cum_few, h) for h in range(heads)]
    scatter(q_ref, qb, 1)
    later(qb.at[others], 1)
    collect(states.at[other_segs], one_recv.at[4])
    collect(ends.at[other_segs], one_recv.at[5])
    carried = []
    for h in range(heads):
        joined = jnp.zeros((dim, dim), f32)
        for c in range(seg_count):
            after = jnp.exp(ends[c, h : h + 1]) * joined + states[c, h].astype(f32)
            joined = jnp.where(c < seg, after, joined)
        carried.append(joined.astype(bf16))
    for h in range(heads):
        rows[seg, :, h * dim : (h + 1) * dim] = (
            inside[h] + before(asked, cum_few, h)
        ).astype(bf16)

    def mix_all():
        collect(qb, one_recv.at[1])
        queries = jnp.concatenate([qb[p] for p in range(ep_count)], axis=0)
        for h in range(heads):
            value = within(queries, causal, cum, h) + before(queries, cum, h)
            mix_ref[:, :, h * dim : (h + 1) * dim] = value.astype(bf16).reshape(
                ep_count, tokens_own, dim
            )

    own_rows = rows.shape[1]
    total = own_rows * seg_count
    mine = own_rows // ep_count
    cols = proj.shape[1]
    features = width * ep_count
    sources = [(d, i) for d in range(y_count) for i in range(2)]
    row_moves = {}
    for d, i in sources[1:]:
        row_moves[d, i] = remote(
            rows.at[seg], rows.at[seg], one_send.at[6], pick_recv.at[d * 2 + i - 1],
            seg=seg_at(d, i),
        )
        row_moves[d, i].start()
    later(rows.at[other_segs], 6)
    lane = lax.broadcasted_iota(jnp.int32, (own_rows, 128), 1)
    pieces = [(0, 128 + tile)] + [(128 + t, tile) for t in range(tile, cols, tile)]
    x_moves = {}

    def source(n):
        d, i = sources[n]
        return seg_at(-d, i)

    def project(end, n):
        if n:
            row_moves[sources[n]].wait_recv()
        picked = rows[source(n)].astype(f32)
        squares = jnp.sum(picked * picked, axis=1, keepdims=True)
        high = squares.astype(bf16).astype(f32)
        pair = jnp.where(lane < 64, high, squares - high).reshape(half, 2, mine, 128).astype(bf16)
        scaled = (picked * gain_ref[:, own]).astype(bf16)
        for i in range(2):
            part[n, i, :, :, :128] = pair[:, i]
        for p, (at, size) in enumerate(pieces):
            t = p * tile
            value = (
                jnp.dot(scaled, proj[:, t : t + tile], preferred_element_type=f32)
                .reshape(half, 2, mine, tile)
                .astype(bf16)
            )
            for i in range(2):
                part[n, i, :, :, 128 + t : 128 + t + tile] = value[:, i]
            span = pl.ds(at, size)
            x_moves[n, p] = remote(
                part.at[n, 1 - x, :, :, span], x_sum.at[n, :, :, span],
                one_send.at[7], rx_recv.at[n, p], ep=x_mate,
            )
            x_moves[n, p].start()

    short_lane = lane[: half * mine]

    def keep_sum(ref, n, p, value):
        at, size = pieces[p]
        ref[n, :, :, pl.ds(at, size)] = value.astype(bf16)
        if p == 0:
            pair = value[:, :, :128].reshape(half * mine, 128)
            squares = pair[:, :1] + pair[:, 64:65]
            high = squares.astype(bf16).astype(f32)
            pair = jnp.where(short_lane < 64, high, squares - high).astype(bf16)
            ref[n, :, :, :128] = pair.reshape(half, mine, 128)

    def combine(end, n, p):
        span = pl.ds(*pieces[p])
        x_moves[n, p].wait_recv()
        value = part[n, x, :, :, span].astype(f32) + x_sum[n, :, :, span].astype(f32)
        keep_sum(z_part, n, p, value)
        if end:
            remote(
                z_part.at[n, :, :, span], chain_in.at[nearer, n, :, :, span],
                one_send.at[8], chain_recv.at[nearer, n, p], ep=ahead,
            ).start()

    def near(end, n, p):
        if end:
            return
        span = pl.ds(*pieces[p])
        collect(x_sum.at[n, :, :, span], chain_recv.at[nearer, n, p])
        value = z_part[n, :, :, span].astype(f32)
        value = value + chain_in[nearer, n, :, :, span].astype(f32)
        keep_sum(near_out, n, p, value)
        remote(
            near_out.at[n, :, :, span], chain_in.at[nearer, n, :, :, span],
            one_send.at[8], chain_recv.at[nearer, n, p], ep=ahead,
        ).start()

    def far(end, n, p):
        at, size = pieces[p]
        span = pl.ds(at, size)
        collect(x_sum.at[n, :, :, span], chain_recv.at[1 - nearer, n, p])

        def settled(value):
            if p == 0:
                square = value[:, :, :1] + value[:, :, 64:65]
                scale_ref[n] = jnp.broadcast_to(
                    lax.rsqrt(square / features + epsilon), (half, mine, 128)
                )
                value = value[:, :, 128:]
            value = (value * scale_ref[n][:, :, :1]).astype(bf16)
            start = max(at - 128, 0)
            for k in range(half):
                full[seg, source(n), k * 2 + x, :, start : start + tile] = value[k]

        value = z_part[n, :, :, span].astype(f32)
        value = value + chain_in[1 - nearer, n, :, :, span].astype(f32)
        if not end:
            keep_sum(far_out, n, p, value)
            remote(
                far_out.at[n, :, :, span], chain_in.at[1 - nearer, n, :, :, span],
                one_send.at[10], chain_recv.at[1 - nearer, n, p], ep=behind,
            ).start()
            value = value + chain_in[nearer, n, :, :, span].astype(f32)
        settled(value)

    loads[0].wait()
    project(None, 0)
    later(x_sum, 7)
    later(x_sum, 8)
    collect(table_ref.at[0, others], one_recv.at[3])
    for k in range(1, seg_count):
        remote(
            table_ref.at[seg], table_ref.at[seg], one_send.at[9], one_recv.at[9],
            seg=lax.rem(seg + k, seg_count),
        ).start()
    later(table_ref.at[other_segs], 9)
    def send(place, index, recv_sem, **target):
        copy = remote(place, place, one_send.at[index], recv_sem, **target)
        copy.start()
        return copy

    def on_line(e, k):
        return k * 2 + lax.rem(e, 2)

    def y_seg(k):
        return seg_at(k, 0)

    def block(n, d, e):
        at, i = sources[n]
        return full.at[y_seg(-d), seg_at(-d - at, i), e]

    x_copies, y_copies = {}, {}

    def spread(end, n):
        for k in range(half):
            place = block(n, 0, on_line(ep, k))
            x_copies[n, k] = send(place, 11, x_recv.at[n, k], ep=x_mate)
            for d in range(1, y_count):
                y_copies[n, k, d] = send(place, 12, y_recv.at[n, k, d - 1], seg=y_seg(d))
            send(place, 15, c_recv.at[0], seg=mate)

    def relay(end, n, k):
        x_copies[n, k].wait_recv()
        place = block(n, 0, on_line(x_mate, k))
        if k not in by_x:
            for d in range(1, y_count):
                send(place, 13, xy_recv.at[n, 0], seg=y_seg(d))
        send(place, 15, c_recv.at[0], seg=mate)
        for d in range(1, y_count):
            y_copies[n, k, d].wait_recv()
            place = block(n, d, on_line(ep, k))
            if k in by_x:
                send(place, 14, xy_recv.at[n, 1], ep=x_mate)
            send(place, 15, c_recv.at[d], seg=mate)

    by_y = [k for k in range(half) if k not in by_x]

    def blocks(count):
        return full.at[0, 0, pl.ds(0, count)]

    def hand_over(end, n):
        for i, ks in enumerate((by_y, by_x)):
            if ks and y_count > 1:
                collect(blocks(len(ks) * (y_count - 1)), xy_recv.at[n, i])
            for k in ks:
                for d in range(1, y_count):
                    send(block(n, d, on_line(x_mate, k)), 15, c_recv.at[d], seg=mate)

    later(full.at[0, :, pl.ds(0, half)], 11)
    if y_count > 1:
        later(full.at[0, :, pl.ds(0, half * (y_count - 1))], 12)
        for i, ks in enumerate((by_y, by_x)):
            if ks:
                later(full.at[0, :, pl.ds(0, len(ks) * (y_count - 1))], 13 + i)
    later(full.at[pl.ds(0, y_count)], 15)

    def attend(end):
        mix_all()

    def proceed(end, start, beat, near_lag, far_lag, first, relay_beat, relay_step, hand_lag, at):
        plan = [(2.0 * n, project, (n,)) for n in range(1, seg_count)] + [(at, attend, ())]
        for n in range(seg_count):
            for p in range(len(pieces)):
                time = start + beat * (n * len(pieces) + p)
                plan += [
                    (time, combine, (n, p)), (time + near_lag, near, (n, p)),
                    (time + far_lag, far, (n, p)),
                ]
            plan += [(time + far_lag + 0.01, spread, (n,))]
            ready = start + beat * (len(pieces) - 1) + far_lag + first + relay_beat * n
            plan += [(ready + relay_step * k, relay, (n, k)) for k in range(half)]
            plan += [(ready + hand_lag, hand_over, (n,))]
        for _, stage, given in sorted(plan, key=lambda item: item[0]):
            stage(end, *given)

    for end, hints in zip((True, False), pace):
        pl.when(at_end if end else jnp.logical_not(at_end))(
            functools.partial(proceed, end, *hints)
        )
    loads[1].wait()
    acc[...] = jnp.zeros_like(acc)

    def multiply(s):
        lines = pl.ds(pl.multiple_of(s * cols, cols), cols)
        acc[...] += lax.dot_general(
            full[s].reshape(total, cols), up[:, lines], (((1,), (1,)), ((), ())),
            preferred_element_type=f32,
        )

    multiply(seg)
    pass
    for d in range(1, y_count):
        multiply(y_seg(-d))
    tokens[ep] = mix_ref[ep]
    for j in range(1, ep_count):
        other = lax.rem(ep + j, ep_count)
        remote(
            mix_ref.at[other], tokens.at[ep], one_send.at[16], one_recv.at[16], ep=other
        ).start()
    later(tokens.at[others], 16)
    for k in range(y_count):
        waiter(full.at[0], c_recv.at[k], seg=mate).wait_recv()
        multiply(seg_at(-k, 1))
    value = acc[...]
    hidden[...] = (value / (1.0 + jnp.exp(-value))).astype(bf16)
    collect(table_ref.at[other_segs], one_recv.at[9])
    table = table_ref[...].reshape(total, 128)
    lane = lax.broadcasted_iota(jnp.int32, (total, 128), 1)
    gate = jnp.sum(jnp.where(lane == z, table, 0.0), axis=1, keepdims=True)
    loads[2].wait()
    steps = seg_count * cols // wide
    core_moves = {}

    def product(c):
        value = jnp.dot(
            hidden[...], down[:, c * wide : (c + 1) * wide], preferred_element_type=f32
        )
        value = jnp.where(gate != 0.0, value * gate, 0.0).astype(bf16)
        terms[c] = value.reshape(y_count, 2, own_rows, wide)
        remote(
            terms.at[c, :, 1 - core], core_in.at[c], one_send.at[17], tc_recv.at[c], seg=mate
        ).start()

    later(core_in, 17)
    def joined(c):
        waiter(core_in.at[c], tc_recv.at[c], seg=mate).wait_recv()
        for k in range(y_count):
            value = (terms[c, k, core].astype(f32) + core_in[c, k].astype(f32)).reshape(
                half, 2, mine, wide
            ).astype(bf16)
            for i in range(2):
                both[c, k, i] = value[:, i]
        if c % 2 == 0:
            for d in range(1, y_count):
                remote(
                    both.at[c, lax.rem(y + d, y_count)], y_in.at[c, d],
                    one_send.at[18], ty_recv.at[c], seg=y_seg(d),
                ).start()
        else:
            remote(
                both.at[c, :, 1 - x], x_in.at[c, pl.ds(0, y_count)], one_send.at[19],
                tx_recv.at[c], ep=x_mate,
            ).start()

    other_ys = pl.ds(1, y_count - 1)
    evens, odds = pl.ds(0, (steps + 1) // 2), pl.ds(0, steps // 2)
    later(y_in.at[evens, other_ys], 18)
    later(x_in.at[odds, pl.ds(0, y_count)], 19)

    def crossed(c):
        if c % 2 == 0:
            collect(y_in.at[c, other_ys], ty_recv.at[c])
            for i in range(2):
                value = both[c, y, i].astype(f32)
                for d in range(1, y_count):
                    value = value + y_in[c, d, i].astype(f32)
                middle[c, i] = value.astype(bf16)
            remote(
                middle.at[c, 1 - x], x_in.at[c, 0], one_send.at[20], tx_recv.at[c], ep=x_mate
            ).start()
        else:
            collect(x_in.at[c, pl.ds(0, y_count)], tx_recv.at[c])
            for k in range(y_count):
                middle[c, k] = (both[c, k, x].astype(f32) + x_in[c, k].astype(f32)).astype(bf16)
            for d in range(1, y_count):
                remote(
                    middle.at[c, lax.rem(y + d, y_count)], y_in.at[c, d, 0],
                    one_send.at[21], ty_recv.at[c], seg=y_seg(d),
                ).start()

    later(x_in.at[evens, 0], 20)
    later(y_in.at[odds, other_ys, 0], 21)

    def along(c):
        if c % 2 == 0:
            collect(x_in.at[c, 0], tx_recv.at[c])
            value = middle[c, x].astype(f32) + x_in[c, 0].astype(f32)
        else:
            collect(y_in.at[c, other_ys, 0], ty_recv.at[c])
            value = middle[c, y].astype(f32)
            for d in range(1, y_count):
                value = value + y_in[c, d, 0].astype(f32)
        line[c] = value.astype(bf16)
        for k in range(1, half):
            other = lax.rem(z + k, half)
            remote(
                line.at[c, other], line_in.at[c, k], one_send.at[22], tz_recv.at[c],
                ep=other * 2 + x,
            ).start()

    later(line_in.at[:, pl.ds(1, half - 1)], 22)

    def settle():
        collect(tokens.at[others], one_recv.at[16])
        mixed = [tokens[p].astype(f32) for p in range(ep_count)]
        square = sum(jnp.sum(m * m, axis=1, keepdims=True) for m in mixed)
        inv_rms = lax.rsqrt(square / features + epsilon)
        for p in range(ep_count):
            at = slice(p * width, (p + 1) * width)
            attn_ref[:, at] = (mixed[p] * inv_rms * gain_ref[:, at]).astype(bf16)
        result.start()

    result = pltpu.make_async_copy(attn_ref, attn_hbm, load_sem.at[8])
    for c in range(steps + lags[2]):
        if c < steps:
            product(c)
        if 0 <= c - lags[0] < steps:
            joined(c - lags[0])
        if 0 <= c - lags[1] < steps:
            crossed(c - lags[1])
        if 0 <= c - lags[2] < steps:
            along(c - lags[2])
    settle()
    for c in range(steps):
        value = line[c, z].astype(f32)
        collect(line_in.at[c, pl.ds(1, half - 1)], tz_recv.at[c])
        for k in range(1, half):
            value = value + line_in[c, k].astype(f32)
        out_ref[:, c * wide : (c + 1) * wide] = value.astype(bf16)
    whole = pltpu.make_async_copy(out_ref, out_hbm, load_sem.at[9])
    whole.start()
    for copy in pending:
        copy.wait_send()

    @pl.when(jnp.logical_not(at_end))
    def _():
        remote(x_sum, x_sum, one_send.at[10], one_recv.at[0], ep=x_mate).wait_send()

    result.wait()
    whole.wait()


def carry_kernel(a_in, b_in, a_out, b_out, a_held, b_held, sem):
    inward = [
        pltpu.make_async_copy(src, held, sem.at[0, i])
        for i, (src, held) in enumerate(((a_in, a_held), (b_in, b_held)))
    ]
    outward = [
        pltpu.make_async_copy(held, dst, sem.at[1, i])
        for i, (held, dst) in enumerate(((a_held, a_out), (b_held, b_out)))
    ]
    for copy in inward:
        copy.start()
    for copy, after in zip(inward, outward):
        copy.wait()
        after.start()
    for copy in outward:
        copy.wait()


def on_device_dense(
    queries, keys, values, log_decay, out_gain, out_proj, experts, gates, up_weight, down_weight
):
    f32, bf16 = jnp.float32, jnp.bfloat16
    dma = pltpu.SemaphoreType.DMA
    seg_count, ep_count = lax.axis_size("seg"), lax.axis_size("ep")
    y_count, half = seg_count // 2, ep_count // 2
    tokens_own, features = queries.shape
    heads = log_decay.shape[1]
    width = features // ep_count
    dim = width // heads
    moe_own = experts.shape[0]
    seg_rows = moe_own * ep_count
    total = seg_rows * seg_count
    cols = out_proj.shape[1]
    model, units = up_weight.shape[1:]
    tile = math.gcd(cols, 512)
    wide = tile
    steps = model // wide
    hbm = pl.BlockSpec(memory_space=pl.ANY)
    results = pl.pallas_call(
        functools.partial(step_kernel, seg_count, ep_count, heads, dim, tile, wide, (1, 6, 11), BYX, PACE),
        out_shape=(
            jax.ShapeDtypeStruct((tokens_own, features), bf16),
            jax.ShapeDtypeStruct((moe_own, model), bf16),
        ),
        in_specs=[hbm] * 10,
        out_specs=(hbm, hbm),
        scratch_shapes=[
            VM((heads, log_decay.shape[0]), f32),
            VM((experts.shape[1], moe_own), jnp.int32),
            VM((experts.shape[1], moe_own), f32),
            VM((1, features), f32),
            VM((tokens_own, features), bf16),
            VM((moe_own, model), bf16),
            VM((2, ep_count, tokens_own, width), bf16),
            VM((ep_count, tokens_own, width), bf16),
            VM((tokens_own, features), bf16),
            VM((ep_count, moe_own, width), bf16),
            VM((ep_count, moe_own, width), bf16),
            VM((seg_count, heads, dim, dim), bf16),
            VM((seg_count, 8, dim), f32),
            VM((seg_count, ep_count, moe_own, 128), f32),
            VM((ep_count, tokens_own, width), bf16),
            VM((units, model), bf16),
            VM((units, model), bf16),
            VM((width, cols), bf16),
            VM((seg_count, seg_rows, width), bf16),
            VM((seg_count, 2, half, moe_own, cols + 128), bf16),
            VM((seg_count, half, moe_own, cols + 128), bf16),
            VM((seg_count, half, moe_own, cols + 128), bf16),
            VM((2, seg_count, half, moe_own, cols + 128), bf16),
            VM((seg_count, half, moe_own, cols + 128), bf16),
            VM((seg_count, half, moe_own, cols + 128), bf16),
            VM((seg_count, half, moe_own, 128), f32),
            VM((seg_count, seg_count, ep_count, moe_own, cols), bf16),
            VM((total, units), f32),
            VM((total, units), bf16),
            VM((ep_count, tokens_own, width), bf16),
            VM((steps, y_count, 2, seg_rows, wide), bf16),
            VM((steps, y_count, seg_rows, wide), bf16),
            VM((steps, y_count, 2, half, moe_own, wide), bf16),
            VM((steps, y_count, 2, half, moe_own, wide), bf16),
            VM((steps, max(2, y_count), half, moe_own, wide), bf16),
            VM((steps, max(2, y_count), half, moe_own, wide), bf16),
            VM((steps, half, moe_own, wide), bf16),
            VM((steps, half, moe_own, wide), bf16),
            dma((10,)),
            dma((23,)),
            dma((17,)),
            dma((seg_count - 1,)),
            dma((seg_count, cols // tile)),
            dma((2, seg_count, cols // tile)),
            dma((seg_count, half)),
            dma((seg_count, half, max(1, y_count - 1))),
            dma((seg_count, 2)),
            dma((y_count,)),
        ]
        + [dma((steps,))] * 4,
        compiler_params=pltpu.CompilerParams(
            collective_id=1, has_side_effects=True, vmem_limit_bytes=62 * 2**20
        ),
    )(
        queries, keys, values, out_proj, jnp.swapaxes(up_weight, 1, 2), down_weight,
        log_decay.T, experts.T, gates.T, out_gain[None, :],
    )
    return pl.pallas_call(
        carry_kernel,
        out_shape=tuple(jax.ShapeDtypeStruct(r.shape, r.dtype) for r in results),
        in_specs=[hbm] * 2,
        out_specs=(hbm, hbm),
        scratch_shapes=[VM(r.shape, r.dtype) for r in results] + [dma((2, 2))],
    )(*results)


def on_device(*args):
    experts, ep_count = args[6], lax.axis_size("ep")
    full_rows = max(2, 4 * experts.shape[0] // (ep_count // 2)) >= experts.shape[0]
    return (on_device_dense if full_rows else on_device_routed)(*args)


def solution(mesh):
    placed = (
        P(("seg", "ep"), None),
        P(("seg", "ep"), None),
        P(("seg", "ep"), None),
        P("seg", "ep"),
        P(),
        P("ep", "seg"),
        P(("seg", "ep"), None),
        P(("seg", "ep"), None),
        P("ep", None, "seg"),
        P("ep", "seg", None),
    )
    return jax.shard_map(
        on_device,
        mesh=mesh,
        in_specs=placed,
        out_specs=(P(("seg", "ep"), None), P(("seg", "ep"), None)),
        check_vma=False,
    )
```

```python
import functools
import math

import jax
import jax.numpy as jnp
from jax import lax
from jax.experimental import pallas as pl
from jax.experimental.pallas import tpu as pltpu
from jax.sharding import PartitionSpec as P

epsilon = 1e-06
BYX = (1, 3)
PACE = ((2.8, 0.71, 3.2, 9.7, 2.5, 3.2, 0.5, 6.0, 11.5), (2.8, 0.71, 3.2, 6.4, 2.5, 3.2, 0.5, 6.0, 13.0))
MESH = pl.DeviceIdType.MESH
VM = pltpu.VMEM


def prefix(x, axis, join, neutral):
    place = lax.axis_index(axis)
    gathered = jax.tree.map(
        lambda a, kind: lax.all_gather(a.astype(kind), axis), x, (jnp.bfloat16, jnp.bfloat16)
    )
    state = jax.tree.map(lambda a, e: jnp.zeros_like(a) + jnp.asarray(e, a.dtype), x, neutral)

    def one(turn, state):
        return join(
            state,
            jax.tree.map(
                lambda a, own: lax.dynamic_index_in_dim(a, turn, 0, False).astype(own.dtype),
                gathered,
                x,
            ),
        )

    return lax.fori_loop(0, place, one, state)


def chain_combine(first_part, second_part):
    return (
        first_part[0] * second_part[0],
        second_part[0][:, None, None] * first_part[1] + second_part[1],
    )


def route_tables(experts, gates, expert_count, capacity):
    token_count = experts.shape[0]
    flattened = experts.reshape(-1)
    onehot = (flattened[:, None] == jnp.arange(expert_count, dtype=jnp.int32)[None, :]).astype(
        jnp.int32
    )
    earlier = jnp.cumsum(onehot, axis=0) - onehot
    position = jnp.sum(earlier * onehot, axis=1)
    slot_index = (flattened * capacity + position).reshape(token_count, 2)
    columns = jnp.arange(expert_count * capacity, dtype=jnp.int32)
    matches = slot_index[:, :, None] == columns[None, None, :]
    dispatch = jnp.any(matches, axis=1).T.astype(jnp.bfloat16)
    combine = jnp.sum(jnp.where(matches, gates[:, :, None], 0.0), axis=1)
    return (dispatch, combine)


def expert_output(row_data, up_piece, down_piece):
    hidden = jax.nn.silu(jnp.dot(row_data, up_piece, preferred_element_type=jnp.float32)).astype(
        jnp.bfloat16
    )
    return jnp.dot(hidden, down_piece, preferred_element_type=jnp.float32)


def on_device_routed(
    queries, keys, values, log_decay, out_gain, out_proj, experts, gates, up_weight, down_weight
):
    highest = lax.Precision.HIGHEST
    ep_count = lax.axis_size("ep")
    heads_local = log_decay.shape[1]
    head_dim = queries.shape[1] // (heads_local * ep_count)
    query_heads, key_heads, value_heads = (
        lax.all_to_all(queries, "ep", split_axis=1, concat_axis=0, tiled=True),
        lax.all_to_all(keys, "ep", split_axis=1, concat_axis=0, tiled=True),
        lax.all_to_all(values, "ep", split_axis=1, concat_axis=0, tiled=True),
    )
    seg_length = query_heads.shape[0]
    query_heads = query_heads.reshape(seg_length, heads_local, head_dim)
    key_heads = key_heads.reshape(seg_length, heads_local, head_dim)
    value_heads = value_heads.reshape(seg_length, heads_local, head_dim)
    cumulative = jnp.cumsum(log_decay, axis=0)
    across = cumulative.T
    block_size = math.gcd(seg_length, 512)
    starts = jnp.arange(seg_length // block_size, dtype=jnp.int32) * block_size
    token_positions = jnp.arange(seg_length, dtype=jnp.int32)

    def block_mix(start):
        query_block = lax.dynamic_slice_in_dim(query_heads, start, block_size, 0)
        cum_block = lax.dynamic_slice_in_dim(across, start, block_size, 1)
        row_ids = start + jnp.arange(block_size, dtype=jnp.int32)
        causal = (row_ids[:, None] >= token_positions[None, :])[None]
        log_gap = cum_block[:, :, None] - across[:, None, :]
        weight = jnp.where(causal, jnp.exp(jnp.where(causal, log_gap, 0.0)), 0.0)
        scores = jnp.einsum(
            "thd,shd->hts", query_block, key_heads, preferred_element_type=jnp.float32
        )
        mixing = (scores * weight).astype(jnp.bfloat16)
        return jnp.einsum("hts,she->the", mixing, value_heads, preferred_element_type=jnp.float32)

    inside = lax.map(block_mix, starts).reshape(seg_length, heads_local, head_dim)
    ending = cumulative[-1]
    to_end = jnp.exp(ending[None, :] - cumulative)
    key_float = key_heads.astype(jnp.float32)
    value_float = value_heads.astype(jnp.float32)
    local_state = jnp.einsum("sh,shd,she->hde", to_end, key_float, value_float, precision=highest)
    identity = (jnp.ones_like(ending), jnp.zeros_like(local_state))
    carried = prefix((jnp.exp(ending), local_state), "seg", chain_combine, identity)[1]
    outside = jnp.exp(cumulative)[:, :, None] * jnp.einsum(
        "thd,hde->the", query_heads.astype(jnp.float32), carried, precision=highest
    )
    mixture = (inside + outside).astype(jnp.bfloat16).reshape(seg_length, heads_local * head_dim)
    token_mix = lax.all_to_all(mixture, "ep", split_axis=0, concat_axis=1, tiled=True)
    as_float = token_mix.astype(jnp.float32)
    inv_rms = lax.rsqrt(jnp.mean(as_float * as_float, axis=1, keepdims=True) + epsilon)
    attn_out = (as_float * inv_rms * out_gain[None, :]).astype(jnp.bfloat16)
    row_stride = 8
    own_width = heads_local * head_dim
    feature_count = own_width * ep_count
    picked_float = mixture.reshape(seg_length // row_stride, row_stride, own_width)[:, 0].astype(
        jnp.float32
    )
    square_sums = lax.psum(jnp.sum(picked_float * picked_float, axis=1), "ep")
    picked_rms = lax.rsqrt(square_sums[:, None] / feature_count + epsilon)
    gain_slice = lax.dynamic_slice_in_dim(out_gain, lax.axis_index("ep") * own_width, own_width, 0)
    normed_rows = (picked_float * picked_rms * gain_slice[None, :]).astype(jnp.bfloat16)
    proj_terms = jnp.dot(
        normed_rows,
        lax.all_gather(out_proj, "seg", axis=1, tiled=True),
        preferred_element_type=jnp.float32,
    )
    moe_in = lax.psum_scatter(
        proj_terms.astype(jnp.bfloat16), "ep", scatter_dimension=0, tiled=True
    )
    expert_count = ep_count // 2
    token_count, model_width = moe_in.shape
    capacity = max(2, 4 * token_count // expert_count)
    dispatch, combine = route_tables(experts, gates, expert_count, capacity)
    up_piece = up_weight[0]
    down_piece = down_weight[0]
    slot_rows = jnp.dot(dispatch, moe_in, preferred_element_type=jnp.float32).astype(jnp.bfloat16)
    outgoing = jnp.repeat(slot_rows.reshape(expert_count, capacity, model_width), 2, axis=0)
    arrived = lax.all_to_all(outgoing, "ep", split_axis=0, concat_axis=0, tiled=True).reshape(
        ep_count * capacity, model_width
    )
    gathered = lax.all_gather(arrived, "seg", axis=0, tiled=True)
    owned_sums = lax.psum_scatter(
        expert_output(gathered, up_piece, down_piece).astype(jnp.bfloat16),
        "seg",
        scatter_dimension=0,
        tiled=True,
    ).astype(jnp.float32)
    returned_back = lax.all_to_all(
        owned_sums.reshape(ep_count, capacity, model_width).astype(jnp.bfloat16),
        "ep",
        split_axis=0,
        concat_axis=0,
        tiled=True,
    ).astype(jnp.float32)
    paired = returned_back.reshape(expert_count, 2, capacity, model_width)
    halves = (paired[:, 0] + paired[:, 1]).reshape(expert_count * capacity, model_width)
    summed = jnp.dot(combine, halves, precision=highest)
    moe_out = summed.astype(jnp.bfloat16)
    return (attn_out, moe_out)


def remote(src, dst, send, recv, **target):
    return pltpu.make_async_remote_copy(
        src_ref=src, dst_ref=dst, send_sem=send, recv_sem=recv,
        device_id=target, device_id_type=MESH,
    )


def greet(seg_count, ep_count):
    seg, ep = lax.axis_index("seg"), lax.axis_index("ep")
    barrier = pltpu.get_barrier_semaphore()
    for j in range(1, ep_count):
        pl.semaphore_signal(
            barrier, inc=1, device_id={"ep": lax.rem(ep + j, ep_count)}, device_id_type=MESH
        )
    for k in range(1, seg_count):
        pl.semaphore_signal(
            barrier, inc=1, device_id={"seg": lax.rem(seg + k, seg_count)}, device_id_type=MESH
        )
    pl.semaphore_wait(barrier, ep_count + seg_count - 2)
    return seg, ep


def step_kernel(
    seg_count, ep_count, heads, dim, tile, wide, lags, by_x, pace,
    q_ref, k_ref, v_ref, proj_hbm, up_hbm, down_hbm,
    turned_hbm, experts_hbm, gates_hbm, gain_hbm,
    attn_hbm, out_hbm,
    turned_ref, experts_ref, gates_ref, gain_ref, attn_ref, out_ref,
    kvb, qb, q_own, q_out, q_in, states, ends, table_ref, mix_ref,
    up, down, proj, rows, part, x_sum, z_part, chain_in, near_out, far_out, scale_ref, full, acc, hidden, tokens,
    terms, core_in, both, y_in, x_in, middle, line, line_in,
    load_sem, one_send, one_recv, pick_recv, rx_recv, chain_recv,
    x_recv, y_recv, xy_recv, c_recv, tc_recv, ty_recv, tx_recv, tz_recv,
):
    f32, bf16 = jnp.float32, jnp.bfloat16
    smalls = [
        pltpu.make_async_copy(src, dst, load_sem.at[4 + i])
        for i, (src, dst) in enumerate(
            (
                (turned_hbm, turned_ref), (experts_hbm, experts_ref), (gates_hbm, gates_ref),
                (gain_hbm, gain_ref),
            )
        )
    ]
    early = pltpu.make_async_copy(q_ref, q_own, load_sem.at[3])
    early.start()
    for copy in smalls:
        copy.start()
    seg, ep = greet(seg_count, ep_count)
    width = heads * dim
    tokens_own, moe_own = q_ref.shape[0], experts_ref.shape[1]
    y_count, half = seg_count // 2, ep_count // 2
    core, y = lax.rem(seg, 2), lax.div(seg, 2)
    x, z = lax.rem(ep, 2), lax.div(ep, 2)
    x_mate = ep + 1 - 2 * x
    mate = seg + 1 - 2 * core

    nearer = jnp.where(z * 2 < half, 0, 1)
    at_end = (z == 0) | (z == half - 1)
    ahead = (z + 1 - 2 * nearer) * 2 + x
    behind = (z - 1 + 2 * nearer) * 2 + x

    def seg_at(d, i):
        return lax.rem(y + d + 2 * y_count, y_count) * 2 + (core if i == 0 else 1 - core)

    own = pl.ds(pl.multiple_of(ep * width, width), width)
    pending = []

    def waiter(ref, recv, **target):
        return remote(ref, ref, one_send.at[0], recv, **target)

    def collect(ref, recv):
        waiter(ref, recv, ep=x_mate).wait_recv()

    def later(ref, index):
        pending.append(remote(ref, ref, one_send.at[index], one_recv.at[0], ep=x_mate))

    def scatter(ref, buf, index):
        for j in range(1, ep_count):
            other = lax.rem(ep + j, ep_count)
            columns = pl.ds(pl.multiple_of(other * width, width), width)
            remote(
                ref.at[:, columns], buf.at[ep], one_send.at[index], one_recv.at[index], ep=other
            ).start()
        pltpu.make_async_copy(ref.at[:, own], buf.at[ep], one_recv.at[index]).start()

    others = pl.ds(1, ep_count - 1)
    other_segs = pl.ds(1, seg_count - 1)
    scatter(k_ref, kvb.at[0], 0)
    scatter(v_ref, kvb.at[1], 0)
    later(kvb.at[:, others], 0)
    loads = [
        pltpu.make_async_copy(proj_hbm, proj, load_sem.at[0]),
        pltpu.make_async_copy(up_hbm.at[0], up, load_sem.at[1]),
        pltpu.make_async_copy(down_hbm.at[0], down, load_sem.at[2]),
    ]
    for load in loads:
        load.start()
    stride = tokens_own // moe_own
    few = (
        lax.broadcasted_iota(jnp.int32, (moe_own, tokens_own), 1)
        == stride * lax.broadcasted_iota(jnp.int32, (moe_own, tokens_own), 0)
    )
    early.wait()
    chosen = jnp.dot(
        few.astype(f32).astype(bf16), q_own[...], preferred_element_type=f32
    ).astype(bf16)
    for p in range(ep_count):
        q_out[p] = chosen[:, p * width : (p + 1) * width]
    for j in range(1, ep_count):
        other = lax.rem(ep + j, ep_count)
        remote(q_out.at[other], q_in.at[ep], one_send.at[2], one_recv.at[2], ep=other).start()
    later(q_in.at[others], 2)
    q_in[ep] = q_out[ep]
    for copy in smalls:
        copy.wait()
    lanes = lax.broadcasted_iota(jnp.int32, (moe_own, 128), 1).astype(f32)
    corner = (
        lax.broadcasted_iota(jnp.int32, (moe_own, moe_own), 0)
        == lax.broadcasted_iota(jnp.int32, (moe_own, moe_own), 1)
    )

    def upright(line):
        spread = jnp.broadcast_to(line, (moe_own, moe_own))
        return jnp.sum(jnp.where(corner, spread, 0.0), axis=1, keepdims=True)

    table_ref[seg, ep] = sum(
        jnp.where(
            upright(experts_ref[i : i + 1, :].astype(f32)) == lanes,
            upright(gates_ref[i : i + 1, :]),
            0.0,
        )
        for i in range(experts_ref.shape[0])
    )
    for j in range(1, ep_count):
        remote(
            table_ref.at[seg, ep], table_ref.at[seg, ep], one_send.at[3], one_recv.at[3],
            ep=lax.rem(ep + j, ep_count),
        ).start()
    later(table_ref.at[0, others], 3)
    length = tokens_own * ep_count
    highest = lax.Precision.HIGHEST
    rows_at = lax.broadcasted_iota(jnp.int32, (length, length), 0)
    columns_at = lax.broadcasted_iota(jnp.int32, (length, length), 1)
    causal = rows_at >= columns_at
    lower = causal.astype(f32)
    turned_decay = turned_ref[...]
    across = lax.dot_general(
        turned_decay, lower, (((1,), (1,)), ((), ())), precision=highest,
        preferred_element_type=f32,
    )
    cum = lax.dot_general(
        lower, turned_decay, (((1,), (1,)), ((), ())), precision=highest,
        preferred_element_type=f32,
    )
    count = ep_count * moe_own
    causal_few = lax.broadcasted_iota(
        jnp.int32, (count, length), 1
    ) <= stride * lax.broadcasted_iota(jnp.int32, (count, length), 0)
    cum_few = lax.dot_general(
        causal_few.astype(f32), turned_decay, (((1,), (1,)), ((), ())), precision=highest,
        preferred_element_type=f32,
    )
    collect(kvb, one_recv.at[0])
    keys, values = (
        jnp.concatenate([kvb[i, p] for p in range(ep_count)], axis=0) for i in range(2)
    )
    ending = cum[length - 1 : length, :]
    unit = (
        lax.broadcasted_iota(jnp.int32, (dim, dim), 0)
        == lax.broadcasted_iota(jnp.int32, (dim, dim), 1)
    ).astype(f32).astype(bf16)
    for h in range(heads):
        cols = slice(h * dim, (h + 1) * dim)
        to_end = jnp.exp(ending[:, h : h + 1] - across[h : h + 1, :])
        turned = lax.dot_general(
            unit, keys[:, cols], (((1,), (1,)), ((), ())), preferred_element_type=f32
        )
        states[seg, h] = jnp.dot(
            (turned * to_end).astype(bf16), values[:, cols],
            preferred_element_type=f32,
        ).astype(bf16)
        ends[seg, h : h + 1] = jnp.broadcast_to(ending[:, h : h + 1], (1, dim))
    for k in range(1, seg_count):
        other = lax.rem(seg + k, seg_count)
        for buf, index in ((states, 4), (ends, 5)):
            remote(
                buf.at[seg], buf.at[seg], one_send.at[index], one_recv.at[index], seg=other
            ).start()
    later(states.at[other_segs], 4)
    later(ends.at[other_segs], 5)

    def within(asked, mask, cum, h):
        cols = slice(h * dim, (h + 1) * dim)
        gap = cum[:, h : h + 1] - across[h : h + 1, :]
        weight = jnp.where(mask, jnp.exp(jnp.where(mask, gap, 0.0)), 0.0)
        scores = lax.dot_general(
            asked[:, cols], keys[:, cols], (((1,), (1,)), ((), ())),
            preferred_element_type=f32,
        )
        return jnp.dot(
            (scores * weight).astype(bf16), values[:, cols], preferred_element_type=f32
        )

    def before(asked, cum, h):
        cols = slice(h * dim, (h + 1) * dim)
        return jnp.exp(cum[:, h : h + 1]) * jnp.dot(
            asked[:, cols], carried[h], preferred_element_type=f32
        )

    collect(q_in.at[others], one_recv.at[2])
    asked = q_in[...].reshape(count, width)
    inside = [within(asked, causal_few, cum_few, h) for h in range(heads)]
    scatter(q_ref, qb, 1)
    later(qb.at[others], 1)
    collect(states.at[other_segs], one_recv.at[4])
    collect(ends.at[other_segs], one_recv.at[5])
    carried = []
    for h in range(heads):
        joined = jnp.zeros((dim, dim), f32)
        for c in range(seg_count):
            after = jnp.exp(ends[c, h : h + 1]) * joined + states[c, h].astype(f32)
            joined = jnp.where(c < seg, after, joined)
        carried.append(joined.astype(bf16))
    for h in range(heads):
        rows[seg, :, h * dim : (h + 1) * dim] = (
            inside[h] + before(asked, cum_few, h)
        ).astype(bf16)

    def mix_all():
        collect(qb, one_recv.at[1])
        queries = jnp.concatenate([qb[p] for p in range(ep_count)], axis=0)
        for h in range(heads):
            value = within(queries, causal, cum, h) + before(queries, cum, h)
            mix_ref[:, :, h * dim : (h + 1) * dim] = value.astype(bf16).reshape(
                ep_count, tokens_own, dim
            )

    own_rows = rows.shape[1]
    total = own_rows * seg_count
    mine = own_rows // ep_count
    cols = proj.shape[1]
    features = width * ep_count
    sources = [(d, i) for d in range(y_count) for i in range(2)]
    row_moves = {}
    for d, i in sources[1:]:
        row_moves[d, i] = remote(
            rows.at[seg], rows.at[seg], one_send.at[6], pick_recv.at[d * 2 + i - 1],
            seg=seg_at(d, i),
        )
        row_moves[d, i].start()
    later(rows.at[other_segs], 6)
    lane = lax.broadcasted_iota(jnp.int32, (own_rows, 128), 1)
    pieces = [(0, 128 + tile)] + [(128 + t, tile) for t in range(tile, cols, tile)]
    x_moves = {}

    def source(n):
        d, i = sources[n]
        return seg_at(-d, i)

    def project(end, n):
        if n:
            row_moves[sources[n]].wait_recv()
        picked = rows[source(n)].astype(f32)
        squares = jnp.sum(picked * picked, axis=1, keepdims=True)
        high = squares.astype(bf16).astype(f32)
        pair = jnp.where(lane < 64, high, squares - high).reshape(half, 2, mine, 128).astype(bf16)
        scaled = (picked * gain_ref[:, own]).astype(bf16)
        for i in range(2):
            part[n, i, :, :, :128] = pair[:, i]
        for p, (at, size) in enumerate(pieces):
            t = p * tile
            value = (
                jnp.dot(scaled, proj[:, t : t + tile], preferred_element_type=f32)
                .reshape(half, 2, mine, tile)
                .astype(bf16)
            )
            for i in range(2):
                part[n, i, :, :, 128 + t : 128 + t + tile] = value[:, i]
            span = pl.ds(at, size)
            x_moves[n, p] = remote(
                part.at[n, 1 - x, :, :, span], x_sum.at[n, :, :, span],
                one_send.at[7], rx_recv.at[n, p], ep=x_mate,
            )
            x_moves[n, p].start()

    short_lane = lane[: half * mine]

    def keep_sum(ref, n, p, value):
        at, size = pieces[p]
        ref[n, :, :, pl.ds(at, size)] = value.astype(bf16)
        if p == 0:
            pair = value[:, :, :128].reshape(half * mine, 128)
            squares = pair[:, :1] + pair[:, 64:65]
            high = squares.astype(bf16).astype(f32)
            pair = jnp.where(short_lane < 64, high, squares - high).astype(bf16)
            ref[n, :, :, :128] = pair.reshape(half, mine, 128)

    def combine(end, n, p):
        span = pl.ds(*pieces[p])
        x_moves[n, p].wait_recv()
        value = part[n, x, :, :, span].astype(f32) + x_sum[n, :, :, span].astype(f32)
        keep_sum(z_part, n, p, value)
        if end:
            remote(
                z_part.at[n, :, :, span], chain_in.at[nearer, n, :, :, span],
                one_send.at[8], chain_recv.at[nearer, n, p], ep=ahead,
            ).start()

    def near(end, n, p):
        if end:
            return
        span = pl.ds(*pieces[p])
        collect(x_sum.at[n, :, :, span], chain_recv.at[nearer, n, p])
        value = z_part[n, :, :, span].astype(f32)
        value = value + chain_in[nearer, n, :, :, span].astype(f32)
        keep_sum(near_out, n, p, value)
        remote(
            near_out.at[n, :, :, span], chain_in.at[nearer, n, :, :, span],
            one_send.at[8], chain_recv.at[nearer, n, p], ep=ahead,
        ).start()

    def far(end, n, p):
        at, size = pieces[p]
        span = pl.ds(at, size)
        collect(x_sum.at[n, :, :, span], chain_recv.at[1 - nearer, n, p])

        def settled(value):
            if p == 0:
                square = value[:, :, :1] + value[:, :, 64:65]
                scale_ref[n] = jnp.broadcast_to(
                    lax.rsqrt(square / features + epsilon), (half, mine, 128)
                )
                value = value[:, :, 128:]
            value = (value * scale_ref[n][:, :, :1]).astype(bf16)
            start = max(at - 128, 0)
            for k in range(half):
                full[seg, source(n), k * 2 + x, :, start : start + tile] = value[k]

        value = z_part[n, :, :, span].astype(f32)
        value = value + chain_in[1 - nearer, n, :, :, span].astype(f32)
        if not end:
            keep_sum(far_out, n, p, value)
            remote(
                far_out.at[n, :, :, span], chain_in.at[1 - nearer, n, :, :, span],
                one_send.at[10], chain_recv.at[1 - nearer, n, p], ep=behind,
            ).start()
            value = value + chain_in[nearer, n, :, :, span].astype(f32)
        settled(value)

    loads[0].wait()
    project(None, 0)
    later(x_sum, 7)
    later(x_sum, 8)
    collect(table_ref.at[0, others], one_recv.at[3])
    for k in range(1, seg_count):
        remote(
            table_ref.at[seg], table_ref.at[seg], one_send.at[9], one_recv.at[9],
            seg=lax.rem(seg + k, seg_count),
        ).start()
    later(table_ref.at[other_segs], 9)
    def send(place, index, recv_sem, **target):
        copy = remote(place, place, one_send.at[index], recv_sem, **target)
        copy.start()
        return copy

    def on_line(e, k):
        return k * 2 + lax.rem(e, 2)

    def y_seg(k):
        return seg_at(k, 0)

    def block(n, d, e):
        at, i = sources[n]
        return full.at[y_seg(-d), seg_at(-d - at, i), e]

    x_copies, y_copies = {}, {}

    def spread(end, n):
        for k in range(half):
            place = block(n, 0, on_line(ep, k))
            x_copies[n, k] = send(place, 11, x_recv.at[n, k], ep=x_mate)
            for d in range(1, y_count):
                y_copies[n, k, d] = send(place, 12, y_recv.at[n, k, d - 1], seg=y_seg(d))
            send(place, 15, c_recv.at[0], seg=mate)

    def relay(end, n, k):
        x_copies[n, k].wait_recv()
        place = block(n, 0, on_line(x_mate, k))
        if k not in by_x:
            for d in range(1, y_count):
                send(place, 13, xy_recv.at[n, 0], seg=y_seg(d))
        send(place, 15, c_recv.at[0], seg=mate)
        for d in range(1, y_count):
            y_copies[n, k, d].wait_recv()
            place = block(n, d, on_line(ep, k))
            if k in by_x:
                send(place, 14, xy_recv.at[n, 1], ep=x_mate)
            send(place, 15, c_recv.at[d], seg=mate)

    by_y = [k for k in range(half) if k not in by_x]

    def blocks(count):
        return full.at[0, 0, pl.ds(0, count)]

    def hand_over(end, n):
        for i, ks in enumerate((by_y, by_x)):
            if ks and y_count > 1:
                collect(blocks(len(ks) * (y_count - 1)), xy_recv.at[n, i])
            for k in ks:
                for d in range(1, y_count):
                    send(block(n, d, on_line(x_mate, k)), 15, c_recv.at[d], seg=mate)

    later(full.at[0, :, pl.ds(0, half)], 11)
    if y_count > 1:
        later(full.at[0, :, pl.ds(0, half * (y_count - 1))], 12)
        for i, ks in enumerate((by_y, by_x)):
            if ks:
                later(full.at[0, :, pl.ds(0, len(ks) * (y_count - 1))], 13 + i)
    later(full.at[pl.ds(0, y_count)], 15)

    def attend(end):
        mix_all()

    def proceed(end, start, beat, near_lag, far_lag, first, relay_beat, relay_step, hand_lag, at):
        plan = [(2.0 * n, project, (n,)) for n in range(1, seg_count)] + [(at, attend, ())]
        for n in range(seg_count):
            for p in range(len(pieces)):
                time = start + beat * (n * len(pieces) + p)
                plan += [
                    (time, combine, (n, p)), (time + near_lag, near, (n, p)),
                    (time + far_lag, far, (n, p)),
                ]
            plan += [(time + far_lag + 0.01, spread, (n,))]
            ready = start + beat * (len(pieces) - 1) + far_lag + first + relay_beat * n
            plan += [(ready + relay_step * k, relay, (n, k)) for k in range(half)]
            if n < seg_count - 1:
                plan += [(ready + hand_lag, hand_over, (n,))]
        for _, stage, given in sorted(plan, key=lambda item: item[0]):
            stage(end, *given)

    for end, hints in zip((True, False), pace):
        pl.when(at_end if end else jnp.logical_not(at_end))(
            functools.partial(proceed, end, *hints)
        )
    loads[1].wait()

    def multiply(s, fresh=False):
        lines = pl.ds(pl.multiple_of(s * cols, cols), cols)
        value = lax.dot_general(
            full[s].reshape(total, cols), up[:, lines], (((1,), (1,)), ((), ())),
            preferred_element_type=f32,
        )
        acc[...] = value if fresh else acc[...] + value

    multiply(seg, True)
    for k in range(y_count):
        waiter(full.at[0], c_recv.at[k], seg=mate).wait_recv()
        multiply(seg_at(-k, 1))
        if k == 0:
            hand_over(None, seg_count - 1)
        if k + 1 < y_count:
            multiply(y_seg(-k - 1))
    tokens[ep] = mix_ref[ep]
    for j in range(1, ep_count):
        other = lax.rem(ep + j, ep_count)
        remote(
            mix_ref.at[other], tokens.at[ep], one_send.at[16], one_recv.at[16], ep=other
        ).start()
    later(tokens.at[others], 16)
    value = acc[...]
    hidden[...] = (value / (1.0 + jnp.exp(-value))).astype(bf16)
    collect(table_ref.at[other_segs], one_recv.at[9])
    table = table_ref[...].reshape(total, 128)
    lane = lax.broadcasted_iota(jnp.int32, (total, 128), 1)
    gate = jnp.sum(jnp.where(lane == z, table, 0.0), axis=1, keepdims=True)
    loads[2].wait()
    steps = seg_count * cols // wide
    core_moves = {}

    def product(c):
        value = jnp.dot(
            hidden[...], down[:, c * wide : (c + 1) * wide], preferred_element_type=f32
        )
        value = jnp.where(gate != 0.0, value * gate, 0.0).astype(bf16)
        terms[c] = value.reshape(y_count, 2, own_rows, wide)
        remote(
            terms.at[c, :, 1 - core], core_in.at[c], one_send.at[17], tc_recv.at[c], seg=mate
        ).start()

    later(core_in, 17)
    def joined(c):
        waiter(core_in.at[c], tc_recv.at[c], seg=mate).wait_recv()
        for k in range(y_count):
            value = (terms[c, k, core].astype(f32) + core_in[c, k].astype(f32)).reshape(
                half, 2, mine, wide
            ).astype(bf16)
            for i in range(2):
                both[c, k, i] = value[:, i]
        if c % 2 == 0:
            for d in range(1, y_count):
                remote(
                    both.at[c, lax.rem(y + d, y_count)], y_in.at[c, d],
                    one_send.at[18], ty_recv.at[c], seg=y_seg(d),
                ).start()
        else:
            remote(
                both.at[c, :, 1 - x], x_in.at[c, pl.ds(0, y_count)], one_send.at[19],
                tx_recv.at[c], ep=x_mate,
            ).start()

    other_ys = pl.ds(1, y_count - 1)
    evens, odds = pl.ds(0, (steps + 1) // 2), pl.ds(0, steps // 2)
    later(y_in.at[evens, other_ys], 18)
    later(x_in.at[odds, pl.ds(0, y_count)], 19)

    def crossed(c):
        if c % 2 == 0:
            collect(y_in.at[c, other_ys], ty_recv.at[c])
            for i in range(2):
                value = both[c, y, i].astype(f32)
                for d in range(1, y_count):
                    value = value + y_in[c, d, i].astype(f32)
                middle[c, i] = value.astype(bf16)
            remote(
                middle.at[c, 1 - x], x_in.at[c, 0], one_send.at[20], tx_recv.at[c], ep=x_mate
            ).start()
        else:
            collect(x_in.at[c, pl.ds(0, y_count)], tx_recv.at[c])
            for k in range(y_count):
                middle[c, k] = (both[c, k, x].astype(f32) + x_in[c, k].astype(f32)).astype(bf16)
            for d in range(1, y_count):
                remote(
                    middle.at[c, lax.rem(y + d, y_count)], y_in.at[c, d, 0],
                    one_send.at[21], ty_recv.at[c], seg=y_seg(d),
                ).start()

    later(x_in.at[evens, 0], 20)
    later(y_in.at[odds, other_ys, 0], 21)

    def along(c):
        if c % 2 == 0:
            collect(x_in.at[c, 0], tx_recv.at[c])
            value = middle[c, x].astype(f32) + x_in[c, 0].astype(f32)
        else:
            collect(y_in.at[c, other_ys, 0], ty_recv.at[c])
            value = middle[c, y].astype(f32)
            for d in range(1, y_count):
                value = value + y_in[c, d, 0].astype(f32)
        line[c] = value.astype(bf16)
        for k in range(1, half):
            other = lax.rem(z + k, half)
            remote(
                line.at[c, other], line_in.at[c, k], one_send.at[22], tz_recv.at[c],
                ep=other * 2 + x,
            ).start()

    later(line_in.at[:, pl.ds(1, half - 1)], 22)

    def settle():
        collect(tokens.at[others], one_recv.at[16])
        mixed = [tokens[p].astype(f32) for p in range(ep_count)]
        square = sum(jnp.sum(m * m, axis=1, keepdims=True) for m in mixed)
        inv_rms = lax.rsqrt(square / features + epsilon)
        for p in range(ep_count):
            at = slice(p * width, (p + 1) * width)
            attn_ref[:, at] = (mixed[p] * inv_rms * gain_ref[:, at]).astype(bf16)
        result.start()

    result = pltpu.make_async_copy(attn_ref, attn_hbm, load_sem.at[8])
    for c in range(steps + lags[2]):
        if c < steps:
            product(c)
        if 0 <= c - lags[0] < steps:
            joined(c - lags[0])
        if 0 <= c - lags[1] < steps:
            crossed(c - lags[1])
        if 0 <= c - lags[2] < steps:
            along(c - lags[2])
    settle()
    for c in range(steps):
        value = line[c, z].astype(f32)
        collect(line_in.at[c, pl.ds(1, half - 1)], tz_recv.at[c])
        for k in range(1, half):
            value = value + line_in[c, k].astype(f32)
        out_ref[:, c * wide : (c + 1) * wide] = value.astype(bf16)
    whole = pltpu.make_async_copy(out_ref, out_hbm, load_sem.at[9])
    whole.start()
    for copy in pending:
        copy.wait_send()

    @pl.when(jnp.logical_not(at_end))
    def _():
        remote(x_sum, x_sum, one_send.at[10], one_recv.at[0], ep=x_mate).wait_send()

    result.wait()
    whole.wait()


def carry_kernel(a_in, b_in, a_out, b_out, a_held, b_held, sem):
    inward = [
        pltpu.make_async_copy(src, held, sem.at[0, i])
        for i, (src, held) in enumerate(((a_in, a_held), (b_in, b_held)))
    ]
    outward = [
        pltpu.make_async_copy(held, dst, sem.at[1, i])
        for i, (held, dst) in enumerate(((a_held, a_out), (b_held, b_out)))
    ]
    for copy in inward:
        copy.start()
    for copy, after in zip(inward, outward):
        copy.wait()
        after.start()
    for copy in outward:
        copy.wait()


def on_device_dense(
    queries, keys, values, log_decay, out_gain, out_proj, experts, gates, up_weight, down_weight
):
    f32, bf16 = jnp.float32, jnp.bfloat16
    dma = pltpu.SemaphoreType.DMA
    seg_count, ep_count = lax.axis_size("seg"), lax.axis_size("ep")
    y_count, half = seg_count // 2, ep_count // 2
    tokens_own, features = queries.shape
    heads = log_decay.shape[1]
    width = features // ep_count
    dim = width // heads
    moe_own = experts.shape[0]
    seg_rows = moe_own * ep_count
    total = seg_rows * seg_count
    cols = out_proj.shape[1]
    model, units = up_weight.shape[1:]
    tile = math.gcd(cols, 512)
    wide = tile
    steps = model // wide
    hbm = pl.BlockSpec(memory_space=pl.ANY)
    results = pl.pallas_call(
        functools.partial(step_kernel, seg_count, ep_count, heads, dim, tile, wide, (2, 8, 13), BYX, PACE),
        out_shape=(
            jax.ShapeDtypeStruct((tokens_own, features), bf16),
            jax.ShapeDtypeStruct((moe_own, model), bf16),
        ),
        in_specs=[hbm] * 10,
        out_specs=(hbm, hbm),
        scratch_shapes=[
            VM((heads, log_decay.shape[0]), f32),
            VM((experts.shape[1], moe_own), jnp.int32),
            VM((experts.shape[1], moe_own), f32),
            VM((1, features), f32),
            VM((tokens_own, features), bf16),
            VM((moe_own, model), bf16),
            VM((2, ep_count, tokens_own, width), bf16),
            VM((ep_count, tokens_own, width), bf16),
            VM((tokens_own, features), bf16),
            VM((ep_count, moe_own, width), bf16),
            VM((ep_count, moe_own, width), bf16),
            VM((seg_count, heads, dim, dim), bf16),
            VM((seg_count, 8, dim), f32),
            VM((seg_count, ep_count, moe_own, 128), f32),
            VM((ep_count, tokens_own, width), bf16),
            VM((units, model), bf16),
            VM((units, model), bf16),
            VM((width, cols), bf16),
            VM((seg_count, seg_rows, width), bf16),
            VM((seg_count, 2, half, moe_own, cols + 128), bf16),
            VM((seg_count, half, moe_own, cols + 128), bf16),
            VM((seg_count, half, moe_own, cols + 128), bf16),
            VM((2, seg_count, half, moe_own, cols + 128), bf16),
            VM((seg_count, half, moe_own, cols + 128), bf16),
            VM((seg_count, half, moe_own, cols + 128), bf16),
            VM((seg_count, half, moe_own, 128), f32),
            VM((seg_count, seg_count, ep_count, moe_own, cols), bf16),
            VM((total, units), f32),
            VM((total, units), bf16),
            VM((ep_count, tokens_own, width), bf16),
            VM((steps, y_count, 2, seg_rows, wide), bf16),
            VM((steps, y_count, seg_rows, wide), bf16),
            VM((steps, y_count, 2, half, moe_own, wide), bf16),
            VM((steps, y_count, 2, half, moe_own, wide), bf16),
            VM((steps, max(2, y_count), half, moe_own, wide), bf16),
            VM((steps, max(2, y_count), half, moe_own, wide), bf16),
            VM((steps, half, moe_own, wide), bf16),
            VM((steps, half, moe_own, wide), bf16),
            dma((10,)),
            dma((23,)),
            dma((17,)),
            dma((seg_count - 1,)),
            dma((seg_count, cols // tile)),
            dma((2, seg_count, cols // tile)),
            dma((seg_count, half)),
            dma((seg_count, half, max(1, y_count - 1))),
            dma((seg_count, 2)),
            dma((y_count,)),
        ]
        + [dma((steps,))] * 4,
        compiler_params=pltpu.CompilerParams(
            collective_id=1, has_side_effects=True, vmem_limit_bytes=62 * 2**20
        ),
    )(
        queries, keys, values, out_proj, jnp.swapaxes(up_weight, 1, 2), down_weight,
        log_decay.T, experts.T, gates.T, out_gain[None, :],
    )
    return pl.pallas_call(
        carry_kernel,
        out_shape=tuple(jax.ShapeDtypeStruct(r.shape, r.dtype) for r in results),
        in_specs=[hbm] * 2,
        out_specs=(hbm, hbm),
        scratch_shapes=[VM(r.shape, r.dtype) for r in results] + [dma((2, 2))],
    )(*results)


def on_device(*args):
    experts, ep_count = args[6], lax.axis_size("ep")
    full_rows = max(2, 4 * experts.shape[0] // (ep_count // 2)) >= experts.shape[0]
    return (on_device_dense if full_rows else on_device_routed)(*args)


def solution(mesh):
    placed = (
        P(("seg", "ep"), None),
        P(("seg", "ep"), None),
        P(("seg", "ep"), None),
        P("seg", "ep"),
        P(),
        P("ep", "seg"),
        P(("seg", "ep"), None),
        P(("seg", "ep"), None),
        P("ep", None, "seg"),
        P("ep", "seg", None),
    )
    return jax.shard_map(
        on_device,
        mesh=mesh,
        in_specs=placed,
        out_specs=(P(("seg", "ep"), None), P(("seg", "ep"), None)),
        check_vma=False,
    )
```

```python
import functools
import math

import jax
import jax.numpy as jnp
from jax import lax
from jax.experimental import pallas as pl
from jax.experimental.pallas import tpu as pltpu
from jax.sharding import PartitionSpec as P

epsilon = 1e-06
BYX = (1, 3)
PACE = ((2.8, 0.71, 3.2, 9.7, 2.5, 3.2, 0.5, 6.0, 11.5), (2.8, 0.71, 3.2, 6.4, 2.5, 3.2, 0.5, 6.0, 13.0))
MESH = pl.DeviceIdType.MESH
VM = pltpu.VMEM


def prefix(x, axis, join, neutral):
    place = lax.axis_index(axis)
    gathered = jax.tree.map(
        lambda a, kind: lax.all_gather(a.astype(kind), axis), x, (jnp.bfloat16, jnp.bfloat16)
    )
    state = jax.tree.map(lambda a, e: jnp.zeros_like(a) + jnp.asarray(e, a.dtype), x, neutral)

    def one(turn, state):
        return join(
            state,
            jax.tree.map(
                lambda a, own: lax.dynamic_index_in_dim(a, turn, 0, False).astype(own.dtype),
                gathered,
                x,
            ),
        )

    return lax.fori_loop(0, place, one, state)


def chain_combine(first_part, second_part):
    return (
        first_part[0] * second_part[0],
        second_part[0][:, None, None] * first_part[1] + second_part[1],
    )


def route_tables(experts, gates, expert_count, capacity):
    token_count = experts.shape[0]
    flattened = experts.reshape(-1)
    onehot = (flattened[:, None] == jnp.arange(expert_count, dtype=jnp.int32)[None, :]).astype(
        jnp.int32
    )
    earlier = jnp.cumsum(onehot, axis=0) - onehot
    position = jnp.sum(earlier * onehot, axis=1)
    slot_index = (flattened * capacity + position).reshape(token_count, 2)
    columns = jnp.arange(expert_count * capacity, dtype=jnp.int32)
    matches = slot_index[:, :, None] == columns[None, None, :]
    dispatch = jnp.any(matches, axis=1).T.astype(jnp.bfloat16)
    combine = jnp.sum(jnp.where(matches, gates[:, :, None], 0.0), axis=1)
    return (dispatch, combine)


def expert_output(row_data, up_piece, down_piece):
    hidden = jax.nn.silu(jnp.dot(row_data, up_piece, preferred_element_type=jnp.float32)).astype(
        jnp.bfloat16
    )
    return jnp.dot(hidden, down_piece, preferred_element_type=jnp.float32)


def on_device_routed(
    queries, keys, values, log_decay, out_gain, out_proj, experts, gates, up_weight, down_weight
):
    highest = lax.Precision.HIGHEST
    ep_count = lax.axis_size("ep")
    heads_local = log_decay.shape[1]
    head_dim = queries.shape[1] // (heads_local * ep_count)
    query_heads, key_heads, value_heads = (
        lax.all_to_all(queries, "ep", split_axis=1, concat_axis=0, tiled=True),
        lax.all_to_all(keys, "ep", split_axis=1, concat_axis=0, tiled=True),
        lax.all_to_all(values, "ep", split_axis=1, concat_axis=0, tiled=True),
    )
    seg_length = query_heads.shape[0]
    query_heads = query_heads.reshape(seg_length, heads_local, head_dim)
    key_heads = key_heads.reshape(seg_length, heads_local, head_dim)
    value_heads = value_heads.reshape(seg_length, heads_local, head_dim)
    cumulative = jnp.cumsum(log_decay, axis=0)
    across = cumulative.T
    block_size = math.gcd(seg_length, 512)
    starts = jnp.arange(seg_length // block_size, dtype=jnp.int32) * block_size
    token_positions = jnp.arange(seg_length, dtype=jnp.int32)

    def block_mix(start):
        query_block = lax.dynamic_slice_in_dim(query_heads, start, block_size, 0)
        cum_block = lax.dynamic_slice_in_dim(across, start, block_size, 1)
        row_ids = start + jnp.arange(block_size, dtype=jnp.int32)
        causal = (row_ids[:, None] >= token_positions[None, :])[None]
        log_gap = cum_block[:, :, None] - across[:, None, :]
        weight = jnp.where(causal, jnp.exp(jnp.where(causal, log_gap, 0.0)), 0.0)
        scores = jnp.einsum(
            "thd,shd->hts", query_block, key_heads, preferred_element_type=jnp.float32
        )
        mixing = (scores * weight).astype(jnp.bfloat16)
        return jnp.einsum("hts,she->the", mixing, value_heads, preferred_element_type=jnp.float32)

    inside = lax.map(block_mix, starts).reshape(seg_length, heads_local, head_dim)
    ending = cumulative[-1]
    to_end = jnp.exp(ending[None, :] - cumulative)
    key_float = key_heads.astype(jnp.float32)
    value_float = value_heads.astype(jnp.float32)
    local_state = jnp.einsum("sh,shd,she->hde", to_end, key_float, value_float, precision=highest)
    identity = (jnp.ones_like(ending), jnp.zeros_like(local_state))
    carried = prefix((jnp.exp(ending), local_state), "seg", chain_combine, identity)[1]
    outside = jnp.exp(cumulative)[:, :, None] * jnp.einsum(
        "thd,hde->the", query_heads.astype(jnp.float32), carried, precision=highest
    )
    mixture = (inside + outside).astype(jnp.bfloat16).reshape(seg_length, heads_local * head_dim)
    token_mix = lax.all_to_all(mixture, "ep", split_axis=0, concat_axis=1, tiled=True)
    as_float = token_mix.astype(jnp.float32)
    inv_rms = lax.rsqrt(jnp.mean(as_float * as_float, axis=1, keepdims=True) + epsilon)
    attn_out = (as_float * inv_rms * out_gain[None, :]).astype(jnp.bfloat16)
    row_stride = 8
    own_width = heads_local * head_dim
    feature_count = own_width * ep_count
    picked_float = mixture.reshape(seg_length // row_stride, row_stride, own_width)[:, 0].astype(
        jnp.float32
    )
    square_sums = lax.psum(jnp.sum(picked_float * picked_float, axis=1), "ep")
    picked_rms = lax.rsqrt(square_sums[:, None] / feature_count + epsilon)
    gain_slice = lax.dynamic_slice_in_dim(out_gain, lax.axis_index("ep") * own_width, own_width, 0)
    normed_rows = (picked_float * picked_rms * gain_slice[None, :]).astype(jnp.bfloat16)
    proj_terms = jnp.dot(
        normed_rows,
        lax.all_gather(out_proj, "seg", axis=1, tiled=True),
        preferred_element_type=jnp.float32,
    )
    moe_in = lax.psum_scatter(
        proj_terms.astype(jnp.bfloat16), "ep", scatter_dimension=0, tiled=True
    )
    expert_count = ep_count // 2
    token_count, model_width = moe_in.shape
    capacity = max(2, 4 * token_count // expert_count)
    dispatch, combine = route_tables(experts, gates, expert_count, capacity)
    up_piece = up_weight[0]
    down_piece = down_weight[0]
    slot_rows = jnp.dot(dispatch, moe_in, preferred_element_type=jnp.float32).astype(jnp.bfloat16)
    outgoing = jnp.repeat(slot_rows.reshape(expert_count, capacity, model_width), 2, axis=0)
    arrived = lax.all_to_all(outgoing, "ep", split_axis=0, concat_axis=0, tiled=True).reshape(
        ep_count * capacity, model_width
    )
    gathered = lax.all_gather(arrived, "seg", axis=0, tiled=True)
    owned_sums = lax.psum_scatter(
        expert_output(gathered, up_piece, down_piece).astype(jnp.bfloat16),
        "seg",
        scatter_dimension=0,
        tiled=True,
    ).astype(jnp.float32)
    returned_back = lax.all_to_all(
        owned_sums.reshape(ep_count, capacity, model_width).astype(jnp.bfloat16),
        "ep",
        split_axis=0,
        concat_axis=0,
        tiled=True,
    ).astype(jnp.float32)
    paired = returned_back.reshape(expert_count, 2, capacity, model_width)
    halves = (paired[:, 0] + paired[:, 1]).reshape(expert_count * capacity, model_width)
    summed = jnp.dot(combine, halves, precision=highest)
    moe_out = summed.astype(jnp.bfloat16)
    return (attn_out, moe_out)


def remote(src, dst, send, recv, **target):
    return pltpu.make_async_remote_copy(
        src_ref=src, dst_ref=dst, send_sem=send, recv_sem=recv,
        device_id=target, device_id_type=MESH,
    )


def greet(seg_count, ep_count):
    seg, ep = lax.axis_index("seg"), lax.axis_index("ep")
    barrier = pltpu.get_barrier_semaphore()
    for j in range(1, ep_count):
        pl.semaphore_signal(
            barrier, inc=1, device_id={"ep": lax.rem(ep + j, ep_count)}, device_id_type=MESH
        )
    for k in range(1, seg_count):
        pl.semaphore_signal(
            barrier, inc=1, device_id={"seg": lax.rem(seg + k, seg_count)}, device_id_type=MESH
        )
    pl.semaphore_wait(barrier, ep_count + seg_count - 2)
    return seg, ep


def step_kernel(
    seg_count, ep_count, heads, dim, tile, wide, lags, by_x, pace,
    q_ref, k_ref, v_ref, proj_hbm, up_hbm, down_hbm,
    turned_hbm, experts_hbm, gates_hbm, gain_hbm,
    attn_hbm, out_hbm,
    turned_ref, experts_ref, gates_ref, gain_ref, attn_ref, out_ref,
    kvb, qb, q_own, q_out, q_in, states, ends, table_ref, mix_ref,
    up, down, proj, rows, part, x_sum, z_part, chain_in, near_out, far_out, scale_ref, full, acc, hidden, tokens,
    terms, core_in, both, y_in, x_in, middle, line, line_in,
    load_sem, one_send, one_recv, pick_recv, rx_recv, chain_recv,
    x_recv, y_recv, xy_recv, c_recv, tc_recv, ty_recv, tx_recv, tz_recv,
):
    f32, bf16 = jnp.float32, jnp.bfloat16
    smalls = [
        pltpu.make_async_copy(src, dst, load_sem.at[4 + i])
        for i, (src, dst) in enumerate(
            (
                (turned_hbm, turned_ref), (experts_hbm, experts_ref), (gates_hbm, gates_ref),
                (gain_hbm, gain_ref),
            )
        )
    ]
    early = pltpu.make_async_copy(q_ref, q_own, load_sem.at[3])
    early.start()
    for copy in smalls:
        copy.start()
    seg, ep = greet(seg_count, ep_count)
    width = heads * dim
    tokens_own, moe_own = q_ref.shape[0], experts_ref.shape[1]
    y_count, half = seg_count // 2, ep_count // 2
    core, y = lax.rem(seg, 2), lax.div(seg, 2)
    x, z = lax.rem(ep, 2), lax.div(ep, 2)
    x_mate = ep + 1 - 2 * x
    mate = seg + 1 - 2 * core

    nearer = jnp.where(z * 2 < half, 0, 1)
    at_end = (z == 0) | (z == half - 1)
    ahead = (z + 1 - 2 * nearer) * 2 + x
    behind = (z - 1 + 2 * nearer) * 2 + x

    def seg_at(d, i):
        return lax.rem(y + d + 2 * y_count, y_count) * 2 + (core if i == 0 else 1 - core)

    own = pl.ds(pl.multiple_of(ep * width, width), width)
    pending = []

    def waiter(ref, recv, **target):
        return remote(ref, ref, one_send.at[0], recv, **target)

    def collect(ref, recv):
        waiter(ref, recv, ep=x_mate).wait_recv()

    def later(ref, index):
        pending.append(remote(ref, ref, one_send.at[index], one_recv.at[0], ep=x_mate))

    def scatter(ref, buf, index):
        for j in sorted(range(1, ep_count), key=lambda j: abs(2 * j - ep_count)):
            other = lax.rem(ep + j, ep_count)
            columns = pl.ds(pl.multiple_of(other * width, width), width)
            remote(
                ref.at[:, columns], buf.at[ep], one_send.at[index], one_recv.at[index], ep=other
            ).start()
        pltpu.make_async_copy(ref.at[:, own], buf.at[ep], one_recv.at[index]).start()

    others = pl.ds(1, ep_count - 1)
    other_segs = pl.ds(1, seg_count - 1)
    scatter(k_ref, kvb.at[0], 0)
    scatter(v_ref, kvb.at[1], 0)
    later(kvb.at[:, others], 0)
    loads = [
        pltpu.make_async_copy(proj_hbm, proj, load_sem.at[0]),
        pltpu.make_async_copy(up_hbm.at[0], up, load_sem.at[1]),
        pltpu.make_async_copy(down_hbm.at[0], down, load_sem.at[2]),
    ]
    for load in loads:
        load.start()
    stride = tokens_own // moe_own
    few = (
        lax.broadcasted_iota(jnp.int32, (moe_own, tokens_own), 1)
        == stride * lax.broadcasted_iota(jnp.int32, (moe_own, tokens_own), 0)
    )
    early.wait()
    chosen = jnp.dot(
        few.astype(f32).astype(bf16), q_own[...], preferred_element_type=f32
    ).astype(bf16)
    for p in range(ep_count):
        q_out[p] = chosen[:, p * width : (p + 1) * width]
    for j in range(1, ep_count):
        other = lax.rem(ep + j, ep_count)
        remote(q_out.at[other], q_in.at[ep], one_send.at[2], one_recv.at[2], ep=other).start()
    later(q_in.at[others], 2)
    q_in[ep] = q_out[ep]
    for copy in smalls:
        copy.wait()
    lanes = lax.broadcasted_iota(jnp.int32, (moe_own, 128), 1).astype(f32)
    corner = (
        lax.broadcasted_iota(jnp.int32, (moe_own, moe_own), 0)
        == lax.broadcasted_iota(jnp.int32, (moe_own, moe_own), 1)
    )

    def upright(line):
        spread = jnp.broadcast_to(line, (moe_own, moe_own))
        return jnp.sum(jnp.where(corner, spread, 0.0), axis=1, keepdims=True)

    table_ref[seg, ep] = sum(
        jnp.where(
            upright(experts_ref[i : i + 1, :].astype(f32)) == lanes,
            upright(gates_ref[i : i + 1, :]),
            0.0,
        )
        for i in range(experts_ref.shape[0])
    )
    for j in range(1, ep_count):
        remote(
            table_ref.at[seg, ep], table_ref.at[seg, ep], one_send.at[3], one_recv.at[3],
            ep=lax.rem(ep + j, ep_count),
        ).start()
    later(table_ref.at[0, others], 3)
    length = tokens_own * ep_count
    highest = lax.Precision.HIGHEST
    rows_at = lax.broadcasted_iota(jnp.int32, (length, length), 0)
    columns_at = lax.broadcasted_iota(jnp.int32, (length, length), 1)
    causal = rows_at >= columns_at
    lower = causal.astype(f32)
    turned_decay = turned_ref[...]
    across = lax.dot_general(
        turned_decay, lower, (((1,), (1,)), ((), ())), precision=highest,
        preferred_element_type=f32,
    )
    cum = lax.dot_general(
        lower, turned_decay, (((1,), (1,)), ((), ())), precision=highest,
        preferred_element_type=f32,
    )
    count = ep_count * moe_own
    causal_few = lax.broadcasted_iota(
        jnp.int32, (count, length), 1
    ) <= stride * lax.broadcasted_iota(jnp.int32, (count, length), 0)
    cum_few = lax.dot_general(
        causal_few.astype(f32), turned_decay, (((1,), (1,)), ((), ())), precision=highest,
        preferred_element_type=f32,
    )
    collect(kvb, one_recv.at[0])
    keys, values = (
        jnp.concatenate([kvb[i, p] for p in range(ep_count)], axis=0) for i in range(2)
    )
    ending = cum[length - 1 : length, :]
    unit = (
        lax.broadcasted_iota(jnp.int32, (dim, dim), 0)
        == lax.broadcasted_iota(jnp.int32, (dim, dim), 1)
    ).astype(f32).astype(bf16)
    for h in range(heads):
        cols = slice(h * dim, (h + 1) * dim)
        to_end = jnp.exp(ending[:, h : h + 1] - across[h : h + 1, :])
        turned = lax.dot_general(
            unit, keys[:, cols], (((1,), (1,)), ((), ())), preferred_element_type=f32
        )
        states[seg, h] = jnp.dot(
            (turned * to_end).astype(bf16), values[:, cols],
            preferred_element_type=f32,
        ).astype(bf16)
        ends[seg, h : h + 1] = jnp.broadcast_to(ending[:, h : h + 1], (1, dim))
    for k in range(1, seg_count):
        other = lax.rem(seg + k, seg_count)
        for buf, index in ((states, 4), (ends, 5)):
            remote(
                buf.at[seg], buf.at[seg], one_send.at[index], one_recv.at[index], seg=other
            ).start()
    later(states.at[other_segs], 4)
    later(ends.at[other_segs], 5)

    def within(asked, mask, cum, h):
        cols = slice(h * dim, (h + 1) * dim)
        gap = cum[:, h : h + 1] - across[h : h + 1, :]
        weight = jnp.where(mask, jnp.exp(jnp.where(mask, gap, 0.0)), 0.0)
        scores = lax.dot_general(
            asked[:, cols], keys[:, cols], (((1,), (1,)), ((), ())),
            preferred_element_type=f32,
        )
        return jnp.dot(
            (scores * weight).astype(bf16), values[:, cols], preferred_element_type=f32
        )

    def before(asked, cum, h):
        cols = slice(h * dim, (h + 1) * dim)
        return jnp.exp(cum[:, h : h + 1]) * jnp.dot(
            asked[:, cols], carried[h], preferred_element_type=f32
        )

    collect(q_in.at[others], one_recv.at[2])
    asked = q_in[...].reshape(count, width)
    inside = [within(asked, causal_few, cum_few, h) for h in range(heads)]
    scatter(q_ref, qb, 1)
    later(qb.at[others], 1)
    collect(states.at[other_segs], one_recv.at[4])
    collect(ends.at[other_segs], one_recv.at[5])
    carried = []
    for h in range(heads):
        joined = jnp.zeros((dim, dim), f32)
        for c in range(seg_count):
            after = jnp.exp(ends[c, h : h + 1]) * joined + states[c, h].astype(f32)
            joined = jnp.where(c < seg, after, joined)
        carried.append(joined.astype(bf16))
    for h in range(heads):
        rows[seg, :, h * dim : (h + 1) * dim] = (
            inside[h] + before(asked, cum_few, h)
        ).astype(bf16)

    def mix_all():
        collect(qb, one_recv.at[1])
        queries = jnp.concatenate([qb[p] for p in range(ep_count)], axis=0)
        for h in range(heads):
            value = within(queries, causal, cum, h) + before(queries, cum, h)
            mix_ref[:, :, h * dim : (h + 1) * dim] = value.astype(bf16).reshape(
                ep_count, tokens_own, dim
            )

    own_rows = rows.shape[1]
    total = own_rows * seg_count
    mine = own_rows // ep_count
    cols = proj.shape[1]
    features = width * ep_count
    sources = [(d, i) for d in range(y_count) for i in range(2)]
    row_moves = {}
    for d, i in sources[1:]:
        row_moves[d, i] = remote(
            rows.at[seg], rows.at[seg], one_send.at[6], pick_recv.at[d * 2 + i - 1],
            seg=seg_at(d, i),
        )
        row_moves[d, i].start()
    later(rows.at[other_segs], 6)
    lane = lax.broadcasted_iota(jnp.int32, (own_rows, 128), 1)
    pieces = [(0, 128 + tile)] + [(128 + t, tile) for t in range(tile, cols, tile)]
    x_moves = {}

    def source(n):
        d, i = sources[n]
        return seg_at(-d, i)

    def project(end, n):
        if n:
            row_moves[sources[n]].wait_recv()
        picked = rows[source(n)].astype(f32)
        squares = jnp.sum(picked * picked, axis=1, keepdims=True)
        high = squares.astype(bf16).astype(f32)
        pair = jnp.where(lane < 64, high, squares - high).reshape(half, 2, mine, 128).astype(bf16)
        scaled = (picked * gain_ref[:, own]).astype(bf16)
        for i in range(2):
            part[n, i, :, :, :128] = pair[:, i]
        for p, (at, size) in enumerate(pieces):
            t = p * tile
            value = (
                jnp.dot(scaled, proj[:, t : t + tile], preferred_element_type=f32)
                .reshape(half, 2, mine, tile)
                .astype(bf16)
            )
            for i in range(2):
                part[n, i, :, :, 128 + t : 128 + t + tile] = value[:, i]
            span = pl.ds(at, size)
            x_moves[n, p] = remote(
                part.at[n, 1 - x, :, :, span], x_sum.at[n, :, :, span],
                one_send.at[7], rx_recv.at[n, p], ep=x_mate,
            )
            x_moves[n, p].start()

    short_lane = lane[: half * mine]

    def keep_sum(ref, n, p, value):
        at, size = pieces[p]
        ref[n, :, :, pl.ds(at, size)] = value.astype(bf16)
        if p == 0:
            pair = value[:, :, :128].reshape(half * mine, 128)
            squares = pair[:, :1] + pair[:, 64:65]
            high = squares.astype(bf16).astype(f32)
            pair = jnp.where(short_lane < 64, high, squares - high).astype(bf16)
            ref[n, :, :, :128] = pair.reshape(half, mine, 128)

    def combine(end, n, p):
        span = pl.ds(*pieces[p])
        x_moves[n, p].wait_recv()
        value = part[n, x, :, :, span].astype(f32) + x_sum[n, :, :, span].astype(f32)
        keep_sum(z_part, n, p, value)
        if end:
            remote(
                z_part.at[n, :, :, span], chain_in.at[nearer, n, :, :, span],
                one_send.at[8], chain_recv.at[nearer, n, p], ep=ahead,
            ).start()

    def near(end, n, p):
        if end:
            return
        span = pl.ds(*pieces[p])
        collect(x_sum.at[n, :, :, span], chain_recv.at[nearer, n, p])
        value = z_part[n, :, :, span].astype(f32)
        value = value + chain_in[nearer, n, :, :, span].astype(f32)
        keep_sum(near_out, n, p, value)
        remote(
            near_out.at[n, :, :, span], chain_in.at[nearer, n, :, :, span],
            one_send.at[8], chain_recv.at[nearer, n, p], ep=ahead,
        ).start()

    def far(end, n, p):
        at, size = pieces[p]
        span = pl.ds(at, size)
        collect(x_sum.at[n, :, :, span], chain_recv.at[1 - nearer, n, p])

        def settled(value):
            if p == 0:
                square = value[:, :, :1] + value[:, :, 64:65]
                scale_ref[n] = jnp.broadcast_to(
                    lax.rsqrt(square / features + epsilon), (half, mine, 128)
                )
                value = value[:, :, 128:]
            value = (value * scale_ref[n][:, :, :1]).astype(bf16)
            start = max(at - 128, 0)
            for k in range(half):
                full[seg, source(n), k * 2 + x, :, start : start + tile] = value[k]

        value = z_part[n, :, :, span].astype(f32)
        value = value + chain_in[1 - nearer, n, :, :, span].astype(f32)
        if not end:
            keep_sum(far_out, n, p, value)
            remote(
                far_out.at[n, :, :, span], chain_in.at[1 - nearer, n, :, :, span],
                one_send.at[10], chain_recv.at[1 - nearer, n, p], ep=behind,
            ).start()
            value = value + chain_in[nearer, n, :, :, span].astype(f32)
        settled(value)

    loads[0].wait()
    project(None, 0)
    later(x_sum, 7)
    later(x_sum, 8)
    collect(table_ref.at[0, others], one_recv.at[3])
    for k in range(1, seg_count):
        remote(
            table_ref.at[seg], table_ref.at[seg], one_send.at[9], one_recv.at[9],
            seg=lax.rem(seg + k, seg_count),
        ).start()
    later(table_ref.at[other_segs], 9)
    def send(place, index, recv_sem, **target):
        copy = remote(place, place, one_send.at[index], recv_sem, **target)
        copy.start()
        return copy

    def on_line(e, k):
        return k * 2 + lax.rem(e, 2)

    def y_seg(k):
        return seg_at(k, 0)

    def block(n, d, e):
        at, i = sources[n]
        return full.at[y_seg(-d), seg_at(-d - at, i), e]

    x_copies, y_copies = {}, {}

    def spread(end, n):
        for k in range(half):
            place = block(n, 0, on_line(ep, k))
            x_copies[n, k] = send(place, 11, x_recv.at[n, k], ep=x_mate)
            for d in range(1, y_count):
                y_copies[n, k, d] = send(place, 12, y_recv.at[n, k, d - 1], seg=y_seg(d))
            send(place, 15, c_recv.at[0], seg=mate)

    def relay(end, n, k):
        x_copies[n, k].wait_recv()
        place = block(n, 0, on_line(x_mate, k))
        if k not in by_x:
            for d in range(1, y_count):
                send(place, 13, xy_recv.at[n, 0], seg=y_seg(d))
        send(place, 15, c_recv.at[0], seg=mate)
        for d in range(1, y_count):
            y_copies[n, k, d].wait_recv()
            place = block(n, d, on_line(ep, k))
            if k in by_x:
                send(place, 14, xy_recv.at[n, 1], ep=x_mate)
            send(place, 15, c_recv.at[d], seg=mate)

    by_y = [k for k in range(half) if k not in by_x]

    def blocks(count):
        return full.at[0, 0, pl.ds(0, count)]

    def hand_over(end, n):
        for i, ks in enumerate((by_y, by_x)):
            if ks and y_count > 1:
                collect(blocks(len(ks) * (y_count - 1)), xy_recv.at[n, i])
            for k in ks:
                for d in range(1, y_count):
                    send(block(n, d, on_line(x_mate, k)), 15, c_recv.at[d], seg=mate)

    later(full.at[0, :, pl.ds(0, half)], 11)
    if y_count > 1:
        later(full.at[0, :, pl.ds(0, half * (y_count - 1))], 12)
        for i, ks in enumerate((by_y, by_x)):
            if ks:
                later(full.at[0, :, pl.ds(0, len(ks) * (y_count - 1))], 13 + i)
    later(full.at[pl.ds(0, y_count)], 15)

    def attend(end):
        mix_all()

    def proceed(end, start, beat, near_lag, far_lag, first, relay_beat, relay_step, hand_lag, at):
        plan = [(2.0 * n, project, (n,)) for n in range(1, seg_count)] + [(at, attend, ())]
        for n in range(seg_count):
            for p in range(len(pieces)):
                time = start + beat * (n * len(pieces) + p)
                plan += [
                    (time, combine, (n, p)), (time + near_lag, near, (n, p)),
                    (time + far_lag, far, (n, p)),
                ]
            plan += [(time + far_lag + 0.01, spread, (n,))]
            ready = start + beat * (len(pieces) - 1) + far_lag + first + relay_beat * n
            plan += [(ready + relay_step * k, relay, (n, k)) for k in range(half)]
            if n < seg_count - 1:
                plan += [(ready + hand_lag, hand_over, (n,))]
        for _, stage, given in sorted(plan, key=lambda item: item[0]):
            stage(end, *given)

    for end, hints in zip((True, False), pace):
        pl.when(at_end if end else jnp.logical_not(at_end))(
            functools.partial(proceed, end, *hints)
        )
    loads[1].wait()

    def multiply(s, fresh=False):
        lines = pl.ds(pl.multiple_of(s * cols, cols), cols)
        value = lax.dot_general(
            full[s].reshape(total, cols), up[:, lines], (((1,), (1,)), ((), ())),
            preferred_element_type=f32,
        )
        acc[...] = value if fresh else acc[...] + value

    multiply(seg, True)
    for k in range(y_count):
        waiter(full.at[0], c_recv.at[k], seg=mate).wait_recv()
        multiply(seg_at(-k, 1))
        if k == 0:
            hand_over(None, seg_count - 1)
        if k + 1 < y_count:
            multiply(y_seg(-k - 1))
    tokens[ep] = mix_ref[ep]
    for j in range(1, ep_count):
        other = lax.rem(ep + j, ep_count)
        remote(
            mix_ref.at[other], tokens.at[ep], one_send.at[16], one_recv.at[16], ep=other
        ).start()
    later(tokens.at[others], 16)
    value = acc[...]
    hidden[...] = (value / (1.0 + jnp.exp(-value))).astype(bf16)
    collect(table_ref.at[other_segs], one_recv.at[9])
    table = table_ref[...].reshape(total, 128)
    lane = lax.broadcasted_iota(jnp.int32, (total, 128), 1)
    gate = jnp.sum(jnp.where(lane == z, table, 0.0), axis=1, keepdims=True)
    loads[2].wait()
    steps = seg_count * cols // wide
    core_moves = {}

    def product(c):
        value = jnp.dot(
            hidden[...], down[:, c * wide : (c + 1) * wide], preferred_element_type=f32
        )
        value = jnp.where(gate != 0.0, value * gate, 0.0).astype(bf16)
        terms[c] = value.reshape(y_count, 2, own_rows, wide)
        remote(
            terms.at[c, :, 1 - core], core_in.at[c], one_send.at[17], tc_recv.at[c], seg=mate
        ).start()

    later(core_in, 17)
    def joined(c):
        waiter(core_in.at[c], tc_recv.at[c], seg=mate).wait_recv()
        for k in range(y_count):
            value = (terms[c, k, core].astype(f32) + core_in[c, k].astype(f32)).reshape(
                half, 2, mine, wide
            ).astype(bf16)
            for i in range(2):
                both[c, k, i] = value[:, i]
        if c % 2 == 0:
            for d in range(1, y_count):
                remote(
                    both.at[c, lax.rem(y + d, y_count)], y_in.at[c, d],
                    one_send.at[18], ty_recv.at[c], seg=y_seg(d),
                ).start()
        else:
            remote(
                both.at[c, :, 1 - x], x_in.at[c, pl.ds(0, y_count)], one_send.at[19],
                tx_recv.at[c], ep=x_mate,
            ).start()

    other_ys = pl.ds(1, y_count - 1)
    evens, odds = pl.ds(0, (steps + 1) // 2), pl.ds(0, steps // 2)
    later(y_in.at[evens, other_ys], 18)
    later(x_in.at[odds, pl.ds(0, y_count)], 19)

    def crossed(c):
        if c % 2 == 0:
            collect(y_in.at[c, other_ys], ty_recv.at[c])
            for i in range(2):
                value = both[c, y, i].astype(f32)
                for d in range(1, y_count):
                    value = value + y_in[c, d, i].astype(f32)
                middle[c, i] = value.astype(bf16)
            remote(
                middle.at[c, 1 - x], x_in.at[c, 0], one_send.at[20], tx_recv.at[c], ep=x_mate
            ).start()
        else:
            collect(x_in.at[c, pl.ds(0, y_count)], tx_recv.at[c])
            for k in range(y_count):
                middle[c, k] = (both[c, k, x].astype(f32) + x_in[c, k].astype(f32)).astype(bf16)
            for d in range(1, y_count):
                remote(
                    middle.at[c, lax.rem(y + d, y_count)], y_in.at[c, d, 0],
                    one_send.at[21], ty_recv.at[c], seg=y_seg(d),
                ).start()

    later(x_in.at[evens, 0], 20)
    later(y_in.at[odds, other_ys, 0], 21)

    def along(c):
        if c % 2 == 0:
            collect(x_in.at[c, 0], tx_recv.at[c])
            value = middle[c, x].astype(f32) + x_in[c, 0].astype(f32)
        else:
            collect(y_in.at[c, other_ys, 0], ty_recv.at[c])
            value = middle[c, y].astype(f32)
            for d in range(1, y_count):
                value = value + y_in[c, d, 0].astype(f32)
        line[c] = value.astype(bf16)
        for k in range(1, half):
            other = lax.rem(z + k, half)
            remote(
                line.at[c, other], line_in.at[c, k], one_send.at[22], tz_recv.at[c],
                ep=other * 2 + x,
            ).start()

    later(line_in.at[:, pl.ds(1, half - 1)], 22)

    def settle():
        collect(tokens.at[others], one_recv.at[16])
        mixed = [tokens[p].astype(f32) for p in range(ep_count)]
        square = sum(jnp.sum(m * m, axis=1, keepdims=True) for m in mixed)
        inv_rms = lax.rsqrt(square / features + epsilon)
        for p in range(ep_count):
            at = slice(p * width, (p + 1) * width)
            attn_ref[:, at] = (mixed[p] * inv_rms * gain_ref[:, at]).astype(bf16)
        result.start()

    result = pltpu.make_async_copy(attn_ref, attn_hbm, load_sem.at[8])
    for c in range(steps + lags[2]):
        if c < steps:
            product(c)
        if 0 <= c - lags[0] < steps:
            joined(c - lags[0])
        if 0 <= c - lags[1] < steps:
            crossed(c - lags[1])
        if 0 <= c - lags[2] < steps:
            along(c - lags[2])
    settle()
    for c in range(steps):
        value = line[c, z].astype(f32)
        collect(line_in.at[c, pl.ds(1, half - 1)], tz_recv.at[c])
        for k in range(1, half):
            value = value + line_in[c, k].astype(f32)
        out_ref[:, c * wide : (c + 1) * wide] = value.astype(bf16)
    whole = pltpu.make_async_copy(out_ref, out_hbm, load_sem.at[9])
    whole.start()
    for copy in pending:
        copy.wait_send()

    @pl.when(jnp.logical_not(at_end))
    def _():
        remote(x_sum, x_sum, one_send.at[10], one_recv.at[0], ep=x_mate).wait_send()

    result.wait()
    whole.wait()


def carry_kernel(a_in, b_in, a_out, b_out, a_held, b_held, sem):
    inward = [
        pltpu.make_async_copy(src, held, sem.at[0, i])
        for i, (src, held) in enumerate(((a_in, a_held), (b_in, b_held)))
    ]
    outward = [
        pltpu.make_async_copy(held, dst, sem.at[1, i])
        for i, (held, dst) in enumerate(((a_held, a_out), (b_held, b_out)))
    ]
    for copy in inward:
        copy.start()
    for copy, after in zip(inward, outward):
        copy.wait()
        after.start()
    for copy in outward:
        copy.wait()


def on_device_dense(
    queries, keys, values, log_decay, out_gain, out_proj, experts, gates, up_weight, down_weight
):
    f32, bf16 = jnp.float32, jnp.bfloat16
    dma = pltpu.SemaphoreType.DMA
    seg_count, ep_count = lax.axis_size("seg"), lax.axis_size("ep")
    y_count, half = seg_count // 2, ep_count // 2
    tokens_own, features = queries.shape
    heads = log_decay.shape[1]
    width = features // ep_count
    dim = width // heads
    moe_own = experts.shape[0]
    seg_rows = moe_own * ep_count
    total = seg_rows * seg_count
    cols = out_proj.shape[1]
    model, units = up_weight.shape[1:]
    tile = math.gcd(cols, 512)
    wide = tile
    steps = model // wide
    hbm = pl.BlockSpec(memory_space=pl.ANY)
    results = pl.pallas_call(
        functools.partial(step_kernel, seg_count, ep_count, heads, dim, tile, wide, (2, 8, 13), BYX, PACE),
        out_shape=(
            jax.ShapeDtypeStruct((tokens_own, features), bf16),
            jax.ShapeDtypeStruct((moe_own, model), bf16),
        ),
        in_specs=[hbm] * 10,
        out_specs=(hbm, hbm),
        scratch_shapes=[
            VM((heads, log_decay.shape[0]), f32),
            VM((experts.shape[1], moe_own), jnp.int32),
            VM((experts.shape[1], moe_own), f32),
            VM((1, features), f32),
            VM((tokens_own, features), bf16),
            VM((moe_own, model), bf16),
            VM((2, ep_count, tokens_own, width), bf16),
            VM((ep_count, tokens_own, width), bf16),
            VM((tokens_own, features), bf16),
            VM((ep_count, moe_own, width), bf16),
            VM((ep_count, moe_own, width), bf16),
            VM((seg_count, heads, dim, dim), bf16),
            VM((seg_count, 8, dim), f32),
            VM((seg_count, ep_count, moe_own, 128), f32),
            VM((ep_count, tokens_own, width), bf16),
            VM((units, model), bf16),
            VM((units, model), bf16),
            VM((width, cols), bf16),
            VM((seg_count, seg_rows, width), bf16),
            VM((seg_count, 2, half, moe_own, cols + 128), bf16),
            VM((seg_count, half, moe_own, cols + 128), bf16),
            VM((seg_count, half, moe_own, cols + 128), bf16),
            VM((2, seg_count, half, moe_own, cols + 128), bf16),
            VM((seg_count, half, moe_own, cols + 128), bf16),
            VM((seg_count, half, moe_own, cols + 128), bf16),
            VM((seg_count, half, moe_own, 128), f32),
            VM((seg_count, seg_count, ep_count, moe_own, cols), bf16),
            VM((total, units), f32),
            VM((total, units), bf16),
            VM((ep_count, tokens_own, width), bf16),
            VM((steps, y_count, 2, seg_rows, wide), bf16),
            VM((steps, y_count, seg_rows, wide), bf16),
            VM((steps, y_count, 2, half, moe_own, wide), bf16),
            VM((steps, y_count, 2, half, moe_own, wide), bf16),
            VM((steps, max(2, y_count), half, moe_own, wide), bf16),
            VM((steps, max(2, y_count), half, moe_own, wide), bf16),
            VM((steps, half, moe_own, wide), bf16),
            VM((steps, half, moe_own, wide), bf16),
            dma((10,)),
            dma((23,)),
            dma((17,)),
            dma((seg_count - 1,)),
            dma((seg_count, cols // tile)),
            dma((2, seg_count, cols // tile)),
            dma((seg_count, half)),
            dma((seg_count, half, max(1, y_count - 1))),
            dma((seg_count, 2)),
            dma((y_count,)),
        ]
        + [dma((steps,))] * 4,
        compiler_params=pltpu.CompilerParams(
            collective_id=1, has_side_effects=True, vmem_limit_bytes=62 * 2**20
        ),
    )(
        queries, keys, values, out_proj, jnp.swapaxes(up_weight, 1, 2), down_weight,
        log_decay.T, experts.T, gates.T, out_gain[None, :],
    )
    return pl.pallas_call(
        carry_kernel,
        out_shape=tuple(jax.ShapeDtypeStruct(r.shape, r.dtype) for r in results),
        in_specs=[hbm] * 2,
        out_specs=(hbm, hbm),
        scratch_shapes=[VM(r.shape, r.dtype) for r in results] + [dma((2, 2))],
    )(*results)


def on_device(*args):
    experts, ep_count = args[6], lax.axis_size("ep")
    full_rows = max(2, 4 * experts.shape[0] // (ep_count // 2)) >= experts.shape[0]
    return (on_device_dense if full_rows else on_device_routed)(*args)


def solution(mesh):
    placed = (
        P(("seg", "ep"), None),
        P(("seg", "ep"), None),
        P(("seg", "ep"), None),
        P("seg", "ep"),
        P(),
        P("ep", "seg"),
        P(("seg", "ep"), None),
        P(("seg", "ep"), None),
        P("ep", None, "seg"),
        P("ep", "seg", None),
    )
    return jax.shard_map(
        on_device,
        mesh=mesh,
        in_specs=placed,
        out_specs=(P(("seg", "ep"), None), P(("seg", "ep"), None)),
        check_vma=False,
    )
```

```python
import functools
import math

import jax
import jax.numpy as jnp
from jax import lax
from jax.experimental import pallas as pl
from jax.experimental.pallas import tpu as pltpu
from jax.sharding import PartitionSpec as P

epsilon = 1e-06
BYX = (1, 3)
PACE = ((2.8, 0.71, 3.2, 9.7, 2.5, 3.2, 0.5, 6.0, 11.5), (2.8, 0.71, 3.2, 6.4, 2.5, 3.2, 0.5, 6.0, 13.0))
MESH = pl.DeviceIdType.MESH
VM = pltpu.VMEM


def prefix(x, axis, join, neutral):
    place = lax.axis_index(axis)
    gathered = jax.tree.map(
        lambda a, kind: lax.all_gather(a.astype(kind), axis), x, (jnp.bfloat16, jnp.bfloat16)
    )
    state = jax.tree.map(lambda a, e: jnp.zeros_like(a) + jnp.asarray(e, a.dtype), x, neutral)

    def one(turn, state):
        return join(
            state,
            jax.tree.map(
                lambda a, own: lax.dynamic_index_in_dim(a, turn, 0, False).astype(own.dtype),
                gathered,
                x,
            ),
        )

    return lax.fori_loop(0, place, one, state)


def chain_combine(first_part, second_part):
    return (
        first_part[0] * second_part[0],
        second_part[0][:, None, None] * first_part[1] + second_part[1],
    )


def route_tables(experts, gates, expert_count, capacity):
    token_count = experts.shape[0]
    flattened = experts.reshape(-1)
    onehot = (flattened[:, None] == jnp.arange(expert_count, dtype=jnp.int32)[None, :]).astype(
        jnp.int32
    )
    earlier = jnp.cumsum(onehot, axis=0) - onehot
    position = jnp.sum(earlier * onehot, axis=1)
    slot_index = (flattened * capacity + position).reshape(token_count, 2)
    columns = jnp.arange(expert_count * capacity, dtype=jnp.int32)
    matches = slot_index[:, :, None] == columns[None, None, :]
    dispatch = jnp.any(matches, axis=1).T.astype(jnp.bfloat16)
    combine = jnp.sum(jnp.where(matches, gates[:, :, None], 0.0), axis=1)
    return (dispatch, combine)


def expert_output(row_data, up_piece, down_piece):
    hidden = jax.nn.silu(jnp.dot(row_data, up_piece, preferred_element_type=jnp.float32)).astype(
        jnp.bfloat16
    )
    return jnp.dot(hidden, down_piece, preferred_element_type=jnp.float32)


def on_device_routed(
    queries, keys, values, log_decay, out_gain, out_proj, experts, gates, up_weight, down_weight
):
    highest = lax.Precision.HIGHEST
    ep_count = lax.axis_size("ep")
    heads_local = log_decay.shape[1]
    head_dim = queries.shape[1] // (heads_local * ep_count)
    query_heads, key_heads, value_heads = (
        lax.all_to_all(queries, "ep", split_axis=1, concat_axis=0, tiled=True),
        lax.all_to_all(keys, "ep", split_axis=1, concat_axis=0, tiled=True),
        lax.all_to_all(values, "ep", split_axis=1, concat_axis=0, tiled=True),
    )
    seg_length = query_heads.shape[0]
    query_heads = query_heads.reshape(seg_length, heads_local, head_dim)
    key_heads = key_heads.reshape(seg_length, heads_local, head_dim)
    value_heads = value_heads.reshape(seg_length, heads_local, head_dim)
    cumulative = jnp.cumsum(log_decay, axis=0)
    across = cumulative.T
    block_size = math.gcd(seg_length, 512)
    starts = jnp.arange(seg_length // block_size, dtype=jnp.int32) * block_size
    token_positions = jnp.arange(seg_length, dtype=jnp.int32)

    def block_mix(start):
        query_block = lax.dynamic_slice_in_dim(query_heads, start, block_size, 0)
        cum_block = lax.dynamic_slice_in_dim(across, start, block_size, 1)
        row_ids = start + jnp.arange(block_size, dtype=jnp.int32)
        causal = (row_ids[:, None] >= token_positions[None, :])[None]
        log_gap = cum_block[:, :, None] - across[:, None, :]
        weight = jnp.where(causal, jnp.exp(jnp.where(causal, log_gap, 0.0)), 0.0)
        scores = jnp.einsum(
            "thd,shd->hts", query_block, key_heads, preferred_element_type=jnp.float32
        )
        mixing = (scores * weight).astype(jnp.bfloat16)
        return jnp.einsum("hts,she->the", mixing, value_heads, preferred_element_type=jnp.float32)

    inside = lax.map(block_mix, starts).reshape(seg_length, heads_local, head_dim)
    ending = cumulative[-1]
    to_end = jnp.exp(ending[None, :] - cumulative)
    key_float = key_heads.astype(jnp.float32)
    value_float = value_heads.astype(jnp.float32)
    local_state = jnp.einsum("sh,shd,she->hde", to_end, key_float, value_float, precision=highest)
    identity = (jnp.ones_like(ending), jnp.zeros_like(local_state))
    carried = prefix((jnp.exp(ending), local_state), "seg", chain_combine, identity)[1]
    outside = jnp.exp(cumulative)[:, :, None] * jnp.einsum(
        "thd,hde->the", query_heads.astype(jnp.float32), carried, precision=highest
    )
    mixture = (inside + outside).astype(jnp.bfloat16).reshape(seg_length, heads_local * head_dim)
    token_mix = lax.all_to_all(mixture, "ep", split_axis=0, concat_axis=1, tiled=True)
    as_float = token_mix.astype(jnp.float32)
    inv_rms = lax.rsqrt(jnp.mean(as_float * as_float, axis=1, keepdims=True) + epsilon)
    attn_out = (as_float * inv_rms * out_gain[None, :]).astype(jnp.bfloat16)
    row_stride = 8
    own_width = heads_local * head_dim
    feature_count = own_width * ep_count
    picked_float = mixture.reshape(seg_length // row_stride, row_stride, own_width)[:, 0].astype(
        jnp.float32
    )
    square_sums = lax.psum(jnp.sum(picked_float * picked_float, axis=1), "ep")
    picked_rms = lax.rsqrt(square_sums[:, None] / feature_count + epsilon)
    gain_slice = lax.dynamic_slice_in_dim(out_gain, lax.axis_index("ep") * own_width, own_width, 0)
    normed_rows = (picked_float * picked_rms * gain_slice[None, :]).astype(jnp.bfloat16)
    proj_terms = jnp.dot(
        normed_rows,
        lax.all_gather(out_proj, "seg", axis=1, tiled=True),
        preferred_element_type=jnp.float32,
    )
    moe_in = lax.psum_scatter(
        proj_terms.astype(jnp.bfloat16), "ep", scatter_dimension=0, tiled=True
    )
    expert_count = ep_count // 2
    token_count, model_width = moe_in.shape
    capacity = max(2, 4 * token_count // expert_count)
    dispatch, combine = route_tables(experts, gates, expert_count, capacity)
    up_piece = up_weight[0]
    down_piece = down_weight[0]
    slot_rows = jnp.dot(dispatch, moe_in, preferred_element_type=jnp.float32).astype(jnp.bfloat16)
    outgoing = jnp.repeat(slot_rows.reshape(expert_count, capacity, model_width), 2, axis=0)
    arrived = lax.all_to_all(outgoing, "ep", split_axis=0, concat_axis=0, tiled=True).reshape(
        ep_count * capacity, model_width
    )
    gathered = lax.all_gather(arrived, "seg", axis=0, tiled=True)
    owned_sums = lax.psum_scatter(
        expert_output(gathered, up_piece, down_piece).astype(jnp.bfloat16),
        "seg",
        scatter_dimension=0,
        tiled=True,
    ).astype(jnp.float32)
    returned_back = lax.all_to_all(
        owned_sums.reshape(ep_count, capacity, model_width).astype(jnp.bfloat16),
        "ep",
        split_axis=0,
        concat_axis=0,
        tiled=True,
    ).astype(jnp.float32)
    paired = returned_back.reshape(expert_count, 2, capacity, model_width)
    halves = (paired[:, 0] + paired[:, 1]).reshape(expert_count * capacity, model_width)
    summed = jnp.dot(combine, halves, precision=highest)
    moe_out = summed.astype(jnp.bfloat16)
    return (attn_out, moe_out)


def remote(src, dst, send, recv, **target):
    return pltpu.make_async_remote_copy(
        src_ref=src, dst_ref=dst, send_sem=send, recv_sem=recv,
        device_id=target, device_id_type=MESH,
    )


def greet(seg_count, ep_count):
    seg, ep = lax.axis_index("seg"), lax.axis_index("ep")
    barrier = pltpu.get_barrier_semaphore()
    for j in range(1, ep_count):
        pl.semaphore_signal(
            barrier, inc=1, device_id={"ep": lax.rem(ep + j, ep_count)}, device_id_type=MESH
        )
    for k in range(1, seg_count):
        pl.semaphore_signal(
            barrier, inc=1, device_id={"seg": lax.rem(seg + k, seg_count)}, device_id_type=MESH
        )
    pl.semaphore_wait(barrier, ep_count + seg_count - 2)
    return seg, ep


def step_kernel(
    seg_count, ep_count, heads, dim, tile, wide, lags, by_x, pace,
    q_ref, k_ref, v_ref, proj_hbm, up_hbm, down_hbm,
    turned_hbm, experts_hbm, gates_hbm, gain_hbm,
    attn_hbm, out_hbm,
    turned_ref, experts_ref, gates_ref, gain_ref, attn_ref, out_ref,
    kvb, qb, q_own, q_out, q_in, states, ends, table_ref, mix_ref,
    up, down, proj, rows, part, x_sum, z_part, chain_in, near_out, far_out, scale_ref, full, acc, hidden, tokens,
    terms, core_in, both, y_in, x_in, middle, line, line_in,
    load_sem, one_send, one_recv, pick_recv, rx_recv, chain_recv,
    x_recv, y_recv, xy_recv, c_recv, tc_recv, ty_recv, tx_recv, tz_recv,
):
    f32, bf16 = jnp.float32, jnp.bfloat16
    smalls = [
        pltpu.make_async_copy(src, dst, load_sem.at[4 + i])
        for i, (src, dst) in enumerate(
            (
                (turned_hbm, turned_ref), (experts_hbm, experts_ref), (gates_hbm, gates_ref),
                (gain_hbm, gain_ref),
            )
        )
    ]
    early = pltpu.make_async_copy(q_ref, q_own, load_sem.at[3])
    early.start()
    for copy in smalls:
        copy.start()
    seg, ep = greet(seg_count, ep_count)
    width = heads * dim
    tokens_own, moe_own = q_ref.shape[0], experts_ref.shape[1]
    y_count, half = seg_count // 2, ep_count // 2
    core, y = lax.rem(seg, 2), lax.div(seg, 2)
    x, z = lax.rem(ep, 2), lax.div(ep, 2)
    x_mate = ep + 1 - 2 * x
    mate = seg + 1 - 2 * core

    nearer = jnp.where(z * 2 < half, 0, 1)
    at_end = (z == 0) | (z == half - 1)
    ahead = (z + 1 - 2 * nearer) * 2 + x
    behind = (z - 1 + 2 * nearer) * 2 + x

    def seg_at(d, i):
        return lax.rem(y + d + 2 * y_count, y_count) * 2 + (core if i == 0 else 1 - core)

    own = pl.ds(pl.multiple_of(ep * width, width), width)
    pending = []

    def waiter(ref, recv, **target):
        return remote(ref, ref, one_send.at[0], recv, **target)

    def collect(ref, recv):
        waiter(ref, recv, ep=x_mate).wait_recv()

    def later(ref, index):
        pending.append(remote(ref, ref, one_send.at[index], one_recv.at[0], ep=x_mate))

    def scatter(ref, buf, index):
        for j in sorted(range(1, ep_count), key=lambda j: abs(2 * j - ep_count)):
            other = lax.rem(ep + j, ep_count)
            columns = pl.ds(pl.multiple_of(other * width, width), width)
            remote(
                ref.at[:, columns], buf.at[ep], one_send.at[index], one_recv.at[index], ep=other
            ).start()
        pltpu.make_async_copy(ref.at[:, own], buf.at[ep], one_recv.at[index]).start()

    others = pl.ds(1, ep_count - 1)
    other_segs = pl.ds(1, seg_count - 1)
    scatter(k_ref, kvb.at[0], 0)
    scatter(v_ref, kvb.at[1], 0)
    later(kvb.at[:, others], 0)
    loads = [
        pltpu.make_async_copy(proj_hbm, proj, load_sem.at[0]),
        pltpu.make_async_copy(up_hbm.at[0], up, load_sem.at[1]),
        pltpu.make_async_copy(down_hbm.at[0], down, load_sem.at[2]),
    ]
    for load in loads:
        load.start()
    stride = tokens_own // moe_own
    few = (
        lax.broadcasted_iota(jnp.int32, (moe_own, tokens_own), 1)
        == stride * lax.broadcasted_iota(jnp.int32, (moe_own, tokens_own), 0)
    )
    early.wait()
    chosen = jnp.dot(
        few.astype(f32).astype(bf16), q_own[...], preferred_element_type=f32
    ).astype(bf16)
    for p in range(ep_count):
        q_out[p] = chosen[:, p * width : (p + 1) * width]
    for j in sorted(range(1, ep_count), key=lambda j: abs(2 * j - ep_count)):
        other = lax.rem(ep + j, ep_count)
        remote(q_out.at[other], q_in.at[ep], one_send.at[2], one_recv.at[2], ep=other).start()
    later(q_in.at[others], 2)
    q_in[ep] = q_out[ep]
    for copy in smalls:
        copy.wait()
    lanes = lax.broadcasted_iota(jnp.int32, (moe_own, 128), 1).astype(f32)
    corner = (
        lax.broadcasted_iota(jnp.int32, (moe_own, moe_own), 0)
        == lax.broadcasted_iota(jnp.int32, (moe_own, moe_own), 1)
    )

    def upright(line):
        spread = jnp.broadcast_to(line, (moe_own, moe_own))
        return jnp.sum(jnp.where(corner, spread, 0.0), axis=1, keepdims=True)

    table_ref[seg, ep] = sum(
        jnp.where(
            upright(experts_ref[i : i + 1, :].astype(f32)) == lanes,
            upright(gates_ref[i : i + 1, :]),
            0.0,
        )
        for i in range(experts_ref.shape[0])
    )
    for j in range(1, ep_count):
        remote(
            table_ref.at[seg, ep], table_ref.at[seg, ep], one_send.at[3], one_recv.at[3],
            ep=lax.rem(ep + j, ep_count),
        ).start()
    later(table_ref.at[0, others], 3)
    length = tokens_own * ep_count
    highest = lax.Precision.HIGHEST
    rows_at = lax.broadcasted_iota(jnp.int32, (length, length), 0)
    columns_at = lax.broadcasted_iota(jnp.int32, (length, length), 1)
    causal = rows_at >= columns_at
    lower = causal.astype(f32)
    turned_decay = turned_ref[...]
    across = lax.dot_general(
        turned_decay, lower, (((1,), (1,)), ((), ())), precision=highest,
        preferred_element_type=f32,
    )
    cum = lax.dot_general(
        lower, turned_decay, (((1,), (1,)), ((), ())), precision=highest,
        preferred_element_type=f32,
    )
    count = ep_count * moe_own
    causal_few = lax.broadcasted_iota(
        jnp.int32, (count, length), 1
    ) <= stride * lax.broadcasted_iota(jnp.int32, (count, length), 0)
    cum_few = lax.dot_general(
        causal_few.astype(f32), turned_decay, (((1,), (1,)), ((), ())), precision=highest,
        preferred_element_type=f32,
    )
    collect(kvb, one_recv.at[0])
    keys, values = (
        jnp.concatenate([kvb[i, p] for p in range(ep_count)], axis=0) for i in range(2)
    )
    ending = cum[length - 1 : length, :]
    unit = (
        lax.broadcasted_iota(jnp.int32, (dim, dim), 0)
        == lax.broadcasted_iota(jnp.int32, (dim, dim), 1)
    ).astype(f32).astype(bf16)
    for h in range(heads):
        cols = slice(h * dim, (h + 1) * dim)
        to_end = jnp.exp(ending[:, h : h + 1] - across[h : h + 1, :])
        turned = lax.dot_general(
            unit, keys[:, cols], (((1,), (1,)), ((), ())), preferred_element_type=f32
        )
        states[seg, h] = jnp.dot(
            (turned * to_end).astype(bf16), values[:, cols],
            preferred_element_type=f32,
        ).astype(bf16)
        ends[seg, h : h + 1] = jnp.broadcast_to(ending[:, h : h + 1], (1, dim))
    for k in range(1, seg_count):
        other = lax.rem(seg + k, seg_count)
        for buf, index in ((states, 4), (ends, 5)):
            remote(
                buf.at[seg], buf.at[seg], one_send.at[index], one_recv.at[index], seg=other
            ).start()
    later(states.at[other_segs], 4)
    later(ends.at[other_segs], 5)

    def within(asked, mask, cum, h):
        cols = slice(h * dim, (h + 1) * dim)
        gap = cum[:, h : h + 1] - across[h : h + 1, :]
        weight = jnp.where(mask, jnp.exp(jnp.where(mask, gap, 0.0)), 0.0)
        scores = lax.dot_general(
            asked[:, cols], keys[:, cols], (((1,), (1,)), ((), ())),
            preferred_element_type=f32,
        )
        return jnp.dot(
            (scores * weight).astype(bf16), values[:, cols], preferred_element_type=f32
        )

    def before(asked, cum, h):
        cols = slice(h * dim, (h + 1) * dim)
        return jnp.exp(cum[:, h : h + 1]) * jnp.dot(
            asked[:, cols], carried[h], preferred_element_type=f32
        )

    collect(q_in.at[others], one_recv.at[2])
    asked = q_in[...].reshape(count, width)
    inside = [within(asked, causal_few, cum_few, h) for h in range(heads)]
    scatter(q_ref, qb, 1)
    later(qb.at[others], 1)
    collect(states.at[other_segs], one_recv.at[4])
    collect(ends.at[other_segs], one_recv.at[5])
    carried = []
    for h in range(heads):
        joined = jnp.zeros((dim, dim), f32)
        for c in range(seg_count):
            after = jnp.exp(ends[c, h : h + 1]) * joined + states[c, h].astype(f32)
            joined = jnp.where(c < seg, after, joined)
        carried.append(joined.astype(bf16))
    for h in range(heads):
        rows[seg, :, h * dim : (h + 1) * dim] = (
            inside[h] + before(asked, cum_few, h)
        ).astype(bf16)

    def mix_all():
        collect(qb, one_recv.at[1])
        queries = jnp.concatenate([qb[p] for p in range(ep_count)], axis=0)
        for h in range(heads):
            value = within(queries, causal, cum, h) + before(queries, cum, h)
            mix_ref[:, :, h * dim : (h + 1) * dim] = value.astype(bf16).reshape(
                ep_count, tokens_own, dim
            )

    own_rows = rows.shape[1]
    total = own_rows * seg_count
    mine = own_rows // ep_count
    cols = proj.shape[1]
    features = width * ep_count
    sources = [(d, i) for d in range(y_count) for i in range(2)]
    row_moves = {}
    for d, i in sources[1:]:
        row_moves[d, i] = remote(
            rows.at[seg], rows.at[seg], one_send.at[6], pick_recv.at[d * 2 + i - 1],
            seg=seg_at(d, i),
        )
        row_moves[d, i].start()
    later(rows.at[other_segs], 6)
    lane = lax.broadcasted_iota(jnp.int32, (own_rows, 128), 1)
    pieces = [(0, 128 + tile)] + [(128 + t, tile) for t in range(tile, cols, tile)]
    x_moves = {}

    def source(n):
        d, i = sources[n]
        return seg_at(-d, i)

    def project(end, n):
        if n:
            row_moves[sources[n]].wait_recv()
        picked = rows[source(n)].astype(f32)
        squares = jnp.sum(picked * picked, axis=1, keepdims=True)
        high = squares.astype(bf16).astype(f32)
        pair = jnp.where(lane < 64, high, squares - high).reshape(half, 2, mine, 128).astype(bf16)
        scaled = (picked * gain_ref[:, own]).astype(bf16)
        for i in range(2):
            part[n, i, :, :, :128] = pair[:, i]
        for p, (at, size) in enumerate(pieces):
            t = p * tile
            value = (
                jnp.dot(scaled, proj[:, t : t + tile], preferred_element_type=f32)
                .reshape(half, 2, mine, tile)
                .astype(bf16)
            )
            for i in range(2):
                part[n, i, :, :, 128 + t : 128 + t + tile] = value[:, i]
            span = pl.ds(at, size)
            x_moves[n, p] = remote(
                part.at[n, 1 - x, :, :, span], x_sum.at[n, :, :, span],
                one_send.at[7], rx_recv.at[n, p], ep=x_mate,
            )
            x_moves[n, p].start()

    short_lane = lane[: half * mine]

    def keep_sum(ref, n, p, value):
        at, size = pieces[p]
        ref[n, :, :, pl.ds(at, size)] = value.astype(bf16)
        if p == 0:
            pair = value[:, :, :128].reshape(half * mine, 128)
            squares = pair[:, :1] + pair[:, 64:65]
            high = squares.astype(bf16).astype(f32)
            pair = jnp.where(short_lane < 64, high, squares - high).astype(bf16)
            ref[n, :, :, :128] = pair.reshape(half, mine, 128)

    def combine(end, n, p):
        span = pl.ds(*pieces[p])
        x_moves[n, p].wait_recv()
        value = part[n, x, :, :, span].astype(f32) + x_sum[n, :, :, span].astype(f32)
        keep_sum(z_part, n, p, value)
        if end:
            remote(
                z_part.at[n, :, :, span], chain_in.at[nearer, n, :, :, span],
                one_send.at[8], chain_recv.at[nearer, n, p], ep=ahead,
            ).start()

    def near(end, n, p):
        if end:
            return
        span = pl.ds(*pieces[p])
        collect(x_sum.at[n, :, :, span], chain_recv.at[nearer, n, p])
        value = z_part[n, :, :, span].astype(f32)
        value = value + chain_in[nearer, n, :, :, span].astype(f32)
        keep_sum(near_out, n, p, value)
        remote(
            near_out.at[n, :, :, span], chain_in.at[nearer, n, :, :, span],
            one_send.at[8], chain_recv.at[nearer, n, p], ep=ahead,
        ).start()

    def far(end, n, p):
        at, size = pieces[p]
        span = pl.ds(at, size)
        collect(x_sum.at[n, :, :, span], chain_recv.at[1 - nearer, n, p])

        def settled(value):
            if p == 0:
                square = value[:, :, :1] + value[:, :, 64:65]
                scale_ref[n] = jnp.broadcast_to(
                    lax.rsqrt(square / features + epsilon), (half, mine, 128)
                )
                value = value[:, :, 128:]
            value = (value * scale_ref[n][:, :, :1]).astype(bf16)
            start = max(at - 128, 0)
            for k in range(half):
                full[seg, source(n), k * 2 + x, :, start : start + tile] = value[k]

        value = z_part[n, :, :, span].astype(f32)
        value = value + chain_in[1 - nearer, n, :, :, span].astype(f32)
        if not end:
            keep_sum(far_out, n, p, value)
            remote(
                far_out.at[n, :, :, span], chain_in.at[1 - nearer, n, :, :, span],
                one_send.at[10], chain_recv.at[1 - nearer, n, p], ep=behind,
            ).start()
            value = value + chain_in[nearer, n, :, :, span].astype(f32)
        settled(value)

    loads[0].wait()
    project(None, 0)
    later(x_sum, 7)
    later(x_sum, 8)
    collect(table_ref.at[0, others], one_recv.at[3])
    for k in range(1, seg_count):
        remote(
            table_ref.at[seg], table_ref.at[seg], one_send.at[9], one_recv.at[9],
            seg=lax.rem(seg + k, seg_count),
        ).start()
    later(table_ref.at[other_segs], 9)
    def send(place, index, recv_sem, **target):
        copy = remote(place, place, one_send.at[index], recv_sem, **target)
        copy.start()
        return copy

    def on_line(e, k):
        return k * 2 + lax.rem(e, 2)

    def y_seg(k):
        return seg_at(k, 0)

    def block(n, d, e):
        at, i = sources[n]
        return full.at[y_seg(-d), seg_at(-d - at, i), e]

    x_copies, y_copies = {}, {}

    def spread(end, n):
        for k in range(half):
            place = block(n, 0, on_line(ep, k))
            x_copies[n, k] = send(place, 11, x_recv.at[n, k], ep=x_mate)
            for d in range(1, y_count):
                y_copies[n, k, d] = send(place, 12, y_recv.at[n, k, d - 1], seg=y_seg(d))
            send(place, 15, c_recv.at[0], seg=mate)

    def relay(end, n, k):
        x_copies[n, k].wait_recv()
        place = block(n, 0, on_line(x_mate, k))
        if k not in by_x:
            for d in range(1, y_count):
                send(place, 13, xy_recv.at[n, 0], seg=y_seg(d))
        send(place, 15, c_recv.at[0], seg=mate)
        for d in range(1, y_count):
            y_copies[n, k, d].wait_recv()
            place = block(n, d, on_line(ep, k))
            if k in by_x:
                send(place, 14, xy_recv.at[n, 1], ep=x_mate)
            send(place, 15, c_recv.at[d], seg=mate)

    by_y = [k for k in range(half) if k not in by_x]

    def blocks(count):
        return full.at[0, 0, pl.ds(0, count)]

    def hand_over(end, n):
        for i, ks in enumerate((by_y, by_x)):
            if ks and y_count > 1:
                collect(blocks(len(ks) * (y_count - 1)), xy_recv.at[n, i])
            for k in ks:
                for d in range(1, y_count):
                    send(block(n, d, on_line(x_mate, k)), 15, c_recv.at[d], seg=mate)

    later(full.at[0, :, pl.ds(0, half)], 11)
    if y_count > 1:
        later(full.at[0, :, pl.ds(0, half * (y_count - 1))], 12)
        for i, ks in enumerate((by_y, by_x)):
            if ks:
                later(full.at[0, :, pl.ds(0, len(ks) * (y_count - 1))], 13 + i)
    later(full.at[pl.ds(0, y_count)], 15)

    def attend(end):
        mix_all()

    def proceed(end, start, beat, near_lag, far_lag, first, relay_beat, relay_step, hand_lag, at):
        plan = [(2.0 * n, project, (n,)) for n in range(1, seg_count)] + [(at, attend, ())]
        for n in range(seg_count):
            for p in range(len(pieces)):
                time = start + beat * (n * len(pieces) + p)
                plan += [
                    (time, combine, (n, p)), (time + near_lag, near, (n, p)),
                    (time + far_lag, far, (n, p)),
                ]
            plan += [(time + far_lag + 0.01, spread, (n,))]
            ready = start + beat * (len(pieces) - 1) + far_lag + first + relay_beat * n
            plan += [(ready + relay_step * k, relay, (n, k)) for k in range(half)]
            if n < seg_count - 1:
                plan += [(ready + hand_lag, hand_over, (n,))]
        for _, stage, given in sorted(plan, key=lambda item: item[0]):
            stage(end, *given)

    for end, hints in zip((True, False), pace):
        pl.when(at_end if end else jnp.logical_not(at_end))(
            functools.partial(proceed, end, *hints)
        )
    loads[1].wait()

    def multiply(s, fresh=False):
        lines = pl.ds(pl.multiple_of(s * cols, cols), cols)
        value = lax.dot_general(
            full[s].reshape(total, cols), up[:, lines], (((1,), (1,)), ((), ())),
            preferred_element_type=f32,
        )
        acc[...] = value if fresh else acc[...] + value

    multiply(seg, True)
    for k in range(y_count):
        waiter(full.at[0], c_recv.at[k], seg=mate).wait_recv()
        multiply(seg_at(-k, 1))
        if k == 0:
            hand_over(None, seg_count - 1)
        if k + 1 < y_count:
            multiply(y_seg(-k - 1))
    tokens[ep] = mix_ref[ep]
    for j in sorted(range(1, ep_count), key=lambda j: abs(2 * j - ep_count)):
        other = lax.rem(ep + j, ep_count)
        remote(
            mix_ref.at[other], tokens.at[ep], one_send.at[16], one_recv.at[16], ep=other
        ).start()
    later(tokens.at[others], 16)
    value = acc[...]
    hidden[...] = (value / (1.0 + jnp.exp(-value))).astype(bf16)
    collect(table_ref.at[other_segs], one_recv.at[9])
    table = table_ref[...].reshape(total, 128)
    lane = lax.broadcasted_iota(jnp.int32, (total, 128), 1)
    gate = jnp.sum(jnp.where(lane == z, table, 0.0), axis=1, keepdims=True)
    loads[2].wait()
    steps = seg_count * cols // wide
    core_moves = {}

    def product(c):
        value = jnp.dot(
            hidden[...], down[:, c * wide : (c + 1) * wide], preferred_element_type=f32
        )
        value = jnp.where(gate != 0.0, value * gate, 0.0).astype(bf16)
        terms[c] = value.reshape(y_count, 2, own_rows, wide)
        remote(
            terms.at[c, :, 1 - core], core_in.at[c], one_send.at[17], tc_recv.at[c], seg=mate
        ).start()

    later(core_in, 17)
    def joined(c):
        waiter(core_in.at[c], tc_recv.at[c], seg=mate).wait_recv()
        for k in range(y_count):
            value = (terms[c, k, core].astype(f32) + core_in[c, k].astype(f32)).reshape(
                half, 2, mine, wide
            ).astype(bf16)
            for i in range(2):
                both[c, k, i] = value[:, i]
        if c % 2 == 0:
            for d in range(1, y_count):
                remote(
                    both.at[c, lax.rem(y + d, y_count)], y_in.at[c, d],
                    one_send.at[18], ty_recv.at[c], seg=y_seg(d),
                ).start()
        else:
            remote(
                both.at[c, :, 1 - x], x_in.at[c, pl.ds(0, y_count)], one_send.at[19],
                tx_recv.at[c], ep=x_mate,
            ).start()

    other_ys = pl.ds(1, y_count - 1)
    evens, odds = pl.ds(0, (steps + 1) // 2), pl.ds(0, steps // 2)
    later(y_in.at[evens, other_ys], 18)
    later(x_in.at[odds, pl.ds(0, y_count)], 19)

    def crossed(c):
        if c % 2 == 0:
            collect(y_in.at[c, other_ys], ty_recv.at[c])
            for i in range(2):
                value = both[c, y, i].astype(f32)
                for d in range(1, y_count):
                    value = value + y_in[c, d, i].astype(f32)
                middle[c, i] = value.astype(bf16)
            remote(
                middle.at[c, 1 - x], x_in.at[c, 0], one_send.at[20], tx_recv.at[c], ep=x_mate
            ).start()
        else:
            collect(x_in.at[c, pl.ds(0, y_count)], tx_recv.at[c])
            for k in range(y_count):
                middle[c, k] = (both[c, k, x].astype(f32) + x_in[c, k].astype(f32)).astype(bf16)
            for d in range(1, y_count):
                remote(
                    middle.at[c, lax.rem(y + d, y_count)], y_in.at[c, d, 0],
                    one_send.at[21], ty_recv.at[c], seg=y_seg(d),
                ).start()

    later(x_in.at[evens, 0], 20)
    later(y_in.at[odds, other_ys, 0], 21)

    def along(c):
        if c % 2 == 0:
            collect(x_in.at[c, 0], tx_recv.at[c])
            value = middle[c, x].astype(f32) + x_in[c, 0].astype(f32)
        else:
            collect(y_in.at[c, other_ys, 0], ty_recv.at[c])
            value = middle[c, y].astype(f32)
            for d in range(1, y_count):
                value = value + y_in[c, d, 0].astype(f32)
        line[c] = value.astype(bf16)
        for k in range(1, half):
            other = lax.rem(z + k, half)
            remote(
                line.at[c, other], line_in.at[c, k], one_send.at[22], tz_recv.at[c],
                ep=other * 2 + x,
            ).start()

    later(line_in.at[:, pl.ds(1, half - 1)], 22)

    def settle():
        collect(tokens.at[others], one_recv.at[16])
        mixed = [tokens[p].astype(f32) for p in range(ep_count)]
        square = sum(jnp.sum(m * m, axis=1, keepdims=True) for m in mixed)
        inv_rms = lax.rsqrt(square / features + epsilon)
        for p in range(ep_count):
            at = slice(p * width, (p + 1) * width)
            attn_ref[:, at] = (mixed[p] * inv_rms * gain_ref[:, at]).astype(bf16)
        result.start()

    result = pltpu.make_async_copy(attn_ref, attn_hbm, load_sem.at[8])
    for c in range(steps + lags[2]):
        if c < steps:
            product(c)
        if 0 <= c - lags[0] < steps:
            joined(c - lags[0])
        if 0 <= c - lags[1] < steps:
            crossed(c - lags[1])
        if 0 <= c - lags[2] < steps:
            along(c - lags[2])
    settle()
    for c in range(steps):
        value = line[c, z].astype(f32)
        collect(line_in.at[c, pl.ds(1, half - 1)], tz_recv.at[c])
        for k in range(1, half):
            value = value + line_in[c, k].astype(f32)
        out_ref[:, c * wide : (c + 1) * wide] = value.astype(bf16)
    whole = pltpu.make_async_copy(out_ref, out_hbm, load_sem.at[9])
    whole.start()
    for copy in pending:
        copy.wait_send()

    @pl.when(jnp.logical_not(at_end))
    def _():
        remote(x_sum, x_sum, one_send.at[10], one_recv.at[0], ep=x_mate).wait_send()

    result.wait()
    whole.wait()


def carry_kernel(a_in, b_in, a_out, b_out, a_held, b_held, sem):
    inward = [
        pltpu.make_async_copy(src, held, sem.at[0, i])
        for i, (src, held) in enumerate(((a_in, a_held), (b_in, b_held)))
    ]
    outward = [
        pltpu.make_async_copy(held, dst, sem.at[1, i])
        for i, (held, dst) in enumerate(((a_held, a_out), (b_held, b_out)))
    ]
    for copy in inward:
        copy.start()
    for copy, after in zip(inward, outward):
        copy.wait()
        after.start()
    for copy in outward:
        copy.wait()


def on_device_dense(
    queries, keys, values, log_decay, out_gain, out_proj, experts, gates, up_weight, down_weight
):
    f32, bf16 = jnp.float32, jnp.bfloat16
    dma = pltpu.SemaphoreType.DMA
    seg_count, ep_count = lax.axis_size("seg"), lax.axis_size("ep")
    y_count, half = seg_count // 2, ep_count // 2
    tokens_own, features = queries.shape
    heads = log_decay.shape[1]
    width = features // ep_count
    dim = width // heads
    moe_own = experts.shape[0]
    seg_rows = moe_own * ep_count
    total = seg_rows * seg_count
    cols = out_proj.shape[1]
    model, units = up_weight.shape[1:]
    tile = math.gcd(cols, 512)
    wide = tile
    steps = model // wide
    hbm = pl.BlockSpec(memory_space=pl.ANY)
    results = pl.pallas_call(
        functools.partial(step_kernel, seg_count, ep_count, heads, dim, tile, wide, (2, 8, 13), BYX, PACE),
        out_shape=(
            jax.ShapeDtypeStruct((tokens_own, features), bf16),
            jax.ShapeDtypeStruct((moe_own, model), bf16),
        ),
        in_specs=[hbm] * 10,
        out_specs=(hbm, hbm),
        scratch_shapes=[
            VM((heads, log_decay.shape[0]), f32),
            VM((experts.shape[1], moe_own), jnp.int32),
            VM((experts.shape[1], moe_own), f32),
            VM((1, features), f32),
            VM((tokens_own, features), bf16),
            VM((moe_own, model), bf16),
            VM((2, ep_count, tokens_own, width), bf16),
            VM((ep_count, tokens_own, width), bf16),
            VM((tokens_own, features), bf16),
            VM((ep_count, moe_own, width), bf16),
            VM((ep_count, moe_own, width), bf16),
            VM((seg_count, heads, dim, dim), bf16),
            VM((seg_count, 8, dim), f32),
            VM((seg_count, ep_count, moe_own, 128), f32),
            VM((ep_count, tokens_own, width), bf16),
            VM((units, model), bf16),
            VM((units, model), bf16),
            VM((width, cols), bf16),
            VM((seg_count, seg_rows, width), bf16),
            VM((seg_count, 2, half, moe_own, cols + 128), bf16),
            VM((seg_count, half, moe_own, cols + 128), bf16),
            VM((seg_count, half, moe_own, cols + 128), bf16),
            VM((2, seg_count, half, moe_own, cols + 128), bf16),
            VM((seg_count, half, moe_own, cols + 128), bf16),
            VM((seg_count, half, moe_own, cols + 128), bf16),
            VM((seg_count, half, moe_own, 128), f32),
            VM((seg_count, seg_count, ep_count, moe_own, cols), bf16),
            VM((total, units), f32),
            VM((total, units), bf16),
            VM((ep_count, tokens_own, width), bf16),
            VM((steps, y_count, 2, seg_rows, wide), bf16),
            VM((steps, y_count, seg_rows, wide), bf16),
            VM((steps, y_count, 2, half, moe_own, wide), bf16),
            VM((steps, y_count, 2, half, moe_own, wide), bf16),
            VM((steps, max(2, y_count), half, moe_own, wide), bf16),
            VM((steps, max(2, y_count), half, moe_own, wide), bf16),
            VM((steps, half, moe_own, wide), bf16),
            VM((steps, half, moe_own, wide), bf16),
            dma((10,)),
            dma((23,)),
            dma((17,)),
            dma((seg_count - 1,)),
            dma((seg_count, cols // tile)),
            dma((2, seg_count, cols // tile)),
            dma((seg_count, half)),
            dma((seg_count, half, max(1, y_count - 1))),
            dma((seg_count, 2)),
            dma((y_count,)),
        ]
        + [dma((steps,))] * 4,
        compiler_params=pltpu.CompilerParams(
            collective_id=1, has_side_effects=True, vmem_limit_bytes=62 * 2**20
        ),
    )(
        queries, keys, values, out_proj, jnp.swapaxes(up_weight, 1, 2), down_weight,
        log_decay.T, experts.T, gates.T, out_gain[None, :],
    )
    return pl.pallas_call(
        carry_kernel,
        out_shape=tuple(jax.ShapeDtypeStruct(r.shape, r.dtype) for r in results),
        in_specs=[hbm] * 2,
        out_specs=(hbm, hbm),
        scratch_shapes=[VM(r.shape, r.dtype) for r in results] + [dma((2, 2))],
    )(*results)


def on_device(*args):
    experts, ep_count = args[6], lax.axis_size("ep")
    full_rows = max(2, 4 * experts.shape[0] // (ep_count // 2)) >= experts.shape[0]
    return (on_device_dense if full_rows else on_device_routed)(*args)


def solution(mesh):
    placed = (
        P(("seg", "ep"), None),
        P(("seg", "ep"), None),
        P(("seg", "ep"), None),
        P("seg", "ep"),
        P(),
        P("ep", "seg"),
        P(("seg", "ep"), None),
        P(("seg", "ep"), None),
        P("ep", None, "seg"),
        P("ep", "seg", None),
    )
    return jax.shard_map(
        on_device,
        mesh=mesh,
        in_specs=placed,
        out_specs=(P(("seg", "ep"), None), P(("seg", "ep"), None)),
        check_vma=False,
    )
```
